32 devices in a mesh: seq: 8 (over y, x, core), clip: 4 (over z).
Axes of the slice: x: 2, y: 2, z: 4, core: 2. Of those that a mesh axis runs over, the one named last changes fastest.
Arguments:
- queries: bfloat16 [4, 4096, 512], P('clip', 'seq'), may hold values from -8 to 8
- keys: bfloat16 [4, 4096, 512], P('clip', 'seq'), may hold values from -8 to 8
- values: bfloat16 [4, 4096, 512], P('clip', 'seq'), may hold values from -6 to 6
- out_cotangent: bfloat16 [4, 4096, 1024], P('clip', 'seq'), may hold values from -6 to 6
- visible_counts: int32 [4, 8], P('clip'), may hold values from 1 to 96, 384 in all within a row
- span_offset: int32 [4, 8], P('clip'), may hold values from 0 to 511
- out_weight: bfloat16 [512, 1024], P('seq'), may hold values from -0.1875 to 0.1875
Outputs:
- query_grads: bfloat16 [4, 4096, 512], P('clip', 'seq')
- key_grads: bfloat16 [4, 4096, 512], P('clip', 'seq')
- value_grads: bfloat16 [4, 4096, 512], P('clip', 'seq')
- weight_grad: float32 [512, 1024], P('seq')
The draws below stay inside these ranges and needn't reach their ends.
Inputs may be any that keep to these rules, and one draw needn't show every extreme that they name: `visible_counts`: in each clip the 8 counts sum to 384, and the largest is exactly 96.
All inputs are finite; a program needn't handle non-finite values.
Results may differ from the reference program's by a relative error of at most 0.014.
Values may be sent and summed in bfloat16 or wider, within the bound.
No kernel may reach another device: no remote copies, remote signals or barrier semaphores. Data moves between devices by JAX's collectives and lax.ppermute only.
A program may use at most 64 MiB of HBM per device.

```python
import math
import jax
import jax.numpy as jnp
import numpy as np
from jax import lax

D = 1024
HEADS = 8
HD = 64
QW = 512
F_DEV = 512
VIS_DEV = 48
MAXV = 96
CYCLE = 8
V_CLIP = 384
FRAMES = 4096
CLIPS = 4


def rough_field(key):
    return 1.6 * jax.random.truncated_normal(key, -4.0, 4.0, (CLIPS, FRAMES, QW), jnp.float32)


def draw_queries(key, part):
    field = rough_field(jax.random.fold_in(key, 11))
    return field.astype(jnp.bfloat16)


def draw_keys(key, part):
    field = rough_field(jax.random.fold_in(key, 13))
    return field.astype(jnp.bfloat16)


def place_ends(array, own_key, least, top_value):
    longest = array.shape.index(max(array.shape))
    spots = []
    for shift in (0, 1):
        where = [jax.random.randint(jax.random.fold_in(own_key, axis), (), 0, length) for axis, length in enumerate(array.shape)]
        where[longest] = (where[longest] + shift) % array.shape[longest]
        spots.append(tuple(where))
    return array.at[spots[0]].set(least).at[spots[1]].set(top_value)


def levels(rng, extent, split, smallest, largest):
    gain = 1.0
    for axis_at, blocks in split:
        heights = jax.random.uniform(jax.random.fold_in(jax.random.fold_in(rng, 6), axis_at), (blocks,), jnp.float32, smallest / len(split), largest / len(split))
        gain = gain * jnp.repeat(jnp.exp(heights), extent[axis_at] // blocks).reshape((-1,) + (1,) * (len(extent) - 1 - axis_at))
    return gain


def length_profile(count, total, reach, slope):
    weights = [(1 << 20) // math.isqrt(grade ** slope) + 1 for grade in range(2, count + 1)]
    surplus, given = total - reach - (count - 1), [1] * (count - 1)
    while surplus > 0:
        candidates = [i for i in range(count - 1) if given[i] < reach]
        whole, budget = sum([weights[i] for i in candidates]), surplus
        for i in candidates:
            addition = min(reach - given[i], max(1, budget * weights[i] // whole), surplus)
            given[i] = given[i] + addition
            surplus = surplus - addition
    return np.array([reach] + given)


def uneven(stream_key, number_of, total, most, skew):
    if number_of == 2:
        one = jax.random.randint(stream_key, (), max(1, total - most), min(most, total - 1) + 1)
        return jnp.stack([one, total - one])
    lengths = jnp.asarray(length_profile(number_of, total, most, skew), jnp.int32)
    pairs = (number_of - 1) // 2
    giver, taker = lengths[1:1 + 2 * pairs:2], lengths[2:2 + 2 * pairs:2]
    room = jnp.minimum(giver - 1, most - taker)
    moved = jax.random.randint(jax.random.fold_in(stream_key, 1), (pairs,), 0, 1 << 20) % (room + 1)
    lengths = lengths.at[1:1 + 2 * pairs:2].set(giver - moved).at[2:2 + 2 * pairs:2].set(taker + moved)
    return lengths[jax.random.permutation(jax.random.fold_in(stream_key, 2), number_of)]


def gaussian(own_key, dims, spread, limit, shards=(), kind=jnp.bfloat16):
    drawn = jax.random.normal(own_key, dims, jnp.float32) * spread
    if len(shards) > 0:
        drawn = levels(own_key, dims, shards, -0.22, 0.18) * drawn
    return jnp.clip(drawn, min=-limit, max=limit).astype(kind)


def setup_inputs(seed: int = 0) -> dict:
    key_of = jax.random.split(jax.random.key(seed), 8)
    return {
        "queries": draw_queries(jax.random.fold_in(key_of[7], 71), 0),
        "keys": draw_keys(jax.random.fold_in(key_of[7], 71), 0),
        "values": gaussian(key_of[2], (CLIPS, FRAMES, QW), 1.0, 6.0, ((0, 4), (1, 8))),
        "out_cotangent": gaussian(key_of[3], (CLIPS, FRAMES, D), 1.0, 6.0, ((0, 4), (1, 8))),
        "visible_counts": jax.vmap(lambda own: uneven(own, CYCLE, V_CLIP, MAXV, 2))(jax.random.split(key_of[4], CLIPS)).reshape((CLIPS, CYCLE)).astype(jnp.int32),
        "span_offset": place_ends(jax.random.randint(key_of[5], (CLIPS, CYCLE), 0, F_DEV), jax.random.fold_in(key_of[5], 1), 0, F_DEV - 1).astype(jnp.int32),
        "out_weight": gaussian(key_of[6], (QW, D), D ** -0.5, 0.1875, ((0, 8),)),
    }


def frame_index(counts, offsets):
    position = jnp.arange(F_DEV, dtype=jnp.int32)[None, :]
    amount = counts[:, None].astype(jnp.int32)
    span_begin = offsets[:, None].astype(jnp.int32) % (amount + 1)
    masked = F_DEV - amount
    visible = (position < span_begin) | (position >= span_begin + masked)
    ranked = jnp.where(position < span_begin, position, position - masked)
    before = (jnp.cumsum(counts) - counts).astype(jnp.int32)[:, None]
    return visible.reshape(-1), (before + ranked).reshape(-1).astype(jnp.int32)


def head_pass(parts):
    query_head, key_head, value_head, dout_head = parts
    factor = HD ** -0.5
    scores = jnp.dot(query_head, key_head.T, preferred_element_type=jnp.float32) * factor
    peak_score = jnp.max(scores, axis=1, keepdims=True)
    log_total = peak_score + jnp.log(jnp.sum(jnp.exp(scores - peak_score), axis=1, keepdims=True))
    weights = jnp.exp(scores - log_total)
    weights_low = weights.astype(jnp.bfloat16)
    attended = jnp.dot(weights_low, value_head, preferred_element_type=jnp.float32).astype(jnp.bfloat16)
    inner_sum = jnp.sum(dout_head.astype(jnp.float32) * attended.astype(jnp.float32), axis=1, keepdims=True)
    dweights = jnp.dot(dout_head, value_head.T, preferred_element_type=jnp.float32)
    dscores = (weights * (dweights - inner_sum)).astype(jnp.bfloat16)
    grad_query = (jnp.dot(dscores, key_head, preferred_element_type=jnp.float32) * factor).astype(jnp.bfloat16)
    grad_key = (jnp.dot(dscores.T, query_head, preferred_element_type=jnp.float32) * factor).astype(jnp.bfloat16)
    grad_value = jnp.dot(weights_low.T, dout_head, preferred_element_type=jnp.float32).astype(jnp.bfloat16)
    return attended, grad_query, grad_key, grad_value


def split_heads(block):
    return block.reshape(V_CLIP, HEADS, HD).transpose(1, 0, 2)


def join_heads(block):
    return block.transpose(1, 0, 2).reshape(V_CLIP, HEADS * HD)


def reference(queries, keys, values, out_cotangent, visible_counts, span_offset, out_weight):
    def one_clip(carry, inputs):
        query_rows, key_rows, value_rows, cotangent_rows, counts, offsets = inputs
        visible, index = frame_index(counts, offsets)
        target = jnp.where(visible, index, V_CLIP).astype(jnp.int32)

        def packed(source):
            return jnp.zeros((V_CLIP, source.shape[1]), source.dtype).at[target].set(source, mode="drop")

        query_pack = packed(query_rows)
        key_pack = packed(key_rows)
        value_pack = packed(value_rows)
        cotangent_pack = packed(cotangent_rows)
        output_grad = jnp.dot(cotangent_pack, out_weight.T, preferred_element_type=jnp.float32).astype(jnp.bfloat16)
        attended, grad_query, grad_key, grad_value = lax.map(
            head_pass, (split_heads(query_pack), split_heads(key_pack), split_heads(value_pack), split_heads(output_grad)))
        attended = join_heads(attended)
        terms = jnp.einsum("kpa,kpb->pab", attended.reshape(VIS_DEV, CYCLE, QW).astype(jnp.float32),
                           cotangent_pack.reshape(VIS_DEV, CYCLE, D).astype(jnp.float32))
        rounded = lax.optimization_barrier(terms.astype(jnp.bfloat16)).astype(jnp.float32)
        carry = carry + jnp.sum(rounded, axis=0)
        lookup = jnp.clip(index, 0, V_CLIP - 1).astype(jnp.int32)

        def unpacked(rows):
            return jnp.where(visible[:, None], rows[lookup], jnp.zeros((), rows.dtype))

        return carry, (unpacked(join_heads(grad_query)), unpacked(join_heads(grad_key)), unpacked(join_heads(grad_value)))

    total, grads = lax.scan(one_clip, jnp.zeros((QW, D), jnp.float32),
                            (queries, keys, values, out_cotangent, visible_counts, span_offset))
    weight_grad = total * (CLIPS * V_CLIP) ** -0.5
    return (grads[0], grads[1], grads[2], weight_grad)
```

```python
import jax
import jax.numpy as jnp
from jax import lax
from jax.experimental import pallas as pl
from jax.experimental.pallas import tpu as pltpu
from jax.sharding import PartitionSpec as P

HEADS = 8
HD = 64
VIS_DEV = 48
MAXV = 96


def pick_entry(table, position):
    order = jnp.arange(table.shape[0], dtype=jnp.int32)
    chosen = jnp.where(order[None, :] == position[:, None], table[None, :], 0)
    return jnp.sum(chosen, axis=1)


def split_heads(block):
    return block.reshape(block.shape[0], HEADS, HD).transpose(1, 0, 2)


def join_heads(block):
    return block.transpose(1, 0, 2).reshape(block.shape[1], HEADS * HD)


def query_side(parts):
    query_head, key_head, value_head, dout_head = parts
    factor = HD ** (-0.5)
    scores = (
        lax.dot_general(
            query_head, key_head, (((1,), (1,)), ((), ())), preferred_element_type=jnp.float32
        )
        * factor
    )
    peak_score = jnp.max(scores, axis=1, keepdims=True)
    log_total = peak_score + jnp.log(jnp.sum(jnp.exp(scores - peak_score), axis=1, keepdims=True))
    weights = jnp.exp(scores - log_total)
    weights_low = weights.astype(jnp.bfloat16)
    attended = jnp.dot(weights_low, value_head, preferred_element_type=jnp.float32).astype(
        jnp.bfloat16
    )
    inner_sum = jnp.sum(
        dout_head.astype(jnp.float32) * attended.astype(jnp.float32), axis=1, keepdims=True
    )
    dweights = lax.dot_general(
        dout_head, value_head, (((1,), (1,)), ((), ())), preferred_element_type=jnp.float32
    )
    dscores = (weights * (dweights - inner_sum)).astype(jnp.bfloat16)
    grad_query = (jnp.dot(dscores, key_head, preferred_element_type=jnp.float32) * factor).astype(
        jnp.bfloat16
    )
    return (attended, grad_query, log_total[:, 0], inner_sum[:, 0])


def key_side_add(query_piece, dout_piece, log_piece, inner_piece, key_heads, value_heads):
    factor = HD ** (-0.5)

    def one_head(parts):
        query_head, dout_head, log_head, inner_head, key_head, value_head = parts
        scores = (
            lax.dot_general(
                query_head, key_head, (((1,), (1,)), ((), ())), preferred_element_type=jnp.float32
            )
            * factor
        )
        weights = jnp.exp(scores - log_head[:, None])
        weights_low = weights.astype(jnp.bfloat16)
        value_part = lax.dot_general(
            weights_low, dout_head, (((0,), (0,)), ((), ())), preferred_element_type=jnp.float32
        )
        dweights = lax.dot_general(
            dout_head, value_head, (((1,), (1,)), ((), ())), preferred_element_type=jnp.float32
        )
        dscores = (weights * (dweights - inner_head[:, None])).astype(jnp.bfloat16)
        key_part = lax.dot_general(
            dscores, query_head, (((0,), (0,)), ((), ())), preferred_element_type=jnp.float32
        )
        return (key_part, value_part)

    key_parts, value_parts = lax.map(
        one_head,
        (
            split_heads(query_piece),
            split_heads(dout_piece),
            log_piece.T,
            inner_piece.T,
            key_heads,
            value_heads,
        ),
    )
    return (key_parts, value_parts)


def by_rows(queries, keys, values, out_cotangent, visible_counts, span_offset, out_weight):
    devices = lax.axis_size("seq")
    device = lax.axis_index("seq")
    frames = queries.shape[1]
    visible_rows = VIS_DEV
    capacity = MAXV // devices
    counts = visible_counts[0]
    offsets = span_offset[0]
    shard_ends = jnp.cumsum(counts)
    starts = shard_ends - counts
    this_device = device.reshape(1)
    count_here = pick_entry(counts, this_device)[0]
    start_here = pick_entry(starts, this_device)[0]
    span_begin = pick_entry(offsets, this_device)[0] % (count_here + 1)
    masked = frames - count_here
    send_slots = jnp.arange(devices * capacity, dtype=jnp.int32)
    peer_index = send_slots // capacity
    within = send_slots % capacity
    first_slot = (start_here - peer_index + devices - 1) // devices
    global_index = (first_slot + within) * devices + peer_index
    ranked = global_index - start_here
    live_slot = ranked < count_here
    frame_of = jnp.clip(jnp.where(ranked < span_begin, ranked, ranked + masked), 0, frames - 1)

    def outgoing(block):
        return jnp.where(
            live_slot[:, None], jnp.take(block[0], frame_of, axis=0), jnp.zeros((), block.dtype)
        )

    arrived = (
        lax.all_to_all(outgoing(queries), "seq", split_axis=0, concat_axis=0, tiled=True),
        lax.all_to_all(outgoing(keys), "seq", split_axis=0, concat_axis=0, tiled=True),
        lax.all_to_all(outgoing(values), "seq", split_axis=0, concat_axis=0, tiled=True),
        lax.all_to_all(outgoing(out_cotangent), "seq", split_axis=0, concat_axis=0, tiled=True),
    )
    packed_slot = jnp.arange(visible_rows, dtype=jnp.int32)
    packed_index = packed_slot * devices + device
    owner_shard = jnp.sum((shard_ends[None, :] <= packed_index[:, None]).astype(jnp.int32), axis=1)
    owner_first = (pick_entry(starts, owner_shard) - device + devices - 1) // devices
    arrived_row = owner_shard * capacity + packed_slot - owner_first
    query_pack = jnp.take(arrived[0], arrived_row, axis=0)
    key_pack = jnp.take(arrived[1], arrived_row, axis=0)
    value_pack = jnp.take(arrived[2], arrived_row, axis=0)
    cotangent_pack = jnp.take(arrived[3], arrived_row, axis=0)
    output_grad = lax.dot_general(
        cotangent_pack,
        lax.all_gather(out_weight, "seq", axis=0, tiled=True),
        (((1,), (1,)), ((), ())),
        preferred_element_type=jnp.float32,
    ).astype(jnp.bfloat16)
    key_all, value_all = (
        lax.all_gather(key_pack, "seq", axis=0, tiled=True),
        lax.all_gather(value_pack, "seq", axis=0, tiled=True),
    )
    attended, query_grad, log_totals, inner_sums = lax.map(
        query_side,
        (
            split_heads(query_pack),
            split_heads(key_all),
            split_heads(value_all),
            split_heads(output_grad),
        ),
    )
    attended = join_heads(attended)
    query_grad = join_heads(query_grad)
    log_rows = log_totals.T
    inner_rows = inner_sums.T
    partial_term = lax.dot_general(
        attended, cotangent_pack, (((0,), (0,)), ((), ())), preferred_element_type=jnp.float32
    )
    seq_sum = lax.psum_scatter(
        partial_term.astype(jnp.bfloat16), "seq", scatter_dimension=0, tiled=True
    )
    clip_sum = lax.psum(seq_sum, "clip").astype(jnp.float32)
    weight_grad = clip_sum * (lax.axis_size("clip") * visible_rows * devices) ** (-0.5)
    log_every, inner_every = (
        lax.all_gather(log_rows, "seq", axis=0, tiled=True),
        lax.all_gather(inner_rows, "seq", axis=0, tiled=True),
    )
    key_heads = split_heads(key_pack)
    value_heads = split_heads(value_pack)
    key_sum, value_sum = key_side_add(
        lax.all_gather(query_pack, "seq", axis=0, tiled=True),
        lax.all_gather(output_grad, "seq", axis=0, tiled=True),
        log_every,
        inner_every,
        key_heads,
        value_heads,
    )
    key_grad = join_heads((key_sum * HD ** (-0.5)).astype(jnp.bfloat16))
    value_grad = join_heads(value_sum.astype(jnp.bfloat16))
    back_first = (pick_entry(starts, peer_index) - device + devices - 1) // devices
    back_slot = back_first + within
    back_live = back_slot * devices + device < pick_entry(shard_ends, peer_index)
    back_row = jnp.clip(back_slot, 0, visible_rows - 1)

    def returning(block):
        return jnp.where(
            back_live[:, None], jnp.take(block, back_row, axis=0), jnp.zeros((), block.dtype)
        )

    returned = (
        lax.all_to_all(returning(query_grad), "seq", split_axis=0, concat_axis=0, tiled=True),
        lax.all_to_all(returning(key_grad), "seq", split_axis=0, concat_axis=0, tiled=True),
        lax.all_to_all(returning(value_grad), "seq", split_axis=0, concat_axis=0, tiled=True),
    )
    position = jnp.arange(frames, dtype=jnp.int32)
    visible = (position < span_begin) | (position >= span_begin + masked)
    frame_rank = jnp.where(position < span_begin, position, position - masked)
    frame_global = start_here + frame_rank
    frame_peer = frame_global % devices
    frame_slot = frame_global // devices
    frame_first = (start_here - frame_peer + devices - 1) // devices
    frame_row = jnp.clip(
        frame_peer * capacity + frame_slot - frame_first, 0, devices * capacity - 1
    )

    def placed(block):
        return jnp.where(
            visible[:, None], jnp.take(block, frame_row, axis=0), jnp.zeros((), block.dtype)
        )[None]

    return (placed(returned[0]), placed(returned[1]), placed(returned[2]), weight_grad)


ROUTES = (0, 2, 4, 6)


def head_lanes(core):
    lane = lax.broadcasted_iota(jnp.int32, (1, 128), 1)
    return ((lane // HD) == core).astype(jnp.float32).astype(jnp.bfloat16)


def span_of(counts_ref, offsets_ref, owner):
    count = counts_ref[0, owner]
    begin = lax.rem(offsets_ref[0, owner], count + 1)
    return begin, MAXV - (count - begin)


def slot_masks(begin, end_start):
    slot = lax.broadcasted_iota(jnp.int32, (MAXV, 1), 0)
    early = (slot < begin).astype(jnp.float32).astype(jnp.bfloat16)
    late = (slot >= end_start).astype(jnp.float32).astype(jnp.bfloat16)
    return early, late


def pack_kernel(counts_ref, offsets_ref, q_ref, k_ref, v_ref, g_ref, *rest):
    sends, cot_ref, narrow, wide, sems = rest[:4], rest[4], rest[5], rest[6], rest[7]
    frames = q_ref.shape[1]
    last = frames - MAXV
    device = lax.axis_index("seq")
    copies = []
    for index, source in enumerate((q_ref, k_ref, v_ref)):
        for side, start in enumerate((0, last)):
            copies.append(
                pltpu.make_async_copy(
                    source.at[0, pl.ds(start, MAXV)], narrow.at[index, side], sems.at[len(copies)]
                )
            )
    for side, start in enumerate((0, last)):
        copies.append(
            pltpu.make_async_copy(
                g_ref.at[0, pl.ds(start, MAXV)], wide.at[side], sems.at[len(copies)]
            )
        )
    for copy in copies:
        copy.start()
    begin, end_start = span_of(counts_ref, offsets_ref, device)
    early, late = slot_masks(begin, end_start)
    for copy in copies:
        copy.wait()
    for route, send in zip(ROUTES, sends):
        chip = (device ^ route) // 2
        lanes = pl.ds(pl.multiple_of(chip * 128, 128), 128)
        for index in range(3):
            send[:, index * 128 : (index + 1) * 128] = (
                narrow[index, 0, :, lanes] * early + narrow[index, 1, :, lanes] * late
            )
    cot_ref[...] = wide[0] * early + wide[1] * late


def attend_kernel(counts_ref, offsets_ref, w_ref, *rest):
    blocks, cots = rest[:8], rest[8:16]
    outs, wg_ref = rest[16:24], rest[24]
    packed, cot, dout, dq, sems = rest[25:]
    device = lax.axis_index("seq")
    core = device % 2
    copies = []
    for index in range(8):
        rows = pl.ds(index * MAXV, MAXV)
        copies.append(pltpu.make_async_copy(blocks[index], packed.at[rows], sems.at[index]))
        copies.append(pltpu.make_async_copy(cots[index], cot.at[rows], sems.at[8 + index]))
    for copy in copies:
        copy.start()
    lanes = head_lanes(core)
    top = (core == 0).astype(jnp.float32).astype(jnp.bfloat16)
    bottom = (core == 1).astype(jnp.float32).astype(jnp.bfloat16)
    w_both = jnp.concatenate([w_ref[...] * top, w_ref[...] * bottom], axis=0)
    dead = []
    for index in range(8):
        begin, end_start = span_of(counts_ref, offsets_ref, device ^ index)
        slot = lax.broadcasted_iota(jnp.int32, (MAXV, 256), 0)
        dead.append((slot >= begin) & (slot < end_start))
    dead = jnp.concatenate(dead, axis=0)
    for copy in copies:
        copy.wait()
    factor = HD ** (-0.5)
    dout[...] = lax.dot_general(
        cot[...], w_both, (((1,), (1,)), ((), ())), preferred_element_type=jnp.float32
    ).astype(jnp.bfloat16)
    key = packed[:, 128:256] * lanes
    value = packed[:, 256:384]
    key_t = key.T
    value_t = value.T
    dout_t = dout[...].astype(jnp.float32).T
    key_grad = jnp.zeros((8 * MAXV, 128), jnp.float32)
    value_grad = jnp.zeros((8 * MAXV, 128), jnp.float32)
    attended = []
    for step in range(3):
        rows = slice(step * 256, (step + 1) * 256)
        query = packed[rows, 0:128]
        query_own = query * lanes
        dout_own = dout[rows, :]
        scores = (
            lax.dot_general(
                key, query, (((1,), (1,)), ((), ())), preferred_element_type=jnp.float32
            )
            * factor
        )
        scores = jnp.where(dead, -1e30, scores)
        scores = jnp.exp(scores - jnp.max(scores, axis=0, keepdims=True))
        weights = scores * (1.0 / jnp.sum(scores, axis=0, keepdims=True))
        low = weights.astype(jnp.bfloat16)
        att = jnp.dot(value_t, low, preferred_element_type=jnp.float32).astype(jnp.bfloat16)
        attended.append(att)
        inner = jnp.sum(dout_t[:, rows] * att.astype(jnp.float32), axis=0, keepdims=True)
        dweights = lax.dot_general(
            value, dout_own, (((1,), (1,)), ((), ())), preferred_element_type=jnp.float32
        )
        dscores = (weights * (dweights - inner)).astype(jnp.bfloat16)
        value_grad += jnp.dot(low, dout_own, preferred_element_type=jnp.float32)
        key_grad += jnp.dot(dscores, query_own, preferred_element_type=jnp.float32)
        dq_t = jnp.dot(key_t, dscores, preferred_element_type=jnp.float32) * factor
        dq[rows, :] = dq_t.T.astype(jnp.bfloat16)
    key_grad = (key_grad * factor).astype(jnp.bfloat16)
    value_grad = value_grad.astype(jnp.bfloat16)
    for index in range(8):
        rows = slice(index * MAXV, (index + 1) * MAXV)
        outs[index][:, 0:128] = dq[rows, :]
        outs[index][:, 128:256] = key_grad[rows]
        outs[index][:, 256:384] = value_grad[rows]
    att = jnp.concatenate(attended, axis=1)
    att = jnp.where(core == 0, att[:HD].astype(jnp.float32), att[HD:].astype(jnp.float32))
    wg_ref[...] = jnp.dot(
        att.astype(jnp.bfloat16), cot[...], preferred_element_type=jnp.float32
    ).astype(jnp.bfloat16)


def combine_kernel(*refs):
    for index in range(4):
        refs[8 + index][...] = refs[index][...] + refs[4 + index][...]


def unpack_kernel(counts_ref, offsets_ref, *rest):
    blocks, outs = rest[:4], rest[4:7]
    edges, blank, sems = rest[7:]
    device = lax.axis_index("seq")
    frames = outs[0].shape[1]
    last = frames - MAXV
    blank[...] = jnp.zeros_like(blank)
    copies = []
    for index in range(3):
        copies.append(
            pltpu.make_async_copy(
                blank, outs[index].at[0, pl.ds(MAXV, last - MAXV)], sems.at[index]
            )
        )
        copies[-1].start()
    begin, end_start = span_of(counts_ref, offsets_ref, device)
    sides = slot_masks(begin, end_start)
    for route, block in zip(ROUTES, blocks):
        chip = (device ^ route) // 2
        lanes = pl.ds(pl.multiple_of(chip * 128, 128), 128)
        for index in range(3):
            piece = block[:, index * 128 : (index + 1) * 128]
            for side in range(2):
                edges[index, side, :, lanes] = piece * sides[side]
    for index in range(3):
        for side, start in enumerate((0, last)):
            copies.append(
                pltpu.make_async_copy(
                    edges.at[index, side],
                    outs[index].at[0, pl.ds(start, MAXV)],
                    sems.at[len(copies)],
                )
            )
            copies[-1].start()
    for copy in copies:
        copy.wait()


ANYWHERE = pl.BlockSpec(memory_space=pl.ANY)
SCALARS = pl.BlockSpec(memory_space=pltpu.SMEM)
LOCAL = pl.BlockSpec(memory_space=pltpu.VMEM)


def by_heads(queries, keys, values, out_cotangent, visible_counts, span_offset, out_weight):
    bf16 = jnp.bfloat16
    pairs = lax.axis_size("seq")
    clips = lax.axis_size("clip")

    def shift(block, step):
        return lax.ppermute(block, "seq", [(i, i ^ step) for i in range(pairs)])

    narrow = jax.ShapeDtypeStruct((MAXV, 384), bf16)
    wide = jax.ShapeDtypeStruct((MAXV, out_cotangent.shape[2]), bf16)
    *sends, cot = pl.pallas_call(
        pack_kernel,
        out_shape=[narrow] * 4 + [wide],
        in_specs=[SCALARS] * 2 + [ANYWHERE] * 4,
        out_specs=[LOCAL] * 5,
        scratch_shapes=[
            pltpu.VMEM((3, 2, MAXV, queries.shape[2]), bf16),
            pltpu.VMEM((2, MAXV, out_cotangent.shape[2]), bf16),
            pltpu.SemaphoreType.DMA((8,)),
        ],
        name="pack",
    )(visible_counts, span_offset, queries, keys, values, out_cotangent)
    even = [sends[0]] + [shift(sends[i], ROUTES[i]) for i in (1, 2, 3)]
    even_cot = [cot] + [shift(cot, ROUTES[i]) for i in (1, 2, 3)]
    odd = [shift(block, 1) for block in even]
    odd_cot = [shift(block, 1) for block in even_cot]
    blocks = [block for pair in zip(even, odd) for block in pair]
    cots = [block for pair in zip(even_cot, odd_cot) for block in pair]
    *grads, partial = pl.pallas_call(
        attend_kernel,
        out_shape=[narrow] * 8 + [jax.ShapeDtypeStruct(out_weight.shape, bf16)],
        in_specs=[SCALARS] * 2 + [LOCAL] + [ANYWHERE] * 16,
        out_specs=[LOCAL] * 9,
        scratch_shapes=[
            pltpu.VMEM((8 * MAXV, 384), bf16),
            pltpu.VMEM((8 * MAXV, out_cotangent.shape[2]), bf16),
            pltpu.VMEM((8 * MAXV, 128), bf16),
            pltpu.VMEM((8 * MAXV, 128), bf16),
            pltpu.SemaphoreType.DMA((16,)),
        ],
        name="attend",
    )(visible_counts, span_offset, out_weight, *blocks, *cots)
    crossed = [shift(grads[i + 1], 1) for i in ROUTES]
    joined = pl.pallas_call(
        combine_kernel,
        out_shape=[narrow] * 4,
        in_specs=[LOCAL] * 8,
        out_specs=[LOCAL] * 4,
        name="combine",
    )(*[grads[i] for i in ROUTES], *crossed)
    home = [joined[0]] + [shift(joined[i], ROUTES[i]) for i in (1, 2, 3)]
    full = jax.ShapeDtypeStruct(queries.shape, bf16)
    frames = queries.shape[1]
    outs = pl.pallas_call(
        unpack_kernel,
        out_shape=[full] * 3,
        in_specs=[SCALARS] * 2 + [LOCAL] * 4,
        out_specs=[ANYWHERE] * 3,
        scratch_shapes=[
            pltpu.VMEM((3, 2, MAXV, queries.shape[2]), bf16),
            pltpu.VMEM((frames - 2 * MAXV, queries.shape[2]), bf16),
            pltpu.SemaphoreType.DMA((9,)),
        ],
        name="unpack",
    )(visible_counts, span_offset, *home)
    step = 1
    while step < clips:
        other = lax.ppermute(partial, "clip", [(i, i ^ step) for i in range(clips)])
        total = partial.astype(jnp.float32) + other.astype(jnp.float32)
        partial = total.astype(bf16)
        step *= 2
    weight_grad = total * (clips * VIS_DEV * pairs) ** (-0.5)
    return (*outs, weight_grad)


def local(*arrays):
    if lax.axis_size("seq") == HEADS and lax.axis_size("clip") in (2, 4, 8, 16):
        return by_heads(*arrays)
    return by_rows(*arrays)


def solution(mesh):
    placed = (
        P("clip", "seq", None),
        P("clip", "seq", None),
        P("clip", "seq", None),
        P("clip", "seq", None),
        P("clip", None),
        P("clip", None),
        P("seq", None),
    )
    return jax.shard_map(
        local,
        mesh=mesh,
        in_specs=placed,
        out_specs=(
            P("clip", "seq", None),
            P("clip", "seq", None),
            P("clip", "seq", None),
            P("seq", None),
        ),
        check_vma=False,
    )
```

```python
import functools

import jax
import jax.numpy as jnp
from jax import lax
from jax.experimental import pallas as pl
from jax.experimental.pallas import tpu as pltpu
from jax.sharding import PartitionSpec as P


HEADS = 8
HD = 64
VIS_DEV = 48
MAXV = 96


def pick_entry(table, position):
    order = jnp.arange(table.shape[0], dtype=jnp.int32)
    chosen = jnp.where(order[None, :] == position[:, None], table[None, :], 0)
    return jnp.sum(chosen, axis=1)


def split_heads(block):
    return block.reshape(block.shape[0], HEADS, HD).transpose(1, 0, 2)


def join_heads(block):
    return block.transpose(1, 0, 2).reshape(block.shape[1], HEADS * HD)


def query_side(parts):
    query_head, key_head, value_head, dout_head = parts
    factor = HD ** (-0.5)
    scores = (
        lax.dot_general(
            query_head, key_head, (((1,), (1,)), ((), ())), preferred_element_type=jnp.float32
        )
        * factor
    )
    peak_score = jnp.max(scores, axis=1, keepdims=True)
    log_total = peak_score + jnp.log(jnp.sum(jnp.exp(scores - peak_score), axis=1, keepdims=True))
    weights = jnp.exp(scores - log_total)
    weights_low = weights.astype(jnp.bfloat16)
    attended = jnp.dot(weights_low, value_head, preferred_element_type=jnp.float32).astype(
        jnp.bfloat16
    )
    inner_sum = jnp.sum(
        dout_head.astype(jnp.float32) * attended.astype(jnp.float32), axis=1, keepdims=True
    )
    dweights = lax.dot_general(
        dout_head, value_head, (((1,), (1,)), ((), ())), preferred_element_type=jnp.float32
    )
    dscores = (weights * (dweights - inner_sum)).astype(jnp.bfloat16)
    grad_query = (jnp.dot(dscores, key_head, preferred_element_type=jnp.float32) * factor).astype(
        jnp.bfloat16
    )
    return (attended, grad_query, log_total[:, 0], inner_sum[:, 0])


def key_side_add(query_piece, dout_piece, log_piece, inner_piece, key_heads, value_heads):
    factor = HD ** (-0.5)

    def one_head(parts):
        query_head, dout_head, log_head, inner_head, key_head, value_head = parts
        scores = (
            lax.dot_general(
                query_head, key_head, (((1,), (1,)), ((), ())), preferred_element_type=jnp.float32
            )
            * factor
        )
        weights = jnp.exp(scores - log_head[:, None])
        weights_low = weights.astype(jnp.bfloat16)
        value_part = lax.dot_general(
            weights_low, dout_head, (((0,), (0,)), ((), ())), preferred_element_type=jnp.float32
        )
        dweights = lax.dot_general(
            dout_head, value_head, (((1,), (1,)), ((), ())), preferred_element_type=jnp.float32
        )
        dscores = (weights * (dweights - inner_head[:, None])).astype(jnp.bfloat16)
        key_part = lax.dot_general(
            dscores, query_head, (((0,), (0,)), ((), ())), preferred_element_type=jnp.float32
        )
        return (key_part, value_part)

    key_parts, value_parts = lax.map(
        one_head,
        (
            split_heads(query_piece),
            split_heads(dout_piece),
            log_piece.T,
            inner_piece.T,
            key_heads,
            value_heads,
        ),
    )
    return (key_parts, value_parts)


def by_rows(queries, keys, values, out_cotangent, visible_counts, span_offset, out_weight):
    devices = lax.axis_size("seq")
    device = lax.axis_index("seq")
    frames = queries.shape[1]
    visible_rows = VIS_DEV
    capacity = MAXV // devices
    counts = visible_counts[0]
    offsets = span_offset[0]
    shard_ends = jnp.cumsum(counts)
    starts = shard_ends - counts
    this_device = device.reshape(1)
    count_here = pick_entry(counts, this_device)[0]
    start_here = pick_entry(starts, this_device)[0]
    span_begin = pick_entry(offsets, this_device)[0] % (count_here + 1)
    masked = frames - count_here
    send_slots = jnp.arange(devices * capacity, dtype=jnp.int32)
    peer_index = send_slots // capacity
    within = send_slots % capacity
    first_slot = (start_here - peer_index + devices - 1) // devices
    global_index = (first_slot + within) * devices + peer_index
    ranked = global_index - start_here
    live_slot = ranked < count_here
    frame_of = jnp.clip(jnp.where(ranked < span_begin, ranked, ranked + masked), 0, frames - 1)

    def outgoing(block):
        return jnp.where(
            live_slot[:, None], jnp.take(block[0], frame_of, axis=0), jnp.zeros((), block.dtype)
        )

    arrived = (
        lax.all_to_all(outgoing(queries), "seq", split_axis=0, concat_axis=0, tiled=True),
        lax.all_to_all(outgoing(keys), "seq", split_axis=0, concat_axis=0, tiled=True),
        lax.all_to_all(outgoing(values), "seq", split_axis=0, concat_axis=0, tiled=True),
        lax.all_to_all(outgoing(out_cotangent), "seq", split_axis=0, concat_axis=0, tiled=True),
    )
    packed_slot = jnp.arange(visible_rows, dtype=jnp.int32)
    packed_index = packed_slot * devices + device
    owner_shard = jnp.sum((shard_ends[None, :] <= packed_index[:, None]).astype(jnp.int32), axis=1)
    owner_first = (pick_entry(starts, owner_shard) - device + devices - 1) // devices
    arrived_row = owner_shard * capacity + packed_slot - owner_first
    query_pack = jnp.take(arrived[0], arrived_row, axis=0)
    key_pack = jnp.take(arrived[1], arrived_row, axis=0)
    value_pack = jnp.take(arrived[2], arrived_row, axis=0)
    cotangent_pack = jnp.take(arrived[3], arrived_row, axis=0)
    output_grad = lax.dot_general(
        cotangent_pack,
        lax.all_gather(out_weight, "seq", axis=0, tiled=True),
        (((1,), (1,)), ((), ())),
        preferred_element_type=jnp.float32,
    ).astype(jnp.bfloat16)
    key_all, value_all = (
        lax.all_gather(key_pack, "seq", axis=0, tiled=True),
        lax.all_gather(value_pack, "seq", axis=0, tiled=True),
    )
    attended, query_grad, log_totals, inner_sums = lax.map(
        query_side,
        (
            split_heads(query_pack),
            split_heads(key_all),
            split_heads(value_all),
            split_heads(output_grad),
        ),
    )
    attended = join_heads(attended)
    query_grad = join_heads(query_grad)
    log_rows = log_totals.T
    inner_rows = inner_sums.T
    partial_term = lax.dot_general(
        attended, cotangent_pack, (((0,), (0,)), ((), ())), preferred_element_type=jnp.float32
    )
    seq_sum = lax.psum_scatter(
        partial_term.astype(jnp.bfloat16), "seq", scatter_dimension=0, tiled=True
    )
    clip_sum = lax.psum(seq_sum, "clip").astype(jnp.float32)
    weight_grad = clip_sum * (lax.axis_size("clip") * visible_rows * devices) ** (-0.5)
    log_every, inner_every = (
        lax.all_gather(log_rows, "seq", axis=0, tiled=True),
        lax.all_gather(inner_rows, "seq", axis=0, tiled=True),
    )
    key_heads = split_heads(key_pack)
    value_heads = split_heads(value_pack)
    key_sum, value_sum = key_side_add(
        lax.all_gather(query_pack, "seq", axis=0, tiled=True),
        lax.all_gather(output_grad, "seq", axis=0, tiled=True),
        log_every,
        inner_every,
        key_heads,
        value_heads,
    )
    key_grad = join_heads((key_sum * HD ** (-0.5)).astype(jnp.bfloat16))
    value_grad = join_heads(value_sum.astype(jnp.bfloat16))
    back_first = (pick_entry(starts, peer_index) - device + devices - 1) // devices
    back_slot = back_first + within
    back_live = back_slot * devices + device < pick_entry(shard_ends, peer_index)
    back_row = jnp.clip(back_slot, 0, visible_rows - 1)

    def returning(block):
        return jnp.where(
            back_live[:, None], jnp.take(block, back_row, axis=0), jnp.zeros((), block.dtype)
        )

    returned = (
        lax.all_to_all(returning(query_grad), "seq", split_axis=0, concat_axis=0, tiled=True),
        lax.all_to_all(returning(key_grad), "seq", split_axis=0, concat_axis=0, tiled=True),
        lax.all_to_all(returning(value_grad), "seq", split_axis=0, concat_axis=0, tiled=True),
    )
    position = jnp.arange(frames, dtype=jnp.int32)
    visible = (position < span_begin) | (position >= span_begin + masked)
    frame_rank = jnp.where(position < span_begin, position, position - masked)
    frame_global = start_here + frame_rank
    frame_peer = frame_global % devices
    frame_slot = frame_global // devices
    frame_first = (start_here - frame_peer + devices - 1) // devices
    frame_row = jnp.clip(
        frame_peer * capacity + frame_slot - frame_first, 0, devices * capacity - 1
    )

    def placed(block):
        return jnp.where(
            visible[:, None], jnp.take(block, frame_row, axis=0), jnp.zeros((), block.dtype)
        )[None]

    return (placed(returned[0]), placed(returned[1]), placed(returned[2]), weight_grad)


ROUTES = (0, 2, 4, 6)
HALF = MAXV // 2


def head_lanes(core):
    lane = lax.broadcasted_iota(jnp.int32, (1, 128), 1)
    return ((lane // HD) == core).astype(jnp.float32).astype(jnp.bfloat16)


def scalar_copies(sources, targets, sems):
    copies = [
        pltpu.make_async_copy(source, target, sems.at[index])
        for index, (source, target) in enumerate(zip(sources, targets))
    ]
    for copy in copies:
        copy.start()
    return copies


def span_of(counts_ref, offsets_ref, owner):
    count = counts_ref[0, owner]
    begin = lax.rem(offsets_ref[0, owner], count + 1)
    return begin, MAXV - (count - begin)


def slot_masks(begin, end_start):
    slot = lax.broadcasted_iota(jnp.int32, (MAXV, 1), 0)
    early = (slot < begin).astype(jnp.float32).astype(jnp.bfloat16)
    late = (slot >= end_start).astype(jnp.float32).astype(jnp.bfloat16)
    return early, late


def pack_kernel(counts_hbm, offsets_hbm, q_ref, k_ref, v_ref, g_ref, *rest):
    sends, cot_refs = rest[:4], rest[4:7]
    narrow, wide, counts_ref, offsets_ref, sems, scalar_sems = rest[7:]
    scalars = scalar_copies((counts_hbm, offsets_hbm), (counts_ref, offsets_ref), scalar_sems)
    frames = q_ref.shape[1]
    last = frames - MAXV
    device = lax.axis_index("seq")
    copies = []
    for index, source in enumerate((q_ref, k_ref, v_ref)):
        for side, start in enumerate((0, last)):
            copies.append(
                pltpu.make_async_copy(
                    source.at[0, pl.ds(start, MAXV)], narrow.at[index, side], sems.at[len(copies)]
                )
            )
    for side, start in enumerate((0, last)):
        copies.append(
            pltpu.make_async_copy(
                g_ref.at[0, pl.ds(start, MAXV)], wide.at[side], sems.at[len(copies)]
            )
        )
    for copy in copies:
        copy.start()
    for copy in scalars:
        copy.wait()
    begin, end_start = span_of(counts_ref, offsets_ref, device)
    early, late = slot_masks(begin, end_start)
    for copy in copies[:6]:
        copy.wait()
    for route, send in zip(ROUTES, sends):
        chip = (device ^ route) // 2
        lanes = pl.ds(pl.multiple_of(chip * 128, 128), 128)
        for index in range(3):
            send[:, index * 128 : (index + 1) * 128] = (
                narrow[index, 0, :, lanes] * early + narrow[index, 1, :, lanes] * late
            )
    for copy in copies[6:]:
        copy.wait()
    cot = wide[0] * early + wide[1] * late
    cot_refs[0][...] = cot
    cot_refs[1][...] = cot[:HALF]
    cot_refs[2][...] = cot[HALF:]


def forward_kernel(counts_hbm, offsets_hbm, *rest):
    blocks = rest[:8]
    packed, weights_ref, attended_ref, counts_ref, offsets_ref, sems, scalar_sems = rest[8:]
    scalars = scalar_copies((counts_hbm, offsets_hbm), (counts_ref, offsets_ref), scalar_sems)
    device = lax.axis_index("seq")
    core = device % 2
    copies = []
    for index in range(8):
        rows = pl.ds(index * MAXV, MAXV)
        copies.append(pltpu.make_async_copy(blocks[index], packed.at[rows], sems.at[index]))
        copies[-1].start()
    lanes = head_lanes(core)
    for copy in scalars:
        copy.wait()
    dead = []
    for index in range(8):
        begin, end_start = span_of(counts_ref, offsets_ref, device ^ index)
        slot = lax.broadcasted_iota(jnp.int32, (MAXV, 256), 0)
        dead.append((slot >= begin) & (slot < end_start))
    dead = jnp.concatenate(dead, axis=0)
    for copy in copies:
        copy.wait()
    factor = HD ** (-0.5)
    key = packed[:, 128:256] * lanes
    value_t = packed[:, 256:384].T
    for step in range(3):
        rows = slice(step * 256, (step + 1) * 256)
        scores = (
            lax.dot_general(
                key, packed[rows, 0:128], (((1,), (1,)), ((), ())), preferred_element_type=jnp.float32
            )
            * factor
        )
        scores = jnp.where(dead, -1e30, scores)
        scores = jnp.exp(scores - jnp.max(scores, axis=0, keepdims=True))
        weights = scores * (1.0 / jnp.sum(scores, axis=0, keepdims=True))
        weights_ref[:, rows] = weights
        attended_ref[:, rows] = jnp.dot(
            value_t, weights.astype(jnp.bfloat16), preferred_element_type=jnp.float32
        ).astype(jnp.bfloat16)


def own_rows(ref, core, columns):
    both = ref[:, columns].astype(jnp.float32)
    return jnp.where(core == 0, both[:HD], both[HD:]).astype(jnp.bfloat16)


def project(cot, w_ref, core):
    top = (core == 0).astype(jnp.float32).astype(jnp.bfloat16)
    bottom = (core == 1).astype(jnp.float32).astype(jnp.bfloat16)
    w_both = jnp.concatenate([w_ref[...] * top, w_ref[...] * bottom], axis=0)
    return lax.dot_general(
        cot[...], w_both, (((1,), (1,)), ((), ())), preferred_element_type=jnp.float32
    ).astype(jnp.bfloat16)


def early_kernel(attended_ref, w_ref, *rest):
    cots, dout_ref, wg_ref, cot = rest[:6], rest[6], rest[7], rest[8]
    core = lax.axis_index("seq") % 2
    for index in range(6):
        cot[index * MAXV : (index + 1) * MAXV, :] = cots[index][...]
    dout_ref[...] = project(cot, w_ref, core)
    wg_ref[...] = jnp.dot(
        own_rows(attended_ref, core, slice(0, 6 * MAXV)),
        cot[...],
        preferred_element_type=jnp.float32,
    )


def late_kernel(attended_ref, w_ref, begun_ref, *rest):
    cots, dout_ref, wg_ref, cot = rest[:2], rest[2], rest[3], rest[4]
    core = lax.axis_index("seq") % 2
    for index in range(2):
        cot[index * MAXV : (index + 1) * MAXV, :] = cots[index][...]
    dout_ref[...] = project(cot, w_ref, core)
    wg_ref[...] = (
        begun_ref[...]
        + jnp.dot(
            own_rows(attended_ref, core, slice(6 * MAXV, 8 * MAXV)),
            cot[...],
            preferred_element_type=jnp.float32,
        )
    ).astype(jnp.bfloat16)


def backward_kernel(packed, weights_ref, attended_ref, begun_ref, ended_ref, *rest):
    outs = rest[:8]
    dout, dq = rest[8:]
    core = lax.axis_index("seq") % 2
    lanes = head_lanes(core)
    dout[: 6 * MAXV, :] = begun_ref[...]
    dout[6 * MAXV :, :] = ended_ref[...]
    key_t = (packed[:, 128:256] * lanes).T
    value = packed[:, 256:384]
    factor = HD ** (-0.5)
    dout_t = dout[...].astype(jnp.float32).T
    key_grad = jnp.zeros((8 * MAXV, 128), jnp.float32)
    value_grad = jnp.zeros((8 * MAXV, 128), jnp.float32)
    for step in range(3):
        rows = slice(step * 256, (step + 1) * 256)
        query_own = packed[rows, 0:128] * lanes
        dout_own = dout[rows, :]
        weights = weights_ref[:, rows]
        inner = jnp.sum(
            dout_t[:, rows] * attended_ref[:, rows].astype(jnp.float32), axis=0, keepdims=True
        )
        dweights = lax.dot_general(
            value, dout_own, (((1,), (1,)), ((), ())), preferred_element_type=jnp.float32
        )
        dscores = (weights * (dweights - inner)).astype(jnp.bfloat16)
        value_grad += jnp.dot(
            weights.astype(jnp.bfloat16), dout_own, preferred_element_type=jnp.float32
        )
        key_grad += jnp.dot(dscores, query_own, preferred_element_type=jnp.float32)
        dq_t = jnp.dot(key_t, dscores, preferred_element_type=jnp.float32) * factor
        dq[rows, :] = dq_t.T.astype(jnp.bfloat16)
    key_grad = (key_grad * factor).astype(jnp.bfloat16)
    value_grad = value_grad.astype(jnp.bfloat16)
    for index in range(8):
        rows = slice(index * MAXV, (index + 1) * MAXV)
        outs[index][:, 0:128] = dq[rows, :]
        outs[index][:, 128:256] = key_grad[rows]
        outs[index][:, 256:384] = value_grad[rows]


def combine_kernel(*refs):
    for index in range(4):
        refs[8 + index][...] = refs[index][...] + refs[4 + index][...]


def unpack_kernel(scale, counts_hbm, offsets_hbm, *rest):
    blocks, shares = rest[:4], rest[4:-10]
    outs, wg_ref = rest[-10:-7], rest[-7]
    edges, blank, counts_ref, offsets_ref, sems, scalar_sems = rest[-6:]
    scalars = scalar_copies((counts_hbm, offsets_hbm), (counts_ref, offsets_ref), scalar_sems)
    device = lax.axis_index("seq")
    frames = outs[0].shape[1]
    last = frames - MAXV
    blank[...] = jnp.zeros_like(blank)
    copies = []
    for index in range(3):
        copies.append(
            pltpu.make_async_copy(
                blank, outs[index].at[0, pl.ds(MAXV, last - MAXV)], sems.at[index]
            )
        )
        copies[-1].start()
    for copy in scalars:
        copy.wait()
    begin, end_start = span_of(counts_ref, offsets_ref, device)
    sides = slot_masks(begin, end_start)
    for route, block in zip(ROUTES, blocks):
        chip = (device ^ route) // 2
        lanes = pl.ds(pl.multiple_of(chip * 128, 128), 128)
        for index in range(3):
            piece = block[:, index * 128 : (index + 1) * 128]
            for side in range(2):
                edges[index, side, :, lanes] = piece * sides[side]
    for index in range(3):
        for side, start in enumerate((0, last)):
            copies.append(
                pltpu.make_async_copy(
                    edges.at[index, side],
                    outs[index].at[0, pl.ds(start, MAXV)],
                    sems.at[len(copies)],
                )
            )
            copies[-1].start()
    terms = [share[...].astype(jnp.float32) for share in shares]
    while len(terms) > 1:
        terms = [left + right for left, right in zip(terms[::2], terms[1::2])]
    wg_ref[...] = terms[0] * scale
    for copy in copies:
        copy.wait()


PARAMS = pltpu.CompilerParams(vmem_limit_bytes=24 << 20)
ANYWHERE = pl.BlockSpec(memory_space=pl.ANY)
SCALARS = pl.BlockSpec(memory_space=pltpu.SMEM)
LOCAL = pl.BlockSpec(memory_space=pltpu.VMEM)


def in_hbm(block):
    return pltpu.with_memory_space_constraint(block, pltpu.HBM)


def by_heads(queries, keys, values, out_cotangent, visible_counts, span_offset, out_weight):
    bf16 = jnp.bfloat16
    pairs = lax.axis_size("seq")
    clips = lax.axis_size("clip")

    def shift(block, step):
        return lax.ppermute(block, "seq", [(i, i ^ step) for i in range(pairs)])

    narrow = jax.ShapeDtypeStruct((MAXV, 384), bf16)
    wide = jax.ShapeDtypeStruct((MAXV, out_cotangent.shape[2]), bf16)

    def seen(kernel, outs, specs, operands, scratch=(), out_specs=None):
        return pl.pallas_call(
            kernel,
            out_shape=outs,
            in_specs=specs,
            out_specs=out_specs or [LOCAL] * len(outs),
            scratch_shapes=scratch,
            compiler_params=PARAMS,
        )(*operands)

    width = out_cotangent.shape[2]
    rows = 8 * MAXV
    counts, offsets = in_hbm(visible_counts), in_hbm(span_offset)
    table = pltpu.SMEM(visible_counts.shape, jnp.int32)
    tables = [table, table]
    pair_sems = pltpu.SemaphoreType.DMA((2,))
    half = jax.ShapeDtypeStruct((HALF, width), bf16)
    *sends, cot, cot_a, cot_b = seen(
        pack_kernel,
        [narrow] * 4 + [wide, half, half],
        [ANYWHERE] * 6,
        (counts, offsets, *map(in_hbm, (queries, keys, values, out_cotangent))),
        [
            pltpu.VMEM((3, 2, MAXV, queries.shape[2]), bf16),
            pltpu.VMEM((2, MAXV, width), bf16),
            *tables,
            pltpu.SemaphoreType.DMA((8,)),
            pair_sems,
        ],
    )
    even = [sends[0]] + [shift(sends[i], ROUTES[i]) for i in (1, 2, 3)]
    x_a, y_b = shift(cot_a, 2), shift(cot_b, 4)
    x_b, y_a = shift(cot_b, 2), shift(cot_a, 4)
    d_a, d_b = shift(x_a, 4), shift(y_b, 2)
    even_cot = [cot] + [
        jnp.concatenate(pair, axis=0) for pair in ((x_a, x_b), (y_a, y_b), (d_a, d_b))
    ]
    odd = [shift(block, 1) for block in even]
    odd_cot = [shift(block, 1) for block in even_cot]
    blocks = [block for pair in zip(even, odd) for block in pair]
    cots = [block for pair in zip(even_cot, odd_cot) for block in pair]
    packed, weights, attended = seen(
        forward_kernel,
        [
            pltpu.VMEM((rows, 384), bf16),
            pltpu.VMEM((rows, rows), jnp.float32),
            pltpu.VMEM((128, rows), bf16),
        ],
        [ANYWHERE] * 2 + [LOCAL] * 8,
        (counts, offsets, *blocks),
        [*tables, pltpu.SemaphoreType.DMA((8,)), pair_sems],
    )
    begun, begun_wg = seen(
        early_kernel,
        [pltpu.VMEM((6 * MAXV, 128), bf16), pltpu.VMEM(out_weight.shape, jnp.float32)],
        [LOCAL] * 8,
        (attended, out_weight, *cots[:6]),
        [pltpu.VMEM((6 * MAXV, width), bf16)],
    )
    ended, partial = seen(
        late_kernel,
        [pltpu.VMEM((2 * MAXV, 128), bf16), jax.ShapeDtypeStruct(out_weight.shape, bf16)],
        [LOCAL] * 5,
        (attended, out_weight, begun_wg, *cots[6:]),
        [pltpu.VMEM((2 * MAXV, width), bf16)],
    )
    shares = [partial]
    for step in range(1, clips):
        shares.append(lax.ppermute(partial, "clip", [(i, i ^ step) for i in range(clips)]))
    grads = seen(
        backward_kernel,
        [narrow] * 8,
        [LOCAL] * 5,
        (packed, weights, attended, begun, ended),
        [pltpu.VMEM((rows, 128), bf16)] * 2,
    )
    crossed = [shift(grads[i + 1], 1) for i in ROUTES]
    joined = seen(
        combine_kernel, [narrow] * 4, [LOCAL] * 8, (*[grads[i] for i in ROUTES], *crossed)
    )
    home = [joined[0]] + [shift(joined[i], ROUTES[i]) for i in (1, 2, 3)]
    frames = queries.shape[1]
    scale = (clips * VIS_DEV * pairs) ** (-0.5)
    return tuple(
        seen(
            functools.partial(unpack_kernel, scale),
            [jax.ShapeDtypeStruct(queries.shape, bf16)] * 3
            + [jax.ShapeDtypeStruct(out_weight.shape, jnp.float32)],
            [ANYWHERE] * 2 + [LOCAL] * (4 + len(shares)),
            (counts, offsets, *home, *shares),
            [
                pltpu.VMEM((3, 2, MAXV, queries.shape[2]), bf16),
                pltpu.VMEM((frames - 2 * MAXV, queries.shape[2]), bf16),
                *tables,
                pltpu.SemaphoreType.DMA((9,)),
                pair_sems,
            ],
            [ANYWHERE] * 3 + [LOCAL],
        )
    )


def local(*arrays):
    if lax.axis_size("seq") == HEADS and lax.axis_size("clip") in (2, 4, 8, 16):
        return by_heads(*arrays)
    return by_rows(*arrays)


def solution(mesh):
    placed = (
        P("clip", "seq", None),
        P("clip", "seq", None),
        P("clip", "seq", None),
        P("clip", "seq", None),
        P("clip", None),
        P("clip", None),
        P("seq", None),
    )
    return jax.shard_map(
        local,
        mesh=mesh,
        in_specs=placed,
        out_specs=(
            P("clip", "seq", None),
            P("clip", "seq", None),
            P("clip", "seq", None),
            P("seq", None),
        ),
        check_vma=False,
    )
```

```python
import functools

import jax
import jax.numpy as jnp
from jax import lax
from jax.experimental import pallas as pl
from jax.experimental.pallas import tpu as pltpu
from jax.sharding import PartitionSpec as P


HEADS = 8
HD = 64
VIS_DEV = 48
MAXV = 96


def pick_entry(table, position):
    order = jnp.arange(table.shape[0], dtype=jnp.int32)
    chosen = jnp.where(order[None, :] == position[:, None], table[None, :], 0)
    return jnp.sum(chosen, axis=1)


def split_heads(block):
    return block.reshape(block.shape[0], HEADS, HD).transpose(1, 0, 2)


def join_heads(block):
    return block.transpose(1, 0, 2).reshape(block.shape[1], HEADS * HD)


def query_side(parts):
    query_head, key_head, value_head, dout_head = parts
    factor = HD ** (-0.5)
    scores = (
        lax.dot_general(
            query_head, key_head, (((1,), (1,)), ((), ())), preferred_element_type=jnp.float32
        )
        * factor
    )
    peak_score = jnp.max(scores, axis=1, keepdims=True)
    log_total = peak_score + jnp.log(jnp.sum(jnp.exp(scores - peak_score), axis=1, keepdims=True))
    weights = jnp.exp(scores - log_total)
    weights_low = weights.astype(jnp.bfloat16)
    attended = jnp.dot(weights_low, value_head, preferred_element_type=jnp.float32).astype(
        jnp.bfloat16
    )
    inner_sum = jnp.sum(
        dout_head.astype(jnp.float32) * attended.astype(jnp.float32), axis=1, keepdims=True
    )
    dweights = lax.dot_general(
        dout_head, value_head, (((1,), (1,)), ((), ())), preferred_element_type=jnp.float32
    )
    dscores = (weights * (dweights - inner_sum)).astype(jnp.bfloat16)
    grad_query = (jnp.dot(dscores, key_head, preferred_element_type=jnp.float32) * factor).astype(
        jnp.bfloat16
    )
    return (attended, grad_query, log_total[:, 0], inner_sum[:, 0])


def key_side_add(query_piece, dout_piece, log_piece, inner_piece, key_heads, value_heads):
    factor = HD ** (-0.5)

    def one_head(parts):
        query_head, dout_head, log_head, inner_head, key_head, value_head = parts
        scores = (
            lax.dot_general(
                query_head, key_head, (((1,), (1,)), ((), ())), preferred_element_type=jnp.float32
            )
            * factor
        )
        weights = jnp.exp(scores - log_head[:, None])
        weights_low = weights.astype(jnp.bfloat16)
        value_part = lax.dot_general(
            weights_low, dout_head, (((0,), (0,)), ((), ())), preferred_element_type=jnp.float32
        )
        dweights = lax.dot_general(
            dout_head, value_head, (((1,), (1,)), ((), ())), preferred_element_type=jnp.float32
        )
        dscores = (weights * (dweights - inner_head[:, None])).astype(jnp.bfloat16)
        key_part = lax.dot_general(
            dscores, query_head, (((0,), (0,)), ((), ())), preferred_element_type=jnp.float32
        )
        return (key_part, value_part)

    key_parts, value_parts = lax.map(
        one_head,
        (
            split_heads(query_piece),
            split_heads(dout_piece),
            log_piece.T,
            inner_piece.T,
            key_heads,
            value_heads,
        ),
    )
    return (key_parts, value_parts)


def by_rows(queries, keys, values, out_cotangent, visible_counts, span_offset, out_weight):
    devices = lax.axis_size("seq")
    device = lax.axis_index("seq")
    frames = queries.shape[1]
    visible_rows = VIS_DEV
    capacity = MAXV // devices
    counts = visible_counts[0]
    offsets = span_offset[0]
    shard_ends = jnp.cumsum(counts)
    starts = shard_ends - counts
    this_device = device.reshape(1)
    count_here = pick_entry(counts, this_device)[0]
    start_here = pick_entry(starts, this_device)[0]
    span_begin = pick_entry(offsets, this_device)[0] % (count_here + 1)
    masked = frames - count_here
    send_slots = jnp.arange(devices * capacity, dtype=jnp.int32)
    peer_index = send_slots // capacity
    within = send_slots % capacity
    first_slot = (start_here - peer_index + devices - 1) // devices
    global_index = (first_slot + within) * devices + peer_index
    ranked = global_index - start_here
    live_slot = ranked < count_here
    frame_of = jnp.clip(jnp.where(ranked < span_begin, ranked, ranked + masked), 0, frames - 1)

    def outgoing(block):
        return jnp.where(
            live_slot[:, None], jnp.take(block[0], frame_of, axis=0), jnp.zeros((), block.dtype)
        )

    arrived = (
        lax.all_to_all(outgoing(queries), "seq", split_axis=0, concat_axis=0, tiled=True),
        lax.all_to_all(outgoing(keys), "seq", split_axis=0, concat_axis=0, tiled=True),
        lax.all_to_all(outgoing(values), "seq", split_axis=0, concat_axis=0, tiled=True),
        lax.all_to_all(outgoing(out_cotangent), "seq", split_axis=0, concat_axis=0, tiled=True),
    )
    packed_slot = jnp.arange(visible_rows, dtype=jnp.int32)
    packed_index = packed_slot * devices + device
    owner_shard = jnp.sum((shard_ends[None, :] <= packed_index[:, None]).astype(jnp.int32), axis=1)
    owner_first = (pick_entry(starts, owner_shard) - device + devices - 1) // devices
    arrived_row = owner_shard * capacity + packed_slot - owner_first
    query_pack = jnp.take(arrived[0], arrived_row, axis=0)
    key_pack = jnp.take(arrived[1], arrived_row, axis=0)
    value_pack = jnp.take(arrived[2], arrived_row, axis=0)
    cotangent_pack = jnp.take(arrived[3], arrived_row, axis=0)
    output_grad = lax.dot_general(
        cotangent_pack,
        lax.all_gather(out_weight, "seq", axis=0, tiled=True),
        (((1,), (1,)), ((), ())),
        preferred_element_type=jnp.float32,
    ).astype(jnp.bfloat16)
    key_all, value_all = (
        lax.all_gather(key_pack, "seq", axis=0, tiled=True),
        lax.all_gather(value_pack, "seq", axis=0, tiled=True),
    )
    attended, query_grad, log_totals, inner_sums = lax.map(
        query_side,
        (
            split_heads(query_pack),
            split_heads(key_all),
            split_heads(value_all),
            split_heads(output_grad),
        ),
    )
    attended = join_heads(attended)
    query_grad = join_heads(query_grad)
    log_rows = log_totals.T
    inner_rows = inner_sums.T
    partial_term = lax.dot_general(
        attended, cotangent_pack, (((0,), (0,)), ((), ())), preferred_element_type=jnp.float32
    )
    seq_sum = lax.psum_scatter(
        partial_term.astype(jnp.bfloat16), "seq", scatter_dimension=0, tiled=True
    )
    clip_sum = lax.psum(seq_sum, "clip").astype(jnp.float32)
    weight_grad = clip_sum * (lax.axis_size("clip") * visible_rows * devices) ** (-0.5)
    log_every, inner_every = (
        lax.all_gather(log_rows, "seq", axis=0, tiled=True),
        lax.all_gather(inner_rows, "seq", axis=0, tiled=True),
    )
    key_heads = split_heads(key_pack)
    value_heads = split_heads(value_pack)
    key_sum, value_sum = key_side_add(
        lax.all_gather(query_pack, "seq", axis=0, tiled=True),
        lax.all_gather(output_grad, "seq", axis=0, tiled=True),
        log_every,
        inner_every,
        key_heads,
        value_heads,
    )
    key_grad = join_heads((key_sum * HD ** (-0.5)).astype(jnp.bfloat16))
    value_grad = join_heads(value_sum.astype(jnp.bfloat16))
    back_first = (pick_entry(starts, peer_index) - device + devices - 1) // devices
    back_slot = back_first + within
    back_live = back_slot * devices + device < pick_entry(shard_ends, peer_index)
    back_row = jnp.clip(back_slot, 0, visible_rows - 1)

    def returning(block):
        return jnp.where(
            back_live[:, None], jnp.take(block, back_row, axis=0), jnp.zeros((), block.dtype)
        )

    returned = (
        lax.all_to_all(returning(query_grad), "seq", split_axis=0, concat_axis=0, tiled=True),
        lax.all_to_all(returning(key_grad), "seq", split_axis=0, concat_axis=0, tiled=True),
        lax.all_to_all(returning(value_grad), "seq", split_axis=0, concat_axis=0, tiled=True),
    )
    position = jnp.arange(frames, dtype=jnp.int32)
    visible = (position < span_begin) | (position >= span_begin + masked)
    frame_rank = jnp.where(position < span_begin, position, position - masked)
    frame_global = start_here + frame_rank
    frame_peer = frame_global % devices
    frame_slot = frame_global // devices
    frame_first = (start_here - frame_peer + devices - 1) // devices
    frame_row = jnp.clip(
        frame_peer * capacity + frame_slot - frame_first, 0, devices * capacity - 1
    )

    def placed(block):
        return jnp.where(
            visible[:, None], jnp.take(block, frame_row, axis=0), jnp.zeros((), block.dtype)
        )[None]

    return (placed(returned[0]), placed(returned[1]), placed(returned[2]), weight_grad)


ROUTES = (0, 2, 4, 6)


def head_lanes(core):
    lane = lax.broadcasted_iota(jnp.int32, (1, 128), 1)
    return ((lane // HD) == core).astype(jnp.float32).astype(jnp.bfloat16)


def scalar_copies(sources, targets, sems):
    copies = [
        pltpu.make_async_copy(source, target, sems.at[index])
        for index, (source, target) in enumerate(zip(sources, targets))
    ]
    for copy in copies:
        copy.start()
    return copies


def span_of(counts_ref, offsets_ref, owner):
    count = counts_ref[0, owner]
    begin = lax.rem(offsets_ref[0, owner], count + 1)
    return begin, MAXV - (count - begin)


def slot_masks(begin, end_start):
    slot = lax.broadcasted_iota(jnp.int32, (MAXV, 1), 0)
    early = (slot < begin).astype(jnp.float32).astype(jnp.bfloat16)
    late = (slot >= end_start).astype(jnp.float32).astype(jnp.bfloat16)
    return early, late


def pack_kernel(counts_hbm, offsets_hbm, q_ref, k_ref, v_ref, g_ref, *rest):
    sends, cot_ref, sides_ref = rest[:4], rest[4], rest[5]
    narrow, wide, counts_ref, offsets_ref, sems, scalar_sems = rest[6:]
    scalars = scalar_copies((counts_hbm, offsets_hbm), (counts_ref, offsets_ref), scalar_sems)
    frames = q_ref.shape[1]
    last = frames - MAXV
    device = lax.axis_index("seq")
    copies = []
    for index, source in enumerate((q_ref, k_ref, v_ref)):
        for side, start in enumerate((0, last)):
            copies.append(
                pltpu.make_async_copy(
                    source.at[0, pl.ds(start, MAXV)], narrow.at[index, side], sems.at[len(copies)]
                )
            )
    for side, start in enumerate((0, last)):
        copies.append(
            pltpu.make_async_copy(
                g_ref.at[0, pl.ds(start, MAXV)], wide.at[side], sems.at[len(copies)]
            )
        )
    for copy in copies:
        copy.start()
    for copy in scalars:
        copy.wait()
    begin, end_start = span_of(counts_ref, offsets_ref, device)
    early, late = slot_masks(begin, end_start)
    for copy in copies[:6]:
        copy.wait()
    for route, send in zip(ROUTES, sends):
        chip = (device ^ route) // 2
        lanes = pl.ds(pl.multiple_of(chip * 128, 128), 128)
        for index in range(3):
            send[:, index * 128 : (index + 1) * 128] = (
                narrow[index, 0, :, lanes] * early + narrow[index, 1, :, lanes] * late
            )
    for copy in copies[6:]:
        copy.wait()
    cot_ref[...] = wide[0] * early + wide[1] * late
    for side, mask in enumerate((early, late)):
        sides_ref[side] = jnp.broadcast_to(mask, (MAXV, 128))


def forward_kernel(counts_hbm, offsets_hbm, *rest):
    blocks = rest[:8]
    packed, weights_ref, attended_ref, counts_ref, offsets_ref, sems, scalar_sems = rest[8:]
    scalars = scalar_copies((counts_hbm, offsets_hbm), (counts_ref, offsets_ref), scalar_sems)
    device = lax.axis_index("seq")
    core = device % 2
    copies = []
    for index in range(8):
        rows = pl.ds(index * MAXV, MAXV)
        copies.append(pltpu.make_async_copy(blocks[index], packed.at[rows], sems.at[index]))
        copies[-1].start()
    lanes = head_lanes(core)
    for copy in scalars:
        copy.wait()
    dead = []
    for index in range(8):
        begin, end_start = span_of(counts_ref, offsets_ref, device ^ index)
        slot = lax.broadcasted_iota(jnp.int32, (MAXV, 256), 0)
        dead.append((slot >= begin) & (slot < end_start))
    dead = jnp.concatenate(dead, axis=0)
    for copy in copies:
        copy.wait()
    factor = HD ** (-0.5)
    key = packed[:, 128:256] * lanes
    value_t = packed[:, 256:384].T
    for step in range(3):
        rows = slice(step * 256, (step + 1) * 256)
        scores = (
            lax.dot_general(
                key, packed[rows, 0:128], (((1,), (1,)), ((), ())), preferred_element_type=jnp.float32
            )
            * factor
        )
        scores = jnp.where(dead, -1e30, scores)
        scores = jnp.exp(scores - jnp.max(scores, axis=0, keepdims=True))
        weights = scores * (1.0 / jnp.sum(scores, axis=0, keepdims=True))
        weights_ref[:, rows] = weights
        attended_ref[:, rows] = jnp.dot(
            value_t, weights.astype(jnp.bfloat16), preferred_element_type=jnp.float32
        ).astype(jnp.bfloat16)


def own_rows(ref, core, columns):
    both = ref[:, columns].astype(jnp.float32)
    return jnp.where(core == 0, both[:HD], both[HD:]).astype(jnp.bfloat16)


def project(cot, w_ref, core):
    top = (core == 0).astype(jnp.float32).astype(jnp.bfloat16)
    bottom = (core == 1).astype(jnp.float32).astype(jnp.bfloat16)
    w_both = jnp.concatenate([w_ref[...] * top, w_ref[...] * bottom], axis=0)
    return lax.dot_general(
        cot[...], w_both, (((1,), (1,)), ((), ())), preferred_element_type=jnp.float32
    ).astype(jnp.bfloat16)


def early_kernel(attended_ref, w_ref, *rest):
    cots, dout_ref, wg_ref, cot = rest[:6], rest[6], rest[7], rest[8]
    core = lax.axis_index("seq") % 2
    for index in range(6):
        cot[index * MAXV : (index + 1) * MAXV, :] = cots[index][...]
    dout_ref[...] = project(cot, w_ref, core)
    wg_ref[...] = jnp.dot(
        own_rows(attended_ref, core, slice(0, 6 * MAXV)),
        cot[...],
        preferred_element_type=jnp.float32,
    )


def late_kernel(attended_ref, w_ref, begun_ref, *rest):
    cots, dout_ref, kept_ref, sent_ref, cot = rest[:2], rest[2], rest[3], rest[4], rest[5]
    core = lax.axis_index("seq") % 2
    for index in range(2):
        cot[index * MAXV : (index + 1) * MAXV, :] = cots[index][...]
    dout_ref[...] = project(cot, w_ref, core)
    total = begun_ref[...] + jnp.dot(
        own_rows(attended_ref, core, slice(6 * MAXV, 8 * MAXV)),
        cot[...],
        preferred_element_type=jnp.float32,
    )
    half = total.shape[0] // 2
    lower = lax.axis_index("clip") % 2 == 0
    kept_ref[...] = jnp.where(lower, total[:half], total[half:]).astype(jnp.bfloat16)
    sent_ref[...] = jnp.where(lower, total[half:], total[:half]).astype(jnp.bfloat16)


def backward_kernel(packed, weights_ref, attended_ref, begun_ref, ended_ref, *rest):
    outs = rest[:2]
    dout, dq = rest[2:]
    core = lax.axis_index("seq") % 2
    lanes = head_lanes(core)
    dout[: 6 * MAXV, :] = begun_ref[...]
    dout[6 * MAXV :, :] = ended_ref[...]
    key_t = (packed[:, 128:256] * lanes).T
    value = packed[:, 256:384]
    factor = HD ** (-0.5)
    dout_t = dout[...].astype(jnp.float32).T
    key_grad = jnp.zeros((8 * MAXV, 128), jnp.float32)
    value_grad = jnp.zeros((8 * MAXV, 128), jnp.float32)
    for step in range(3):
        rows = slice(step * 256, (step + 1) * 256)
        query_own = packed[rows, 0:128] * lanes
        dout_own = dout[rows, :]
        weights = weights_ref[:, rows]
        inner = jnp.sum(
            dout_t[:, rows] * attended_ref[:, rows].astype(jnp.float32), axis=0, keepdims=True
        )
        dweights = lax.dot_general(
            value, dout_own, (((1,), (1,)), ((), ())), preferred_element_type=jnp.float32
        )
        dscores = (weights * (dweights - inner)).astype(jnp.bfloat16)
        value_grad += jnp.dot(
            weights.astype(jnp.bfloat16), dout_own, preferred_element_type=jnp.float32
        )
        key_grad += jnp.dot(dscores, query_own, preferred_element_type=jnp.float32)
        dq_t = jnp.dot(key_t, dscores, preferred_element_type=jnp.float32) * factor
        dq[rows, :] = dq_t.T.astype(jnp.bfloat16)
    key_grad = (key_grad * factor).astype(jnp.bfloat16)
    value_grad = value_grad.astype(jnp.bfloat16)
    for index in range(8):
        rows = slice(index * MAXV, (index + 1) * MAXV)
        outs[index % 2][index // 2, :, 0:128] = dq[rows, :]
        outs[index % 2][index // 2, :, 128:256] = key_grad[rows]
        outs[index % 2][index // 2, :, 256:384] = value_grad[rows]


def combine_kernel(kept, crossed, *outs):
    for index in range(4):
        outs[index][...] = kept[index] + crossed[index]


def unpack_kernel(scale, sides_ref, *rest):
    blocks, shares, outs, wg_ref = rest[:4], rest[4:6], rest[6:9], rest[9]
    edges, blank, sems = rest[10:]
    device = lax.axis_index("seq")
    frames = outs[0].shape[1]
    last = frames - MAXV
    blank[...] = jnp.zeros_like(blank)
    copies = []
    for index in range(3):
        copies.append(
            pltpu.make_async_copy(
                blank, outs[index].at[0, pl.ds(MAXV, last - MAXV)], sems.at[index]
            )
        )
        copies[-1].start()
    for route, block in zip(ROUTES, blocks):
        chip = (device ^ route) // 2
        lanes = pl.ds(pl.multiple_of(chip * 128, 128), 128)
        for index in range(3):
            piece = block[:, index * 128 : (index + 1) * 128]
            for side in range(2):
                edges[index, side, :, lanes] = piece * sides_ref[side]
    for index in range(3):
        for side, start in enumerate((0, last)):
            copies.append(
                pltpu.make_async_copy(
                    edges.at[index, side],
                    outs[index].at[0, pl.ds(start, MAXV)],
                    sems.at[len(copies)],
                )
            )
            copies[-1].start()
    lower = lax.axis_index("clip") % 2 == 0
    mine, other = [share[...].astype(jnp.float32) * scale for share in shares]
    half = mine.shape[0]
    wg_ref[:half, :] = jnp.where(lower, mine, other)
    wg_ref[half:, :] = jnp.where(lower, other, mine)
    for copy in copies:
        copy.wait()


PARAMS = pltpu.CompilerParams(vmem_limit_bytes=24 << 20)
ANYWHERE = pl.BlockSpec(memory_space=pl.ANY)
SCALARS = pl.BlockSpec(memory_space=pltpu.SMEM)
LOCAL = pl.BlockSpec(memory_space=pltpu.VMEM)


def in_hbm(block):
    return pltpu.with_memory_space_constraint(block, pltpu.HBM)


def by_heads(queries, keys, values, out_cotangent, visible_counts, span_offset, out_weight):
    bf16 = jnp.bfloat16
    pairs = lax.axis_size("seq")
    clips = lax.axis_size("clip")

    def shift(block, step):
        return lax.ppermute(block, "seq", [(i, i ^ step) for i in range(pairs)])

    narrow = jax.ShapeDtypeStruct((MAXV, 384), bf16)
    wide = jax.ShapeDtypeStruct((MAXV, out_cotangent.shape[2]), bf16)

    def seen(kernel, outs, specs, operands, scratch=(), out_specs=None):
        return pl.pallas_call(
            kernel,
            out_shape=outs,
            in_specs=specs,
            out_specs=out_specs or [LOCAL] * len(outs),
            scratch_shapes=scratch,
            compiler_params=PARAMS,
        )(*operands)

    width = out_cotangent.shape[2]
    rows = 8 * MAXV
    counts, offsets = in_hbm(visible_counts), in_hbm(span_offset)
    table = pltpu.SMEM(visible_counts.shape, jnp.int32)
    tables = [table, table]
    pair_sems = pltpu.SemaphoreType.DMA((2,))
    *sends, cot, sides = seen(
        pack_kernel,
        [narrow] * 4 + [wide, pltpu.VMEM((2, MAXV, 128), bf16)],
        [ANYWHERE] * 6,
        (counts, offsets, *map(in_hbm, (queries, keys, values, out_cotangent))),
        [
            pltpu.VMEM((3, 2, MAXV, queries.shape[2]), bf16),
            pltpu.VMEM((2, MAXV, width), bf16),
            *tables,
            pltpu.SemaphoreType.DMA((8,)),
            pair_sems,
        ],
    )
    even = [sends[0]] + [shift(sends[i], ROUTES[i]) for i in (1, 2, 3)]
    even_cot = [cot] + [shift(cot, ROUTES[i]) for i in (1, 2, 3)]
    odd = [shift(block, 1) for block in even]
    odd_cot = [shift(block, 1) for block in even_cot]
    blocks = [block for pair in zip(even, odd) for block in pair]
    cots = [block for pair in zip(even_cot, odd_cot) for block in pair]
    packed, weights, attended = seen(
        forward_kernel,
        [
            pltpu.VMEM((rows, 384), bf16),
            pltpu.VMEM((rows, rows), jnp.float32),
            pltpu.VMEM((128, rows), bf16),
        ],
        [ANYWHERE] * 2 + [LOCAL] * 8,
        (counts, offsets, *blocks),
        [*tables, pltpu.SemaphoreType.DMA((8,)), pair_sems],
    )
    begun, begun_wg = seen(
        early_kernel,
        [pltpu.VMEM((6 * MAXV, 128), bf16), pltpu.VMEM(out_weight.shape, jnp.float32)],
        [LOCAL] * 8,
        (attended, out_weight, *cots[:6]),
        [pltpu.VMEM((6 * MAXV, width), bf16)],
    )
    share = jax.ShapeDtypeStruct((out_weight.shape[0] // 2, width), bf16)
    ended, mine, sent = seen(
        late_kernel,
        [pltpu.VMEM((2 * MAXV, 128), bf16), share, share],
        [LOCAL] * 5,
        (attended, out_weight, begun_wg, *cots[6:]),
        [pltpu.VMEM((2 * MAXV, width), bf16)],
    )

    def across(block, step):
        return lax.ppermute(block, "clip", [(i, i ^ step) for i in range(clips)])

    other = across(sent, 1)
    step = 1
    while step < clips:
        mine = (mine.astype(jnp.float32) + other.astype(jnp.float32)).astype(bf16)
        step *= 2
        if step < clips:
            other = across(mine, step)
    shares = [mine, across(mine, 1)]
    kept, leaving = seen(
        backward_kernel,
        [jax.ShapeDtypeStruct((4, MAXV, 384), bf16)] * 2,
        [LOCAL] * 5,
        (packed, weights, attended, begun, ended),
        [pltpu.VMEM((rows, 128), bf16)] * 2,
    )
    crossed = shift(leaving, 1)
    joined = seen(combine_kernel, [narrow] * 4, [LOCAL] * 2, (kept, crossed))
    home = [joined[0]] + [shift(joined[i], ROUTES[i]) for i in (1, 2, 3)]
    frames = queries.shape[1]
    scale = (clips * VIS_DEV * pairs) ** (-0.5)
    return tuple(
        seen(
            functools.partial(unpack_kernel, scale),
            [jax.ShapeDtypeStruct(queries.shape, bf16)] * 3
            + [jax.ShapeDtypeStruct(out_weight.shape, jnp.float32)],
            [LOCAL] * 7,
            (sides, *home, *shares),
            [
                pltpu.VMEM((3, 2, MAXV, queries.shape[2]), bf16),
                pltpu.VMEM((frames - 2 * MAXV, queries.shape[2]), bf16),
                pltpu.SemaphoreType.DMA((9,)),
            ],
            [ANYWHERE] * 3 + [LOCAL],
        )
    )


def local(*arrays):
    if lax.axis_size("seq") == HEADS and lax.axis_size("clip") in (2, 4, 8, 16):
        return by_heads(*arrays)
    return by_rows(*arrays)


def solution(mesh):
    placed = (
        P("clip", "seq", None),
        P("clip", "seq", None),
        P("clip", "seq", None),
        P("clip", "seq", None),
        P("clip", None),
        P("clip", None),
        P("seq", None),
    )
    return jax.shard_map(
        local,
        mesh=mesh,
        in_specs=placed,
        out_specs=(
            P("clip", "seq", None),
            P("clip", "seq", None),
            P("clip", "seq", None),
            P("seq", None),
        ),
        check_vma=False,
    )
```

```python
import functools

import jax
import jax.numpy as jnp
from jax import lax
from jax.experimental import pallas as pl
from jax.experimental.pallas import tpu as pltpu
from jax.sharding import PartitionSpec as P


HEADS = 8
HD = 64
VIS_DEV = 48
MAXV = 96


def pick_entry(table, position):
    order = jnp.arange(table.shape[0], dtype=jnp.int32)
    chosen = jnp.where(order[None, :] == position[:, None], table[None, :], 0)
    return jnp.sum(chosen, axis=1)


def split_heads(block):
    return block.reshape(block.shape[0], HEADS, HD).transpose(1, 0, 2)


def join_heads(block):
    return block.transpose(1, 0, 2).reshape(block.shape[1], HEADS * HD)


def query_side(parts):
    query_head, key_head, value_head, dout_head = parts
    factor = HD ** (-0.5)
    scores = (
        lax.dot_general(
            query_head, key_head, (((1,), (1,)), ((), ())), preferred_element_type=jnp.float32
        )
        * factor
    )
    peak_score = jnp.max(scores, axis=1, keepdims=True)
    log_total = peak_score + jnp.log(jnp.sum(jnp.exp(scores - peak_score), axis=1, keepdims=True))
    weights = jnp.exp(scores - log_total)
    weights_low = weights.astype(jnp.bfloat16)
    attended = jnp.dot(weights_low, value_head, preferred_element_type=jnp.float32).astype(
        jnp.bfloat16
    )
    inner_sum = jnp.sum(
        dout_head.astype(jnp.float32) * attended.astype(jnp.float32), axis=1, keepdims=True
    )
    dweights = lax.dot_general(
        dout_head, value_head, (((1,), (1,)), ((), ())), preferred_element_type=jnp.float32
    )
    dscores = (weights * (dweights - inner_sum)).astype(jnp.bfloat16)
    grad_query = (jnp.dot(dscores, key_head, preferred_element_type=jnp.float32) * factor).astype(
        jnp.bfloat16
    )
    return (attended, grad_query, log_total[:, 0], inner_sum[:, 0])


def key_side_add(query_piece, dout_piece, log_piece, inner_piece, key_heads, value_heads):
    factor = HD ** (-0.5)

    def one_head(parts):
        query_head, dout_head, log_head, inner_head, key_head, value_head = parts
        scores = (
            lax.dot_general(
                query_head, key_head, (((1,), (1,)), ((), ())), preferred_element_type=jnp.float32
            )
            * factor
        )
        weights = jnp.exp(scores - log_head[:, None])
        weights_low = weights.astype(jnp.bfloat16)
        value_part = lax.dot_general(
            weights_low, dout_head, (((0,), (0,)), ((), ())), preferred_element_type=jnp.float32
        )
        dweights = lax.dot_general(
            dout_head, value_head, (((1,), (1,)), ((), ())), preferred_element_type=jnp.float32
        )
        dscores = (weights * (dweights - inner_head[:, None])).astype(jnp.bfloat16)
        key_part = lax.dot_general(
            dscores, query_head, (((0,), (0,)), ((), ())), preferred_element_type=jnp.float32
        )
        return (key_part, value_part)

    key_parts, value_parts = lax.map(
        one_head,
        (
            split_heads(query_piece),
            split_heads(dout_piece),
            log_piece.T,
            inner_piece.T,
            key_heads,
            value_heads,
        ),
    )
    return (key_parts, value_parts)


def by_rows(queries, keys, values, out_cotangent, visible_counts, span_offset, out_weight):
    devices = lax.axis_size("seq")
    device = lax.axis_index("seq")
    frames = queries.shape[1]
    visible_rows = VIS_DEV
    capacity = MAXV // devices
    counts = visible_counts[0]
    offsets = span_offset[0]
    shard_ends = jnp.cumsum(counts)
    starts = shard_ends - counts
    this_device = device.reshape(1)
    count_here = pick_entry(counts, this_device)[0]
    start_here = pick_entry(starts, this_device)[0]
    span_begin = pick_entry(offsets, this_device)[0] % (count_here + 1)
    masked = frames - count_here
    send_slots = jnp.arange(devices * capacity, dtype=jnp.int32)
    peer_index = send_slots // capacity
    within = send_slots % capacity
    first_slot = (start_here - peer_index + devices - 1) // devices
    global_index = (first_slot + within) * devices + peer_index
    ranked = global_index - start_here
    live_slot = ranked < count_here
    frame_of = jnp.clip(jnp.where(ranked < span_begin, ranked, ranked + masked), 0, frames - 1)

    def outgoing(block):
        return jnp.where(
            live_slot[:, None], jnp.take(block[0], frame_of, axis=0), jnp.zeros((), block.dtype)
        )

    arrived = (
        lax.all_to_all(outgoing(queries), "seq", split_axis=0, concat_axis=0, tiled=True),
        lax.all_to_all(outgoing(keys), "seq", split_axis=0, concat_axis=0, tiled=True),
        lax.all_to_all(outgoing(values), "seq", split_axis=0, concat_axis=0, tiled=True),
        lax.all_to_all(outgoing(out_cotangent), "seq", split_axis=0, concat_axis=0, tiled=True),
    )
    packed_slot = jnp.arange(visible_rows, dtype=jnp.int32)
    packed_index = packed_slot * devices + device
    owner_shard = jnp.sum((shard_ends[None, :] <= packed_index[:, None]).astype(jnp.int32), axis=1)
    owner_first = (pick_entry(starts, owner_shard) - device + devices - 1) // devices
    arrived_row = owner_shard * capacity + packed_slot - owner_first
    query_pack = jnp.take(arrived[0], arrived_row, axis=0)
    key_pack = jnp.take(arrived[1], arrived_row, axis=0)
    value_pack = jnp.take(arrived[2], arrived_row, axis=0)
    cotangent_pack = jnp.take(arrived[3], arrived_row, axis=0)
    output_grad = lax.dot_general(
        cotangent_pack,
        lax.all_gather(out_weight, "seq", axis=0, tiled=True),
        (((1,), (1,)), ((), ())),
        preferred_element_type=jnp.float32,
    ).astype(jnp.bfloat16)
    key_all, value_all = (
        lax.all_gather(key_pack, "seq", axis=0, tiled=True),
        lax.all_gather(value_pack, "seq", axis=0, tiled=True),
    )
    attended, query_grad, log_totals, inner_sums = lax.map(
        query_side,
        (
            split_heads(query_pack),
            split_heads(key_all),
            split_heads(value_all),
            split_heads(output_grad),
        ),
    )
    attended = join_heads(attended)
    query_grad = join_heads(query_grad)
    log_rows = log_totals.T
    inner_rows = inner_sums.T
    partial_term = lax.dot_general(
        attended, cotangent_pack, (((0,), (0,)), ((), ())), preferred_element_type=jnp.float32
    )
    seq_sum = lax.psum_scatter(
        partial_term.astype(jnp.bfloat16), "seq", scatter_dimension=0, tiled=True
    )
    clip_sum = lax.psum(seq_sum, "clip").astype(jnp.float32)
    weight_grad = clip_sum * (lax.axis_size("clip") * visible_rows * devices) ** (-0.5)
    log_every, inner_every = (
        lax.all_gather(log_rows, "seq", axis=0, tiled=True),
        lax.all_gather(inner_rows, "seq", axis=0, tiled=True),
    )
    key_heads = split_heads(key_pack)
    value_heads = split_heads(value_pack)
    key_sum, value_sum = key_side_add(
        lax.all_gather(query_pack, "seq", axis=0, tiled=True),
        lax.all_gather(output_grad, "seq", axis=0, tiled=True),
        log_every,
        inner_every,
        key_heads,
        value_heads,
    )
    key_grad = join_heads((key_sum * HD ** (-0.5)).astype(jnp.bfloat16))
    value_grad = join_heads(value_sum.astype(jnp.bfloat16))
    back_first = (pick_entry(starts, peer_index) - device + devices - 1) // devices
    back_slot = back_first + within
    back_live = back_slot * devices + device < pick_entry(shard_ends, peer_index)
    back_row = jnp.clip(back_slot, 0, visible_rows - 1)

    def returning(block):
        return jnp.where(
            back_live[:, None], jnp.take(block, back_row, axis=0), jnp.zeros((), block.dtype)
        )

    returned = (
        lax.all_to_all(returning(query_grad), "seq", split_axis=0, concat_axis=0, tiled=True),
        lax.all_to_all(returning(key_grad), "seq", split_axis=0, concat_axis=0, tiled=True),
        lax.all_to_all(returning(value_grad), "seq", split_axis=0, concat_axis=0, tiled=True),
    )
    position = jnp.arange(frames, dtype=jnp.int32)
    visible = (position < span_begin) | (position >= span_begin + masked)
    frame_rank = jnp.where(position < span_begin, position, position - masked)
    frame_global = start_here + frame_rank
    frame_peer = frame_global % devices
    frame_slot = frame_global // devices
    frame_first = (start_here - frame_peer + devices - 1) // devices
    frame_row = jnp.clip(
        frame_peer * capacity + frame_slot - frame_first, 0, devices * capacity - 1
    )

    def placed(block):
        return jnp.where(
            visible[:, None], jnp.take(block, frame_row, axis=0), jnp.zeros((), block.dtype)
        )[None]

    return (placed(returned[0]), placed(returned[1]), placed(returned[2]), weight_grad)


ROUTES = (0, 2, 4, 6)


def head_lanes(core):
    lane = lax.broadcasted_iota(jnp.int32, (1, 128), 1)
    return ((lane // HD) == core).astype(jnp.float32).astype(jnp.bfloat16)


def scalar_copies(sources, targets, sems):
    copies = [
        pltpu.make_async_copy(source, target, sems.at[index])
        for index, (source, target) in enumerate(zip(sources, targets))
    ]
    for copy in copies:
        copy.start()
    return copies


def span_of(counts_ref, offsets_ref, owner):
    count = counts_ref[0, owner]
    begin = lax.rem(offsets_ref[0, owner], count + 1)
    return begin, MAXV - (count - begin)


def slot_masks(begin, end_start):
    slot = lax.broadcasted_iota(jnp.int32, (MAXV, 1), 0)
    early = (slot < begin).astype(jnp.float32).astype(jnp.bfloat16)
    late = (slot >= end_start).astype(jnp.float32).astype(jnp.bfloat16)
    return early, late


def pack_kernel(counts_hbm, offsets_hbm, q_ref, k_ref, v_ref, g_ref, *rest):
    sends, cot_ref, sides_ref = rest[:4], rest[4], rest[5]
    narrow, wide, counts_ref, offsets_ref, sems, scalar_sems = rest[6:]
    scalars = scalar_copies((counts_hbm, offsets_hbm), (counts_ref, offsets_ref), scalar_sems)
    frames = q_ref.shape[1]
    last = frames - MAXV
    device = lax.axis_index("seq")
    copies = []
    for index, source in enumerate((q_ref, k_ref, v_ref)):
        for side, start in enumerate((0, last)):
            copies.append(
                pltpu.make_async_copy(
                    source.at[0, pl.ds(start, MAXV)], narrow.at[index, side], sems.at[len(copies)]
                )
            )
    for side, start in enumerate((0, last)):
        copies.append(
            pltpu.make_async_copy(
                g_ref.at[0, pl.ds(start, MAXV)], wide.at[side], sems.at[len(copies)]
            )
        )
    for copy in copies:
        copy.start()
    for copy in scalars:
        copy.wait()
    begin, end_start = span_of(counts_ref, offsets_ref, device)
    early, late = slot_masks(begin, end_start)
    for copy in copies[:6]:
        copy.wait()
    for route, send in zip(ROUTES, sends):
        chip = (device ^ route) // 2
        lanes = pl.ds(pl.multiple_of(chip * 128, 128), 128)
        for index in range(3):
            send[:, index * 128 : (index + 1) * 128] = (
                narrow[index, 0, :, lanes] * early + narrow[index, 1, :, lanes] * late
            )
    for copy in copies[6:]:
        copy.wait()
    cot_ref[...] = wide[0] * early + wide[1] * late
    for side, mask in enumerate((early, late)):
        sides_ref[side] = jnp.broadcast_to(mask, (MAXV, 128))


def tables_kernel(counts_hbm, offsets_hbm, bias_ref, *rest):
    outs, (blank, counts_ref, offsets_ref, sems, scalar_sems) = rest[:3], rest[3:]
    scalars = scalar_copies((counts_hbm, offsets_hbm), (counts_ref, offsets_ref), scalar_sems)
    blank[...] = jnp.zeros_like(blank)
    copies = [
        pltpu.make_async_copy(blank, out.at[0, pl.ds(MAXV, blank.shape[0])], sems.at[index])
        for index, out in enumerate(outs)
    ]
    for copy in copies:
        copy.start()
    device = lax.axis_index("seq")
    for copy in scalars:
        copy.wait()
    slot = lax.broadcasted_iota(jnp.int32, (MAXV, 128), 0)
    for index in range(8):
        owner = device ^ (ROUTES[index // 2] + index % 2)
        begin, end_start = span_of(counts_ref, offsets_ref, owner)
        dead = (slot >= begin) & (slot < end_start)
        bias_ref[index * MAXV : (index + 1) * MAXV, :] = jnp.where(dead, -1e30, 0.0)
    for copy in copies:
        copy.wait()


def forward_kernel(bias_ref, *rest):
    blocks = rest[:8]
    packed, weights_ref, attended_ref = rest[8:]
    lanes = head_lanes(lax.axis_index("seq") % 2)
    for index in range(8):
        packed[index * MAXV : (index + 1) * MAXV, :] = blocks[index][...]
    bias = bias_ref[...]
    bias = jnp.concatenate([bias, bias], axis=1)
    factor = HD ** (-0.5)
    key = packed[:, 128:256] * lanes
    value_t = packed[:, 256:384].T
    for step in range(3):
        rows = slice(step * 256, (step + 1) * 256)
        scores = (
            lax.dot_general(
                key, packed[rows, 0:128], (((1,), (1,)), ((), ())), preferred_element_type=jnp.float32
            )
            * factor
        )
        scores = scores + bias
        scores = jnp.exp(scores - jnp.max(scores, axis=0, keepdims=True))
        weights = scores * (1.0 / jnp.sum(scores, axis=0, keepdims=True))
        weights_ref[:, rows] = weights
        attended_ref[:, rows] = jnp.dot(
            value_t, weights.astype(jnp.bfloat16), preferred_element_type=jnp.float32
        ).astype(jnp.bfloat16)


def own_rows(ref, core, columns):
    both = ref[:, columns].astype(jnp.float32)
    return jnp.where(core == 0, both[:HD], both[HD:]).astype(jnp.bfloat16)


def project(cot, w_ref, core):
    top = (core == 0).astype(jnp.float32).astype(jnp.bfloat16)
    bottom = (core == 1).astype(jnp.float32).astype(jnp.bfloat16)
    w_both = jnp.concatenate([w_ref[...] * top, w_ref[...] * bottom], axis=0)
    return lax.dot_general(
        cot[...], w_both, (((1,), (1,)), ((), ())), preferred_element_type=jnp.float32
    ).astype(jnp.bfloat16)


def early_kernel(attended_ref, w_ref, *rest):
    cots, dout_ref, wg_ref, cot = rest[:6], rest[6], rest[7], rest[8]
    core = lax.axis_index("seq") % 2
    for index in range(6):
        cot[index * MAXV : (index + 1) * MAXV, :] = cots[index][...]
    dout_ref[...] = project(cot, w_ref, core)
    wg_ref[...] = jnp.dot(
        own_rows(attended_ref, core, slice(0, 6 * MAXV)),
        cot[...],
        preferred_element_type=jnp.float32,
    )


def late_kernel(attended_ref, w_ref, begun_ref, *rest):
    cots, dout_ref, kept_ref, sent_ref, cot = rest[:2], rest[2], rest[3], rest[4], rest[5]
    core = lax.axis_index("seq") % 2
    for index in range(2):
        cot[index * MAXV : (index + 1) * MAXV, :] = cots[index][...]
    dout_ref[...] = project(cot, w_ref, core)
    total = begun_ref[...] + jnp.dot(
        own_rows(attended_ref, core, slice(6 * MAXV, 8 * MAXV)),
        cot[...],
        preferred_element_type=jnp.float32,
    )
    half = total.shape[0] // 2
    lower = lax.axis_index("clip") % 2 == 0
    kept_ref[...] = jnp.where(lower, total[:half], total[half:]).astype(jnp.bfloat16)
    sent_ref[...] = jnp.where(lower, total[half:], total[:half]).astype(jnp.bfloat16)


def backward_kernel(packed, weights_ref, attended_ref, begun_ref, ended_ref, *rest):
    outs = rest[:2]
    dout, dq = rest[2:]
    core = lax.axis_index("seq") % 2
    lanes = head_lanes(core)
    dout[: 6 * MAXV, :] = begun_ref[...]
    dout[6 * MAXV :, :] = ended_ref[...]
    key_t = (packed[:, 128:256] * lanes).T
    value = packed[:, 256:384]
    factor = HD ** (-0.5)
    dout_t = dout[...].astype(jnp.float32).T
    key_grad = jnp.zeros((8 * MAXV, 128), jnp.float32)
    value_grad = jnp.zeros((8 * MAXV, 128), jnp.float32)
    for step in range(3):
        rows = slice(step * 256, (step + 1) * 256)
        query_own = packed[rows, 0:128] * lanes
        dout_own = dout[rows, :]
        weights = weights_ref[:, rows]
        inner = jnp.sum(
            dout_t[:, rows] * attended_ref[:, rows].astype(jnp.float32), axis=0, keepdims=True
        )
        dweights = lax.dot_general(
            value, dout_own, (((1,), (1,)), ((), ())), preferred_element_type=jnp.float32
        )
        dscores = (weights * (dweights - inner)).astype(jnp.bfloat16)
        value_grad += jnp.dot(
            weights.astype(jnp.bfloat16), dout_own, preferred_element_type=jnp.float32
        )
        key_grad += jnp.dot(dscores, query_own, preferred_element_type=jnp.float32)
        dq_t = jnp.dot(key_t, dscores, preferred_element_type=jnp.float32) * factor
        dq[rows, :] = dq_t.T.astype(jnp.bfloat16)
    key_grad = (key_grad * factor).astype(jnp.bfloat16)
    value_grad = value_grad.astype(jnp.bfloat16)
    for index in range(8):
        rows = slice(index * MAXV, (index + 1) * MAXV)
        outs[index % 2][index // 2, :, 0:128] = dq[rows, :]
        outs[index % 2][index // 2, :, 128:256] = key_grad[rows]
        outs[index % 2][index // 2, :, 256:384] = value_grad[rows]


def combine_kernel(kept, crossed, *outs):
    for index in range(4):
        outs[index][...] = kept[index] + crossed[index]


def unpack_kernel(scale, sides_ref, *rest):
    blocks, shares, outs, wg_hbm = rest[:4], rest[4:6], rest[9:12], rest[12]
    edges, wg_ref, sems = rest[13:]
    device = lax.axis_index("seq")
    last = outs[0].shape[1] - MAXV
    copies = []
    for index in range(3):
        for route, block in zip(ROUTES, blocks):
            chip = (device ^ route) // 2
            lanes = pl.ds(pl.multiple_of(chip * 128, 128), 128)
            piece = block[:, index * 128 : (index + 1) * 128]
            for side in range(2):
                edges[index, side, :, lanes] = piece * sides_ref[side]
        for side, start in enumerate((0, last)):
            copies.append(
                pltpu.make_async_copy(
                    edges.at[index, side],
                    outs[index].at[0, pl.ds(start, MAXV)],
                    sems.at[len(copies)],
                )
            )
            copies[-1].start()
    lower = lax.axis_index("clip") % 2 == 0
    mine, other = [share[...].astype(jnp.float32) * scale for share in shares]
    half = mine.shape[0]
    wg_ref[:half, :] = jnp.where(lower, mine, other)
    wg_ref[half:, :] = jnp.where(lower, other, mine)
    copies.append(pltpu.make_async_copy(wg_ref, wg_hbm, sems.at[len(copies)]))
    copies[-1].start()
    for copy in copies:
        copy.wait()


PARAMS = pltpu.CompilerParams(vmem_limit_bytes=24 << 20)
ANYWHERE = pl.BlockSpec(memory_space=pl.ANY)
SCALARS = pl.BlockSpec(memory_space=pltpu.SMEM)
LOCAL = pl.BlockSpec(memory_space=pltpu.VMEM)


def in_hbm(block):
    return pltpu.with_memory_space_constraint(block, pltpu.HBM)


def by_heads(queries, keys, values, out_cotangent, visible_counts, span_offset, out_weight):
    bf16 = jnp.bfloat16
    pairs = lax.axis_size("seq")
    clips = lax.axis_size("clip")

    def shift(block, step):
        return lax.ppermute(block, "seq", [(i, i ^ step) for i in range(pairs)])

    narrow = jax.ShapeDtypeStruct((MAXV, 384), bf16)
    wide = jax.ShapeDtypeStruct((MAXV, out_cotangent.shape[2]), bf16)

    def seen(kernel, outs, specs, operands, scratch=(), out_specs=None):
        return pl.pallas_call(
            kernel,
            out_shape=outs,
            in_specs=specs,
            out_specs=out_specs or [LOCAL] * len(outs),
            scratch_shapes=scratch,
            compiler_params=PARAMS,
        )(*operands)

    width = out_cotangent.shape[2]
    rows = 8 * MAXV
    counts, offsets = in_hbm(visible_counts), in_hbm(span_offset)
    table = pltpu.SMEM(visible_counts.shape, jnp.int32)
    tables = [table, table]
    pair_sems = pltpu.SemaphoreType.DMA((2,))
    *sends, cot, sides = seen(
        pack_kernel,
        [narrow] * 4 + [wide, pltpu.VMEM((2, MAXV, 128), bf16)],
        [ANYWHERE] * 6,
        (counts, offsets, *map(in_hbm, (queries, keys, values, out_cotangent))),
        [
            pltpu.VMEM((3, 2, MAXV, queries.shape[2]), bf16),
            pltpu.VMEM((2, MAXV, width), bf16),
            *tables,
            pltpu.SemaphoreType.DMA((8,)),
            pair_sems,
        ],
    )
    even = [sends[0]] + [shift(sends[i], ROUTES[i]) for i in (1, 2, 3)]
    even_cot = [cot] + [shift(cot, ROUTES[i]) for i in (1, 2, 3)]
    odd = [shift(block, 1) for block in even]
    odd_cot = [shift(block, 1) for block in even_cot]
    blocks = [block for pair in zip(even, odd) for block in pair]
    cots = [block for pair in zip(even_cot, odd_cot) for block in pair]
    full = jax.ShapeDtypeStruct(queries.shape, bf16)
    bias, *blanks = seen(
        tables_kernel,
        [pltpu.VMEM((rows, 128), jnp.float32)] + [full] * 3,
        [ANYWHERE] * 2,
        (counts, offsets),
        [
            pltpu.VMEM((queries.shape[1] - 2 * MAXV, queries.shape[2]), bf16),
            *tables,
            pltpu.SemaphoreType.DMA((3,)),
            pair_sems,
        ],
        [LOCAL] + [ANYWHERE] * 3,
    )
    packed, weights, attended = seen(
        forward_kernel,
        [
            pltpu.VMEM((rows, 384), bf16),
            pltpu.VMEM((rows, rows), jnp.float32),
            pltpu.VMEM((128, rows), bf16),
        ],
        [LOCAL] * 9,
        (bias, *blocks),
    )
    begun, begun_wg = seen(
        early_kernel,
        [pltpu.VMEM((6 * MAXV, 128), bf16), pltpu.VMEM(out_weight.shape, jnp.float32)],
        [LOCAL] * 8,
        (attended, out_weight, *cots[:6]),
        [pltpu.VMEM((6 * MAXV, width), bf16)],
    )
    share = jax.ShapeDtypeStruct((out_weight.shape[0] // 2, width), bf16)
    ended, mine, sent = seen(
        late_kernel,
        [pltpu.VMEM((2 * MAXV, 128), bf16), share, share],
        [LOCAL] * 5,
        (attended, out_weight, begun_wg, *cots[6:]),
        [pltpu.VMEM((2 * MAXV, width), bf16)],
    )

    def across(block, step):
        return lax.ppermute(block, "clip", [(i, i ^ step) for i in range(clips)])

    other = across(sent, 1)
    step = 1
    while step < clips:
        mine = (mine.astype(jnp.float32) + other.astype(jnp.float32)).astype(bf16)
        step *= 2
        if step < clips:
            other = across(mine, step)
    shares = [mine, across(mine, 1)]
    kept, leaving = seen(
        backward_kernel,
        [jax.ShapeDtypeStruct((4, MAXV, 384), bf16)] * 2,
        [LOCAL] * 5,
        (packed, weights, attended, begun, ended),
        [pltpu.VMEM((rows, 128), bf16)] * 2,
    )
    crossed = shift(leaving, 1)
    joined = seen(combine_kernel, [narrow] * 4, [LOCAL] * 2, (kept, crossed))
    home = [joined[0]] + [shift(joined[i], ROUTES[i]) for i in (1, 2, 3)]
    scale = (clips * VIS_DEV * pairs) ** (-0.5)
    return tuple(
        pl.pallas_call(
            functools.partial(unpack_kernel, scale),
            out_shape=[full] * 3 + [jax.ShapeDtypeStruct(out_weight.shape, jnp.float32)],
            in_specs=[LOCAL] * 7 + [ANYWHERE] * 3,
            out_specs=[ANYWHERE] * 4,
            scratch_shapes=[
                pltpu.VMEM((3, 2, MAXV, queries.shape[2]), bf16),
                pltpu.VMEM(out_weight.shape, jnp.float32),
                pltpu.SemaphoreType.DMA((7,)),
            ],
            input_output_aliases={7: 0, 8: 1, 9: 2},
            compiler_params=PARAMS,
            name="unpack",
        )(sides, *home, *shares, *blanks)
    )


def local(*arrays):
    if lax.axis_size("seq") == HEADS and lax.axis_size("clip") in (2, 4, 8, 16):
        return by_heads(*arrays)
    return by_rows(*arrays)


def solution(mesh):
    placed = (
        P("clip", "seq", None),
        P("clip", "seq", None),
        P("clip", "seq", None),
        P("clip", "seq", None),
        P("clip", None),
        P("clip", None),
        P("seq", None),
    )
    return jax.shard_map(
        local,
        mesh=mesh,
        in_specs=placed,
        out_specs=(
            P("clip", "seq", None),
            P("clip", "seq", None),
            P("clip", "seq", None),
            P("seq", None),
        ),
        check_vma=False,
    )
```

```python
import functools

import jax
import jax.numpy as jnp
from jax import lax
from jax.experimental import pallas as pl
from jax.experimental.pallas import tpu as pltpu
from jax.sharding import PartitionSpec as P


HEADS = 8
HD = 64
VIS_DEV = 48
MAXV = 96


def pick_entry(table, position):
    order = jnp.arange(table.shape[0], dtype=jnp.int32)
    chosen = jnp.where(order[None, :] == position[:, None], table[None, :], 0)
    return jnp.sum(chosen, axis=1)


def split_heads(block):
    return block.reshape(block.shape[0], HEADS, HD).transpose(1, 0, 2)


def join_heads(block):
    return block.transpose(1, 0, 2).reshape(block.shape[1], HEADS * HD)


def query_side(parts):
    query_head, key_head, value_head, dout_head = parts
    factor = HD ** (-0.5)
    scores = (
        lax.dot_general(
            query_head, key_head, (((1,), (1,)), ((), ())), preferred_element_type=jnp.float32
        )
        * factor
    )
    peak_score = jnp.max(scores, axis=1, keepdims=True)
    log_total = peak_score + jnp.log(jnp.sum(jnp.exp(scores - peak_score), axis=1, keepdims=True))
    weights = jnp.exp(scores - log_total)
    weights_low = weights.astype(jnp.bfloat16)
    attended = jnp.dot(weights_low, value_head, preferred_element_type=jnp.float32).astype(
        jnp.bfloat16
    )
    inner_sum = jnp.sum(
        dout_head.astype(jnp.float32) * attended.astype(jnp.float32), axis=1, keepdims=True
    )
    dweights = lax.dot_general(
        dout_head, value_head, (((1,), (1,)), ((), ())), preferred_element_type=jnp.float32
    )
    dscores = (weights * (dweights - inner_sum)).astype(jnp.bfloat16)
    grad_query = (jnp.dot(dscores, key_head, preferred_element_type=jnp.float32) * factor).astype(
        jnp.bfloat16
    )
    return (attended, grad_query, log_total[:, 0], inner_sum[:, 0])


def key_side_add(query_piece, dout_piece, log_piece, inner_piece, key_heads, value_heads):
    factor = HD ** (-0.5)

    def one_head(parts):
        query_head, dout_head, log_head, inner_head, key_head, value_head = parts
        scores = (
            lax.dot_general(
                query_head, key_head, (((1,), (1,)), ((), ())), preferred_element_type=jnp.float32
            )
            * factor
        )
        weights = jnp.exp(scores - log_head[:, None])
        weights_low = weights.astype(jnp.bfloat16)
        value_part = lax.dot_general(
            weights_low, dout_head, (((0,), (0,)), ((), ())), preferred_element_type=jnp.float32
        )
        dweights = lax.dot_general(
            dout_head, value_head, (((1,), (1,)), ((), ())), preferred_element_type=jnp.float32
        )
        dscores = (weights * (dweights - inner_head[:, None])).astype(jnp.bfloat16)
        key_part = lax.dot_general(
            dscores, query_head, (((0,), (0,)), ((), ())), preferred_element_type=jnp.float32
        )
        return (key_part, value_part)

    key_parts, value_parts = lax.map(
        one_head,
        (
            split_heads(query_piece),
            split_heads(dout_piece),
            log_piece.T,
            inner_piece.T,
            key_heads,
            value_heads,
        ),
    )
    return (key_parts, value_parts)


def by_rows(queries, keys, values, out_cotangent, visible_counts, span_offset, out_weight):
    devices = lax.axis_size("seq")
    device = lax.axis_index("seq")
    frames = queries.shape[1]
    visible_rows = VIS_DEV
    capacity = MAXV // devices
    counts = visible_counts[0]
    offsets = span_offset[0]
    shard_ends = jnp.cumsum(counts)
    starts = shard_ends - counts
    this_device = device.reshape(1)
    count_here = pick_entry(counts, this_device)[0]
    start_here = pick_entry(starts, this_device)[0]
    span_begin = pick_entry(offsets, this_device)[0] % (count_here + 1)
    masked = frames - count_here
    send_slots = jnp.arange(devices * capacity, dtype=jnp.int32)
    peer_index = send_slots // capacity
    within = send_slots % capacity
    first_slot = (start_here - peer_index + devices - 1) // devices
    global_index = (first_slot + within) * devices + peer_index
    ranked = global_index - start_here
    live_slot = ranked < count_here
    frame_of = jnp.clip(jnp.where(ranked < span_begin, ranked, ranked + masked), 0, frames - 1)

    def outgoing(block):
        return jnp.where(
            live_slot[:, None], jnp.take(block[0], frame_of, axis=0), jnp.zeros((), block.dtype)
        )

    arrived = (
        lax.all_to_all(outgoing(queries), "seq", split_axis=0, concat_axis=0, tiled=True),
        lax.all_to_all(outgoing(keys), "seq", split_axis=0, concat_axis=0, tiled=True),
        lax.all_to_all(outgoing(values), "seq", split_axis=0, concat_axis=0, tiled=True),
        lax.all_to_all(outgoing(out_cotangent), "seq", split_axis=0, concat_axis=0, tiled=True),
    )
    packed_slot = jnp.arange(visible_rows, dtype=jnp.int32)
    packed_index = packed_slot * devices + device
    owner_shard = jnp.sum((shard_ends[None, :] <= packed_index[:, None]).astype(jnp.int32), axis=1)
    owner_first = (pick_entry(starts, owner_shard) - device + devices - 1) // devices
    arrived_row = owner_shard * capacity + packed_slot - owner_first
    query_pack = jnp.take(arrived[0], arrived_row, axis=0)
    key_pack = jnp.take(arrived[1], arrived_row, axis=0)
    value_pack = jnp.take(arrived[2], arrived_row, axis=0)
    cotangent_pack = jnp.take(arrived[3], arrived_row, axis=0)
    output_grad = lax.dot_general(
        cotangent_pack,
        lax.all_gather(out_weight, "seq", axis=0, tiled=True),
        (((1,), (1,)), ((), ())),
        preferred_element_type=jnp.float32,
    ).astype(jnp.bfloat16)
    key_all, value_all = (
        lax.all_gather(key_pack, "seq", axis=0, tiled=True),
        lax.all_gather(value_pack, "seq", axis=0, tiled=True),
    )
    attended, query_grad, log_totals, inner_sums = lax.map(
        query_side,
        (
            split_heads(query_pack),
            split_heads(key_all),
            split_heads(value_all),
            split_heads(output_grad),
        ),
    )
    attended = join_heads(attended)
    query_grad = join_heads(query_grad)
    log_rows = log_totals.T
    inner_rows = inner_sums.T
    partial_term = lax.dot_general(
        attended, cotangent_pack, (((0,), (0,)), ((), ())), preferred_element_type=jnp.float32
    )
    seq_sum = lax.psum_scatter(
        partial_term.astype(jnp.bfloat16), "seq", scatter_dimension=0, tiled=True
    )
    clip_sum = lax.psum(seq_sum, "clip").astype(jnp.float32)
    weight_grad = clip_sum * (lax.axis_size("clip") * visible_rows * devices) ** (-0.5)
    log_every, inner_every = (
        lax.all_gather(log_rows, "seq", axis=0, tiled=True),
        lax.all_gather(inner_rows, "seq", axis=0, tiled=True),
    )
    key_heads = split_heads(key_pack)
    value_heads = split_heads(value_pack)
    key_sum, value_sum = key_side_add(
        lax.all_gather(query_pack, "seq", axis=0, tiled=True),
        lax.all_gather(output_grad, "seq", axis=0, tiled=True),
        log_every,
        inner_every,
        key_heads,
        value_heads,
    )
    key_grad = join_heads((key_sum * HD ** (-0.5)).astype(jnp.bfloat16))
    value_grad = join_heads(value_sum.astype(jnp.bfloat16))
    back_first = (pick_entry(starts, peer_index) - device + devices - 1) // devices
    back_slot = back_first + within
    back_live = back_slot * devices + device < pick_entry(shard_ends, peer_index)
    back_row = jnp.clip(back_slot, 0, visible_rows - 1)

    def returning(block):
        return jnp.where(
            back_live[:, None], jnp.take(block, back_row, axis=0), jnp.zeros((), block.dtype)
        )

    returned = (
        lax.all_to_all(returning(query_grad), "seq", split_axis=0, concat_axis=0, tiled=True),
        lax.all_to_all(returning(key_grad), "seq", split_axis=0, concat_axis=0, tiled=True),
        lax.all_to_all(returning(value_grad), "seq", split_axis=0, concat_axis=0, tiled=True),
    )
    position = jnp.arange(frames, dtype=jnp.int32)
    visible = (position < span_begin) | (position >= span_begin + masked)
    frame_rank = jnp.where(position < span_begin, position, position - masked)
    frame_global = start_here + frame_rank
    frame_peer = frame_global % devices
    frame_slot = frame_global // devices
    frame_first = (start_here - frame_peer + devices - 1) // devices
    frame_row = jnp.clip(
        frame_peer * capacity + frame_slot - frame_first, 0, devices * capacity - 1
    )

    def placed(block):
        return jnp.where(
            visible[:, None], jnp.take(block, frame_row, axis=0), jnp.zeros((), block.dtype)
        )[None]

    return (placed(returned[0]), placed(returned[1]), placed(returned[2]), weight_grad)


ROUTES = (0, 6, 4, 2)
EARLY = 4


def head_lanes(core):
    lane = lax.broadcasted_iota(jnp.int32, (1, 128), 1)
    return ((lane // HD) == core).astype(jnp.float32).astype(jnp.bfloat16)


def scalar_copies(sources, targets, sems):
    copies = [
        pltpu.make_async_copy(source, target, sems.at[index])
        for index, (source, target) in enumerate(zip(sources, targets))
    ]
    for copy in copies:
        copy.start()
    return copies


def span_of(counts_ref, offsets_ref, owner):
    count = counts_ref[0, owner]
    begin = lax.rem(offsets_ref[0, owner], count + 1)
    return begin, MAXV - (count - begin)


def slot_masks(begin, end_start):
    slot = lax.broadcasted_iota(jnp.int32, (MAXV, 1), 0)
    early = (slot < begin).astype(jnp.float32).astype(jnp.bfloat16)
    late = (slot >= end_start).astype(jnp.float32).astype(jnp.bfloat16)
    return early, late


def pack_kernel(counts_hbm, offsets_hbm, q_ref, k_ref, v_ref, g_ref, *rest):
    sends, cot_ref, sides_ref = rest[:4], rest[4], rest[5]
    narrow, wide, counts_ref, offsets_ref, sems, scalar_sems = rest[6:]
    scalars = scalar_copies((counts_hbm, offsets_hbm), (counts_ref, offsets_ref), scalar_sems)
    frames = q_ref.shape[1]
    last = frames - MAXV
    device = lax.axis_index("seq")
    copies = []
    for index, source in enumerate((q_ref, k_ref, v_ref)):
        for side, start in enumerate((0, last)):
            copies.append(
                pltpu.make_async_copy(
                    source.at[0, pl.ds(start, MAXV)], narrow.at[index, side], sems.at[len(copies)]
                )
            )
    for side, start in enumerate((0, last)):
        copies.append(
            pltpu.make_async_copy(
                g_ref.at[0, pl.ds(start, MAXV)], wide.at[side], sems.at[len(copies)]
            )
        )
    for copy in copies:
        copy.start()
    for copy in scalars:
        copy.wait()
    begin, end_start = span_of(counts_ref, offsets_ref, device)
    early, late = slot_masks(begin, end_start)
    for copy in copies[:6]:
        copy.wait()
    for route, send in zip(ROUTES, sends):
        chip = (device ^ route) // 2
        lanes = pl.ds(pl.multiple_of(chip * 128, 128), 128)
        for index in range(3):
            send[:, index * 128 : (index + 1) * 128] = (
                narrow[index, 0, :, lanes] * early + narrow[index, 1, :, lanes] * late
            )
    for copy in copies[6:]:
        copy.wait()
    cot_ref[...] = wide[0] * early + wide[1] * late
    for side, mask in enumerate((early, late)):
        sides_ref[side] = jnp.broadcast_to(mask, (MAXV, 128))


def tables_kernel(counts_hbm, offsets_hbm, bias_ref, *rest):
    outs, (blank, counts_ref, offsets_ref, sems, scalar_sems) = rest[:3], rest[3:]
    scalars = scalar_copies((counts_hbm, offsets_hbm), (counts_ref, offsets_ref), scalar_sems)
    blank[...] = jnp.zeros_like(blank)
    copies = [
        pltpu.make_async_copy(blank, out.at[0, pl.ds(MAXV, blank.shape[0])], sems.at[index])
        for index, out in enumerate(outs)
    ]
    for copy in copies:
        copy.start()
    device = lax.axis_index("seq")
    for copy in scalars:
        copy.wait()
    slot = lax.broadcasted_iota(jnp.int32, (MAXV, 128), 0)
    for index in range(8):
        owner = device ^ (ROUTES[index // 2] + index % 2)
        begin, end_start = span_of(counts_ref, offsets_ref, owner)
        dead = (slot >= begin) & (slot < end_start)
        bias_ref[index * MAXV : (index + 1) * MAXV, :] = jnp.where(dead, -1e30, 0.0)
    for copy in copies:
        copy.wait()


def forward_kernel(bias_ref, *rest):
    blocks = rest[:8]
    packed, weights_ref, attended_ref = rest[8:]
    lanes = head_lanes(lax.axis_index("seq") % 2)
    for index in range(8):
        packed[index * MAXV : (index + 1) * MAXV, :] = blocks[index][...]
    bias = bias_ref[...]
    bias = jnp.concatenate([bias, bias], axis=1)
    factor = HD ** (-0.5)
    key = packed[:, 128:256] * lanes
    value_t = packed[:, 256:384].T
    for step in range(3):
        rows = slice(step * 256, (step + 1) * 256)
        scores = (
            lax.dot_general(
                key, packed[rows, 0:128], (((1,), (1,)), ((), ())), preferred_element_type=jnp.float32
            )
            * factor
        )
        scores = scores + bias
        scores = jnp.exp(scores - jnp.max(scores, axis=0, keepdims=True))
        weights = scores * (1.0 / jnp.sum(scores, axis=0, keepdims=True))
        weights_ref[:, rows] = weights
        attended_ref[:, rows] = jnp.dot(
            value_t, weights.astype(jnp.bfloat16), preferred_element_type=jnp.float32
        ).astype(jnp.bfloat16)


def own_rows(ref, core, columns):
    both = ref[:, columns].astype(jnp.float32)
    return jnp.where(core == 0, both[:HD], both[HD:]).astype(jnp.bfloat16)


def project(cot, w_ref, core):
    top = (core == 0).astype(jnp.float32).astype(jnp.bfloat16)
    bottom = (core == 1).astype(jnp.float32).astype(jnp.bfloat16)
    w_both = jnp.concatenate([w_ref[...] * top, w_ref[...] * bottom], axis=0)
    return lax.dot_general(
        cot[...], w_both, (((1,), (1,)), ((), ())), preferred_element_type=jnp.float32
    ).astype(jnp.bfloat16)


def early_kernel(attended_ref, w_ref, *rest):
    cots, dout_ref, wg_ref, cot = rest[:EARLY], rest[EARLY], rest[EARLY + 1], rest[EARLY + 2]
    core = lax.axis_index("seq") % 2
    for index in range(EARLY):
        cot[index * MAXV : (index + 1) * MAXV, :] = cots[index][...]
    dout_ref[...] = project(cot, w_ref, core)
    wg_ref[...] = jnp.dot(
        own_rows(attended_ref, core, slice(0, EARLY * MAXV)),
        cot[...],
        preferred_element_type=jnp.float32,
    )


def late_kernel(attended_ref, w_ref, begun_ref, *rest):
    cots = rest[: 8 - EARLY]
    dout_ref, kept_ref, sent_ref, cot = rest[8 - EARLY :]
    core = lax.axis_index("seq") % 2
    for index in range(8 - EARLY):
        cot[index * MAXV : (index + 1) * MAXV, :] = cots[index][...]
    dout_ref[...] = project(cot, w_ref, core)
    total = begun_ref[...] + jnp.dot(
        own_rows(attended_ref, core, slice(EARLY * MAXV, 8 * MAXV)),
        cot[...],
        preferred_element_type=jnp.float32,
    )
    half = total.shape[0] // 2
    lower = lax.axis_index("clip") % 2 == 0
    kept_ref[...] = jnp.where(lower, total[:half], total[half:]).astype(jnp.bfloat16)
    sent_ref[...] = jnp.where(lower, total[half:], total[:half]).astype(jnp.bfloat16)


def backward_kernel(packed, weights_ref, attended_ref, begun_ref, ended_ref, *rest):
    outs = rest[:2]
    dout, dq = rest[2:]
    core = lax.axis_index("seq") % 2
    lanes = head_lanes(core)
    dout[: EARLY * MAXV, :] = begun_ref[...]
    dout[EARLY * MAXV :, :] = ended_ref[...]
    key_t = (packed[:, 128:256] * lanes).T
    value = packed[:, 256:384]
    factor = HD ** (-0.5)
    dout_t = dout[...].astype(jnp.float32).T
    key_grad = jnp.zeros((8 * MAXV, 128), jnp.float32)
    value_grad = jnp.zeros((8 * MAXV, 128), jnp.float32)
    for step in range(3):
        rows = slice(step * 256, (step + 1) * 256)
        query_own = packed[rows, 0:128] * lanes
        dout_own = dout[rows, :]
        weights = weights_ref[:, rows]
        inner = jnp.sum(
            dout_t[:, rows] * attended_ref[:, rows].astype(jnp.float32), axis=0, keepdims=True
        )
        dweights = lax.dot_general(
            value, dout_own, (((1,), (1,)), ((), ())), preferred_element_type=jnp.float32
        )
        dscores = (weights * (dweights - inner)).astype(jnp.bfloat16)
        value_grad += jnp.dot(
            weights.astype(jnp.bfloat16), dout_own, preferred_element_type=jnp.float32
        )
        key_grad += jnp.dot(dscores, query_own, preferred_element_type=jnp.float32)
        dq_t = jnp.dot(key_t, dscores, preferred_element_type=jnp.float32) * factor
        dq[rows, :] = dq_t.T.astype(jnp.bfloat16)
    key_grad = (key_grad * factor).astype(jnp.bfloat16)
    value_grad = value_grad.astype(jnp.bfloat16)
    for index in range(8):
        rows = slice(index * MAXV, (index + 1) * MAXV)
        outs[index % 2][index // 2, :, 0:128] = dq[rows, :]
        outs[index % 2][index // 2, :, 128:256] = key_grad[rows]
        outs[index % 2][index // 2, :, 256:384] = value_grad[rows]


def combine_kernel(kept, crossed, *outs):
    for index in range(4):
        outs[index][...] = kept[index] + crossed[index]


def unpack_kernel(scale, sides_ref, *rest):
    blocks, shares, outs, wg_hbm = rest[:4], rest[4:6], rest[9:12], rest[12]
    edges, wg_ref, sems = rest[13:]
    device = lax.axis_index("seq")
    last = outs[0].shape[1] - MAXV
    copies = []
    for index in range(3):
        for route, block in zip(ROUTES, blocks):
            chip = (device ^ route) // 2
            lanes = pl.ds(pl.multiple_of(chip * 128, 128), 128)
            piece = block[:, index * 128 : (index + 1) * 128]
            for side in range(2):
                edges[index, side, :, lanes] = piece * sides_ref[side]
        for side, start in enumerate((0, last)):
            copies.append(
                pltpu.make_async_copy(
                    edges.at[index, side],
                    outs[index].at[0, pl.ds(start, MAXV)],
                    sems.at[len(copies)],
                )
            )
            copies[-1].start()
    lower = lax.axis_index("clip") % 2 == 0
    mine, other = [share[...].astype(jnp.float32) * scale for share in shares]
    half = mine.shape[0]
    wg_ref[:half, :] = jnp.where(lower, mine, other)
    wg_ref[half:, :] = jnp.where(lower, other, mine)
    copies.append(pltpu.make_async_copy(wg_ref, wg_hbm, sems.at[len(copies)]))
    copies[-1].start()
    for copy in copies:
        copy.wait()


PARAMS = pltpu.CompilerParams(vmem_limit_bytes=24 << 20)
ANYWHERE = pl.BlockSpec(memory_space=pl.ANY)
SCALARS = pl.BlockSpec(memory_space=pltpu.SMEM)
LOCAL = pl.BlockSpec(memory_space=pltpu.VMEM)


def in_hbm(block):
    return pltpu.with_memory_space_constraint(block, pltpu.HBM)


def by_heads(queries, keys, values, out_cotangent, visible_counts, span_offset, out_weight):
    bf16 = jnp.bfloat16
    pairs = lax.axis_size("seq")
    clips = lax.axis_size("clip")

    def shift(block, step):
        return lax.ppermute(block, "seq", [(i, i ^ step) for i in range(pairs)])

    narrow = jax.ShapeDtypeStruct((MAXV, 384), bf16)
    wide = jax.ShapeDtypeStruct((MAXV, out_cotangent.shape[2]), bf16)

    def seen(kernel, outs, specs, operands, scratch=(), out_specs=None):
        return pl.pallas_call(
            kernel,
            out_shape=outs,
            in_specs=specs,
            out_specs=out_specs or [LOCAL] * len(outs),
            scratch_shapes=scratch,
            compiler_params=PARAMS,
        )(*operands)

    width = out_cotangent.shape[2]
    rows = 8 * MAXV
    counts, offsets = in_hbm(visible_counts), in_hbm(span_offset)
    table = pltpu.SMEM(visible_counts.shape, jnp.int32)
    tables = [table, table]
    pair_sems = pltpu.SemaphoreType.DMA((2,))
    *sends, cot, sides = seen(
        pack_kernel,
        [narrow] * 4 + [wide, pltpu.VMEM((2, MAXV, 128), bf16)],
        [ANYWHERE] * 6,
        (counts, offsets, *map(in_hbm, (queries, keys, values, out_cotangent))),
        [
            pltpu.VMEM((3, 2, MAXV, queries.shape[2]), bf16),
            pltpu.VMEM((2, MAXV, width), bf16),
            *tables,
            pltpu.SemaphoreType.DMA((8,)),
            pair_sems,
        ],
    )
    even = [sends[0]] + [shift(sends[i], ROUTES[i]) for i in (1, 2, 3)]
    even_cot = [cot] + [shift(cot, ROUTES[i]) for i in (1, 2, 3)]
    odd = [shift(block, 1) for block in even]
    odd_cot = [shift(block, 1) for block in even_cot]
    blocks = [block for pair in zip(even, odd) for block in pair]
    cots = [block for pair in zip(even_cot, odd_cot) for block in pair]
    full = jax.ShapeDtypeStruct(queries.shape, bf16)
    bias, *blanks = seen(
        tables_kernel,
        [pltpu.VMEM((rows, 128), jnp.float32)] + [full] * 3,
        [ANYWHERE] * 2,
        (counts, offsets),
        [
            pltpu.VMEM((queries.shape[1] - 2 * MAXV, queries.shape[2]), bf16),
            *tables,
            pltpu.SemaphoreType.DMA((3,)),
            pair_sems,
        ],
        [LOCAL] + [ANYWHERE] * 3,
    )
    packed, weights, attended = seen(
        forward_kernel,
        [
            pltpu.VMEM((rows, 384), bf16),
            pltpu.VMEM((rows, rows), jnp.float32),
            pltpu.VMEM((128, rows), bf16),
        ],
        [LOCAL] * 9,
        (bias, *blocks),
    )
    begun, begun_wg = seen(
        early_kernel,
        [pltpu.VMEM((EARLY * MAXV, 128), bf16), pltpu.VMEM(out_weight.shape, jnp.float32)],
        [LOCAL] * (2 + EARLY),
        (attended, out_weight, *cots[:EARLY]),
        [pltpu.VMEM((EARLY * MAXV, width), bf16)],
    )
    share = jax.ShapeDtypeStruct((out_weight.shape[0] // 2, width), bf16)
    ended, mine, sent = seen(
        late_kernel,
        [pltpu.VMEM(((8 - EARLY) * MAXV, 128), bf16), share, share],
        [LOCAL] * (3 + 8 - EARLY),
        (attended, out_weight, begun_wg, *cots[EARLY:]),
        [pltpu.VMEM(((8 - EARLY) * MAXV, width), bf16)],
    )

    def across(block, step):
        return lax.ppermute(block, "clip", [(i, i ^ step) for i in range(clips)])

    other = across(sent, 1)
    step = 1
    while step < clips:
        mine = (mine.astype(jnp.float32) + other.astype(jnp.float32)).astype(bf16)
        step *= 2
        if step < clips:
            other = across(mine, step)
    shares = [mine, across(mine, 1)]
    kept, leaving = seen(
        backward_kernel,
        [jax.ShapeDtypeStruct((4, MAXV, 384), bf16)] * 2,
        [LOCAL] * 5,
        (packed, weights, attended, begun, ended),
        [pltpu.VMEM((rows, 128), bf16)] * 2,
    )
    crossed = shift(leaving, 1)
    joined = seen(combine_kernel, [narrow] * 4, [LOCAL] * 2, (kept, crossed))
    home = [joined[0]] + [shift(joined[i], ROUTES[i]) for i in (1, 2, 3)]
    scale = (clips * VIS_DEV * pairs) ** (-0.5)
    return tuple(
        pl.pallas_call(
            functools.partial(unpack_kernel, scale),
            out_shape=[full] * 3 + [jax.ShapeDtypeStruct(out_weight.shape, jnp.float32)],
            in_specs=[LOCAL] * 7 + [ANYWHERE] * 3,
            out_specs=[ANYWHERE] * 4,
            scratch_shapes=[
                pltpu.VMEM((3, 2, MAXV, queries.shape[2]), bf16),
                pltpu.VMEM(out_weight.shape, jnp.float32),
                pltpu.SemaphoreType.DMA((7,)),
            ],
            input_output_aliases={7: 0, 8: 1, 9: 2},
            compiler_params=PARAMS,
            name="unpack",
        )(sides, *home, *shares, *blanks)
    )


def local(*arrays):
    if lax.axis_size("seq") == HEADS and lax.axis_size("clip") in (2, 4, 8, 16):
        return by_heads(*arrays)
    return by_rows(*arrays)


def solution(mesh):
    placed = (
        P("clip", "seq", None),
        P("clip", "seq", None),
        P("clip", "seq", None),
        P("clip", "seq", None),
        P("clip", None),
        P("clip", None),
        P("seq", None),
    )
    return jax.shard_map(
        local,
        mesh=mesh,
        in_specs=placed,
        out_specs=(
            P("clip", "seq", None),
            P("clip", "seq", None),
            P("clip", "seq", None),
            P("seq", None),
        ),
        check_vma=False,
    )
```

```python
import functools

import jax
import jax.numpy as jnp
from jax import lax
from jax.experimental import pallas as pl
from jax.experimental.pallas import tpu as pltpu
from jax.sharding import PartitionSpec as P


HEADS = 8
HD = 64
VIS_DEV = 48
MAXV = 96


def pick_entry(table, position):
    order = jnp.arange(table.shape[0], dtype=jnp.int32)
    chosen = jnp.where(order[None, :] == position[:, None], table[None, :], 0)
    return jnp.sum(chosen, axis=1)


def split_heads(block):
    return block.reshape(block.shape[0], HEADS, HD).transpose(1, 0, 2)


def join_heads(block):
    return block.transpose(1, 0, 2).reshape(block.shape[1], HEADS * HD)


def query_side(parts):
    query_head, key_head, value_head, dout_head = parts
    factor = HD ** (-0.5)
    scores = (
        lax.dot_general(
            query_head, key_head, (((1,), (1,)), ((), ())), preferred_element_type=jnp.float32
        )
        * factor
    )
    peak_score = jnp.max(scores, axis=1, keepdims=True)
    log_total = peak_score + jnp.log(jnp.sum(jnp.exp(scores - peak_score), axis=1, keepdims=True))
    weights = jnp.exp(scores - log_total)
    weights_low = weights.astype(jnp.bfloat16)
    attended = jnp.dot(weights_low, value_head, preferred_element_type=jnp.float32).astype(
        jnp.bfloat16
    )
    inner_sum = jnp.sum(
        dout_head.astype(jnp.float32) * attended.astype(jnp.float32), axis=1, keepdims=True
    )
    dweights = lax.dot_general(
        dout_head, value_head, (((1,), (1,)), ((), ())), preferred_element_type=jnp.float32
    )
    dscores = (weights * (dweights - inner_sum)).astype(jnp.bfloat16)
    grad_query = (jnp.dot(dscores, key_head, preferred_element_type=jnp.float32) * factor).astype(
        jnp.bfloat16
    )
    return (attended, grad_query, log_total[:, 0], inner_sum[:, 0])


def key_side_add(query_piece, dout_piece, log_piece, inner_piece, key_heads, value_heads):
    factor = HD ** (-0.5)

    def one_head(parts):
        query_head, dout_head, log_head, inner_head, key_head, value_head = parts
        scores = (
            lax.dot_general(
                query_head, key_head, (((1,), (1,)), ((), ())), preferred_element_type=jnp.float32
            )
            * factor
        )
        weights = jnp.exp(scores - log_head[:, None])
        weights_low = weights.astype(jnp.bfloat16)
        value_part = lax.dot_general(
            weights_low, dout_head, (((0,), (0,)), ((), ())), preferred_element_type=jnp.float32
        )
        dweights = lax.dot_general(
            dout_head, value_head, (((1,), (1,)), ((), ())), preferred_element_type=jnp.float32
        )
        dscores = (weights * (dweights - inner_head[:, None])).astype(jnp.bfloat16)
        key_part = lax.dot_general(
            dscores, query_head, (((0,), (0,)), ((), ())), preferred_element_type=jnp.float32
        )
        return (key_part, value_part)

    key_parts, value_parts = lax.map(
        one_head,
        (
            split_heads(query_piece),
            split_heads(dout_piece),
            log_piece.T,
            inner_piece.T,
            key_heads,
            value_heads,
        ),
    )
    return (key_parts, value_parts)


def by_rows(queries, keys, values, out_cotangent, visible_counts, span_offset, out_weight):
    devices = lax.axis_size("seq")
    device = lax.axis_index("seq")
    frames = queries.shape[1]
    visible_rows = VIS_DEV
    capacity = MAXV // devices
    counts = visible_counts[0]
    offsets = span_offset[0]
    shard_ends = jnp.cumsum(counts)
    starts = shard_ends - counts
    this_device = device.reshape(1)
    count_here = pick_entry(counts, this_device)[0]
    start_here = pick_entry(starts, this_device)[0]
    span_begin = pick_entry(offsets, this_device)[0] % (count_here + 1)
    masked = frames - count_here
    send_slots = jnp.arange(devices * capacity, dtype=jnp.int32)
    peer_index = send_slots // capacity
    within = send_slots % capacity
    first_slot = (start_here - peer_index + devices - 1) // devices
    global_index = (first_slot + within) * devices + peer_index
    ranked = global_index - start_here
    live_slot = ranked < count_here
    frame_of = jnp.clip(jnp.where(ranked < span_begin, ranked, ranked + masked), 0, frames - 1)

    def outgoing(block):
        return jnp.where(
            live_slot[:, None], jnp.take(block[0], frame_of, axis=0), jnp.zeros((), block.dtype)
        )

    arrived = (
        lax.all_to_all(outgoing(queries), "seq", split_axis=0, concat_axis=0, tiled=True),
        lax.all_to_all(outgoing(keys), "seq", split_axis=0, concat_axis=0, tiled=True),
        lax.all_to_all(outgoing(values), "seq", split_axis=0, concat_axis=0, tiled=True),
        lax.all_to_all(outgoing(out_cotangent), "seq", split_axis=0, concat_axis=0, tiled=True),
    )
    packed_slot = jnp.arange(visible_rows, dtype=jnp.int32)
    packed_index = packed_slot * devices + device
    owner_shard = jnp.sum((shard_ends[None, :] <= packed_index[:, None]).astype(jnp.int32), axis=1)
    owner_first = (pick_entry(starts, owner_shard) - device + devices - 1) // devices
    arrived_row = owner_shard * capacity + packed_slot - owner_first
    query_pack = jnp.take(arrived[0], arrived_row, axis=0)
    key_pack = jnp.take(arrived[1], arrived_row, axis=0)
    value_pack = jnp.take(arrived[2], arrived_row, axis=0)
    cotangent_pack = jnp.take(arrived[3], arrived_row, axis=0)
    output_grad = lax.dot_general(
        cotangent_pack,
        lax.all_gather(out_weight, "seq", axis=0, tiled=True),
        (((1,), (1,)), ((), ())),
        preferred_element_type=jnp.float32,
    ).astype(jnp.bfloat16)
    key_all, value_all = (
        lax.all_gather(key_pack, "seq", axis=0, tiled=True),
        lax.all_gather(value_pack, "seq", axis=0, tiled=True),
    )
    attended, query_grad, log_totals, inner_sums = lax.map(
        query_side,
        (
            split_heads(query_pack),
            split_heads(key_all),
            split_heads(value_all),
            split_heads(output_grad),
        ),
    )
    attended = join_heads(attended)
    query_grad = join_heads(query_grad)
    log_rows = log_totals.T
    inner_rows = inner_sums.T
    partial_term = lax.dot_general(
        attended, cotangent_pack, (((0,), (0,)), ((), ())), preferred_element_type=jnp.float32
    )
    seq_sum = lax.psum_scatter(
        partial_term.astype(jnp.bfloat16), "seq", scatter_dimension=0, tiled=True
    )
    clip_sum = lax.psum(seq_sum, "clip").astype(jnp.float32)
    weight_grad = clip_sum * (lax.axis_size("clip") * visible_rows * devices) ** (-0.5)
    log_every, inner_every = (
        lax.all_gather(log_rows, "seq", axis=0, tiled=True),
        lax.all_gather(inner_rows, "seq", axis=0, tiled=True),
    )
    key_heads = split_heads(key_pack)
    value_heads = split_heads(value_pack)
    key_sum, value_sum = key_side_add(
        lax.all_gather(query_pack, "seq", axis=0, tiled=True),
        lax.all_gather(output_grad, "seq", axis=0, tiled=True),
        log_every,
        inner_every,
        key_heads,
        value_heads,
    )
    key_grad = join_heads((key_sum * HD ** (-0.5)).astype(jnp.bfloat16))
    value_grad = join_heads(value_sum.astype(jnp.bfloat16))
    back_first = (pick_entry(starts, peer_index) - device + devices - 1) // devices
    back_slot = back_first + within
    back_live = back_slot * devices + device < pick_entry(shard_ends, peer_index)
    back_row = jnp.clip(back_slot, 0, visible_rows - 1)

    def returning(block):
        return jnp.where(
            back_live[:, None], jnp.take(block, back_row, axis=0), jnp.zeros((), block.dtype)
        )

    returned = (
        lax.all_to_all(returning(query_grad), "seq", split_axis=0, concat_axis=0, tiled=True),
        lax.all_to_all(returning(key_grad), "seq", split_axis=0, concat_axis=0, tiled=True),
        lax.all_to_all(returning(value_grad), "seq", split_axis=0, concat_axis=0, tiled=True),
    )
    position = jnp.arange(frames, dtype=jnp.int32)
    visible = (position < span_begin) | (position >= span_begin + masked)
    frame_rank = jnp.where(position < span_begin, position, position - masked)
    frame_global = start_here + frame_rank
    frame_peer = frame_global % devices
    frame_slot = frame_global // devices
    frame_first = (start_here - frame_peer + devices - 1) // devices
    frame_row = jnp.clip(
        frame_peer * capacity + frame_slot - frame_first, 0, devices * capacity - 1
    )

    def placed(block):
        return jnp.where(
            visible[:, None], jnp.take(block, frame_row, axis=0), jnp.zeros((), block.dtype)
        )[None]

    return (placed(returned[0]), placed(returned[1]), placed(returned[2]), weight_grad)


ROUTES = (0, 6, 4, 2)


def head_lanes(core):
    lane = lax.broadcasted_iota(jnp.int32, (1, 128), 1)
    return ((lane // HD) == core).astype(jnp.float32).astype(jnp.bfloat16)


def scalar_copies(sources, targets, sems):
    copies = [
        pltpu.make_async_copy(source, target, sems.at[index])
        for index, (source, target) in enumerate(zip(sources, targets))
    ]
    for copy in copies:
        copy.start()
    return copies


def span_of(counts_ref, offsets_ref, owner):
    count = counts_ref[0, owner]
    begin = lax.rem(offsets_ref[0, owner], count + 1)
    return begin, MAXV - (count - begin)


def slot_masks(begin, end_start):
    slot = lax.broadcasted_iota(jnp.int32, (MAXV, 1), 0)
    early = (slot < begin).astype(jnp.float32).astype(jnp.bfloat16)
    late = (slot >= end_start).astype(jnp.float32).astype(jnp.bfloat16)
    return early, late


def pack_kernel(counts_hbm, offsets_hbm, q_ref, k_ref, v_ref, g_ref, *rest):
    sends, cot_ref, sides_ref = rest[:4], rest[4], rest[5]
    narrow, wide, counts_ref, offsets_ref, sems, scalar_sems = rest[6:]
    scalars = scalar_copies((counts_hbm, offsets_hbm), (counts_ref, offsets_ref), scalar_sems)
    frames = q_ref.shape[1]
    last = frames - MAXV
    device = lax.axis_index("seq")
    copies = []
    for index, source in enumerate((q_ref, k_ref, v_ref)):
        for side, start in enumerate((0, last)):
            copies.append(
                pltpu.make_async_copy(
                    source.at[0, pl.ds(start, MAXV)], narrow.at[index, side], sems.at[len(copies)]
                )
            )
    for side, start in enumerate((0, last)):
        copies.append(
            pltpu.make_async_copy(
                g_ref.at[0, pl.ds(start, MAXV)], wide.at[side], sems.at[len(copies)]
            )
        )
    for copy in copies:
        copy.start()
    for copy in scalars:
        copy.wait()
    begin, end_start = span_of(counts_ref, offsets_ref, device)
    early, late = slot_masks(begin, end_start)
    for copy in copies[:6]:
        copy.wait()
    for route, send in zip(ROUTES, sends):
        chip = (device ^ route) // 2
        lanes = pl.ds(pl.multiple_of(chip * 128, 128), 128)
        for index in range(3):
            send[:, index * 128 : (index + 1) * 128] = (
                narrow[index, 0, :, lanes] * early + narrow[index, 1, :, lanes] * late
            )
    for copy in copies[6:]:
        copy.wait()
    cot_ref[...] = wide[0] * early + wide[1] * late
    for side, mask in enumerate((early, late)):
        sides_ref[side] = jnp.broadcast_to(mask, (MAXV, 128))


def tables_kernel(counts_hbm, offsets_hbm, bias_ref, *rest):
    outs, (blank, counts_ref, offsets_ref, sems, scalar_sems) = rest[:3], rest[3:]
    scalars = scalar_copies((counts_hbm, offsets_hbm), (counts_ref, offsets_ref), scalar_sems)
    blank[...] = jnp.zeros_like(blank)
    copies = [
        pltpu.make_async_copy(blank, out.at[0, pl.ds(MAXV, blank.shape[0])], sems.at[index])
        for index, out in enumerate(outs)
    ]
    for copy in copies:
        copy.start()
    device = lax.axis_index("seq")
    for copy in scalars:
        copy.wait()
    slot = lax.broadcasted_iota(jnp.int32, (MAXV, 128), 0)
    for index in range(8):
        owner = device ^ (ROUTES[index // 2] + index % 2)
        begin, end_start = span_of(counts_ref, offsets_ref, owner)
        dead = (slot >= begin) & (slot < end_start)
        bias_ref[index * MAXV : (index + 1) * MAXV, :] = jnp.where(dead, -1e30, 0.0)
    for copy in copies:
        copy.wait()


def forward_kernel(bias_ref, *rest):
    blocks = rest[:8]
    shared, query, weights_ref, attended_ref = rest[8:]
    for index in range(8):
        shared[index * MAXV : (index + 1) * MAXV, :] = blocks[index][:, 128:384]
    for index in range(4):
        query[index * MAXV : (index + 1) * MAXV, :] = blocks[2 * index][:, 0:128]
    bias = bias_ref[...]
    bias = jnp.concatenate([bias, bias, bias], axis=1)
    factor = HD ** (-0.5)
    value_t = shared[:, 128:256].T
    for head in range(2):
        key = shared[:, 0:128] * head_lanes(head)
        scores = (
            lax.dot_general(
                key, query[...], (((1,), (1,)), ((), ())), preferred_element_type=jnp.float32
            )
            * factor
        )
        scores = scores + bias
        scores = jnp.exp(scores - jnp.max(scores, axis=0, keepdims=True))
        weights = scores * (1.0 / jnp.sum(scores, axis=0, keepdims=True))
        weights_ref[head] = weights
        own = slice(head * HD, (head + 1) * HD)
        attended_ref[own, :] = jnp.dot(
            value_t, weights.astype(jnp.bfloat16), preferred_element_type=jnp.float32
        )[own].astype(jnp.bfloat16)


def gather_cots(cots, cot):
    for index, block in enumerate(cots):
        cot[index * MAXV : (index + 1) * MAXV, :] = block[...]


def project(cot, w_ref, w_other_ref, core):
    first = (core == 0).astype(jnp.float32).astype(jnp.bfloat16)
    second = (core == 1).astype(jnp.float32).astype(jnp.bfloat16)
    top = w_ref[...] * first + w_other_ref[...] * second
    bottom = w_ref[...] * second + w_other_ref[...] * first
    return lax.dot_general(
        cot[...],
        jnp.concatenate([top, bottom], axis=0),
        (((1,), (1,)), ((), ())),
        preferred_element_type=jnp.float32,
    ).astype(jnp.bfloat16)


def early_kernel(attended_ref, w_ref, w_other_ref, *rest):
    cots, dout_ref, wg_ref, cot = rest[:2], rest[2], rest[3], rest[4]
    gather_cots(cots, cot)
    dout_ref[...] = project(cot, w_ref, w_other_ref, lax.axis_index("seq") % 2)
    wg_ref[...] = jnp.dot(
        attended_ref[:, : 2 * MAXV], cot[...], preferred_element_type=jnp.float32
    )


def late_kernel(attended_ref, w_ref, w_other_ref, begun_ref, *rest):
    cots, dout_ref, own_ref, other_ref, cot = rest[:2], rest[2], rest[3], rest[4], rest[5]
    core = lax.axis_index("seq") % 2
    gather_cots(cots, cot)
    total = begun_ref[...] + jnp.dot(
        attended_ref[:, 2 * MAXV :], cot[...], preferred_element_type=jnp.float32
    )
    own_ref[...] = jnp.where(core == 0, total[:HD], total[HD:])
    other_ref[...] = jnp.where(core == 0, total[HD:], total[:HD]).astype(jnp.bfloat16)
    dout_ref[...] = project(cot, w_ref, w_other_ref, core)


def backward_kernel(shared, query, weights_ref, attended_ref, begun_ref, ended_ref, *rest):
    kept_query, kept_shared, leaving, dout = rest
    dout[: 2 * MAXV, :] = begun_ref[...]
    dout[2 * MAXV :, :] = ended_ref[...]
    factor = HD ** (-0.5)
    products = dout[...].astype(jnp.float32).T * attended_ref[...].astype(jnp.float32)
    value = shared[:, 128:256]
    key_grad = jnp.zeros((8 * MAXV, 128), jnp.float32)
    value_grad = jnp.zeros((8 * MAXV, 128), jnp.float32)
    query_grad = jnp.zeros((128, 4 * MAXV), jnp.float32)
    for head in range(2):
        lanes = head_lanes(head)
        dout_own = dout[...] * lanes
        key_t = (shared[:, 0:128] * lanes).T
        inner = jnp.sum(products[head * HD : (head + 1) * HD], axis=0, keepdims=True)
        weights = weights_ref[head]
        dweights = lax.dot_general(
            value, dout_own, (((1,), (1,)), ((), ())), preferred_element_type=jnp.float32
        )
        dscores = (weights * (dweights - inner)).astype(jnp.bfloat16)
        value_grad += jnp.dot(
            weights.astype(jnp.bfloat16), dout_own, preferred_element_type=jnp.float32
        )
        key_grad += jnp.dot(dscores, query[...] * lanes, preferred_element_type=jnp.float32)
        query_grad += jnp.dot(key_t, dscores, preferred_element_type=jnp.float32)
    query_grad = (query_grad * factor).T.astype(jnp.bfloat16)
    key_grad = key_grad * factor
    for index in range(4):
        kept_query[index] = query_grad[index * MAXV : (index + 1) * MAXV]
        rows = slice(2 * index * MAXV, (2 * index + 1) * MAXV)
        kept_shared[index, :, 0:128] = key_grad[rows]
        kept_shared[index, :, 128:256] = value_grad[rows]
        rows = slice((2 * index + 1) * MAXV, (2 * index + 2) * MAXV)
        leaving[index, :, 0:128] = key_grad[rows].astype(jnp.bfloat16)
        leaving[index, :, 128:256] = value_grad[rows].astype(jnp.bfloat16)


def combine_kernel(kept_query, kept_shared, crossed, *outs):
    for index in range(4):
        outs[index][:, 0:128] = kept_query[index]
        outs[index][:, 128:384] = (
            kept_shared[index] + crossed[index].astype(jnp.float32)
        ).astype(jnp.bfloat16)


def unpack_kernel(scale, sides_ref, *rest):
    blocks, shares, outs, wg_hbm = rest[:4], rest[4:6], rest[9:12], rest[12]
    edges, wg_ref, sems = rest[13:]
    device = lax.axis_index("seq")
    last = outs[0].shape[1] - MAXV
    copies = []
    for index in range(3):
        for route, block in zip(ROUTES, blocks):
            chip = (device ^ route) // 2
            lanes = pl.ds(pl.multiple_of(chip * 128, 128), 128)
            piece = block[:, index * 128 : (index + 1) * 128]
            for side in range(2):
                edges[index, side, :, lanes] = piece * sides_ref[side]
        for side, start in enumerate((0, last)):
            copies.append(
                pltpu.make_async_copy(
                    edges.at[index, side],
                    outs[index].at[0, pl.ds(start, MAXV)],
                    sems.at[len(copies)],
                )
            )
            copies[-1].start()
    wg_ref[...] = (shares[0][...].astype(jnp.float32) + shares[1][...].astype(jnp.float32)) * scale
    copies.append(pltpu.make_async_copy(wg_ref, wg_hbm, sems.at[len(copies)]))
    copies[-1].start()
    for copy in copies:
        copy.wait()


PARAMS = pltpu.CompilerParams(vmem_limit_bytes=24 << 20)
ANYWHERE = pl.BlockSpec(memory_space=pl.ANY)
SCALARS = pl.BlockSpec(memory_space=pltpu.SMEM)
LOCAL = pl.BlockSpec(memory_space=pltpu.VMEM)


def in_hbm(block):
    return pltpu.with_memory_space_constraint(block, pltpu.HBM)


def by_heads(queries, keys, values, out_cotangent, visible_counts, span_offset, out_weight):
    bf16 = jnp.bfloat16
    pairs = lax.axis_size("seq")
    clips = lax.axis_size("clip")

    def shift(block, step):
        return lax.ppermute(block, "seq", [(i, i ^ step) for i in range(pairs)])

    narrow = jax.ShapeDtypeStruct((MAXV, 384), bf16)
    wide = jax.ShapeDtypeStruct((MAXV, out_cotangent.shape[2]), bf16)

    def seen(kernel, outs, specs, operands, scratch=(), out_specs=None):
        return pl.pallas_call(
            kernel,
            out_shape=outs,
            in_specs=specs,
            out_specs=out_specs or [LOCAL] * len(outs),
            scratch_shapes=scratch,
            compiler_params=PARAMS,
        )(*operands)

    width = out_cotangent.shape[2]
    rows = 8 * MAXV
    counts, offsets = in_hbm(visible_counts), in_hbm(span_offset)
    table = pltpu.SMEM(visible_counts.shape, jnp.int32)
    tables = [table, table]
    pair_sems = pltpu.SemaphoreType.DMA((2,))
    *sends, cot, sides = seen(
        pack_kernel,
        [narrow] * 4 + [wide, pltpu.VMEM((2, MAXV, 128), bf16)],
        [ANYWHERE] * 6,
        (counts, offsets, *map(in_hbm, (queries, keys, values, out_cotangent))),
        [
            pltpu.VMEM((3, 2, MAXV, queries.shape[2]), bf16),
            pltpu.VMEM((2, MAXV, width), bf16),
            *tables,
            pltpu.SemaphoreType.DMA((8,)),
            pair_sems,
        ],
    )
    even = [sends[0]] + [shift(sends[i], ROUTES[i]) for i in (1, 2, 3)]
    even_cot = [cot] + [shift(cot, ROUTES[i]) for i in (1, 2, 3)]
    odd = [shift(block, 1) for block in even]
    w_other = shift(out_weight, 1)
    blocks = [block for pair in zip(even, odd) for block in pair]
    full = jax.ShapeDtypeStruct(queries.shape, bf16)
    bias, *blanks = seen(
        tables_kernel,
        [pltpu.VMEM((rows, 128), jnp.float32)] + [full] * 3,
        [ANYWHERE] * 2,
        (counts, offsets),
        [
            pltpu.VMEM((queries.shape[1] - 2 * MAXV, queries.shape[2]), bf16),
            *tables,
            pltpu.SemaphoreType.DMA((3,)),
            pair_sems,
        ],
        [LOCAL] + [ANYWHERE] * 3,
    )
    own_rows = 4 * MAXV
    shared, query, weights, attended = seen(
        forward_kernel,
        [
            pltpu.VMEM((rows, 256), bf16),
            pltpu.VMEM((own_rows, 128), bf16),
            pltpu.VMEM((2, rows, own_rows), jnp.float32),
            pltpu.VMEM((128, own_rows), bf16),
        ],
        [LOCAL] * 9,
        (bias, *blocks),
    )
    projected = pltpu.VMEM((2 * MAXV, 128), bf16)
    gathered = [pltpu.VMEM((2 * MAXV, width), bf16)]
    begun, begun_wg = seen(
        early_kernel,
        [projected, pltpu.VMEM((128, width), jnp.float32)],
        [LOCAL] * 5,
        (attended, out_weight, w_other, *even_cot[:2]),
        gathered,
    )
    ended, wg_own, wg_other = seen(
        late_kernel,
        [
            projected,
            pltpu.VMEM(out_weight.shape, jnp.float32),
            jax.ShapeDtypeStruct(out_weight.shape, bf16),
        ],
        [LOCAL] * 6,
        (attended, out_weight, w_other, begun_wg, *even_cot[2:]),
        gathered,
    )
    wg_crossed = shift(wg_other, 1)
    mine = (wg_own + wg_crossed.astype(jnp.float32)).astype(bf16)

    def across(block, step):
        return lax.ppermute(block, "clip", [(i, i ^ step) for i in range(clips)])

    other = across(mine, 1)
    step = 3
    while step < clips:
        mine = (mine.astype(jnp.float32) + other.astype(jnp.float32)).astype(bf16)
        other = across(mine, step)
        step = 2 * step + 1
    shares = [mine, other]
    kept_query, kept_shared, leaving = seen(
        backward_kernel,
        [
            jax.ShapeDtypeStruct((4, MAXV, 128), bf16),
            jax.ShapeDtypeStruct((4, MAXV, 256), jnp.float32),
            jax.ShapeDtypeStruct((4, MAXV, 256), bf16),
        ],
        [LOCAL] * 6,
        (shared, query, weights, attended, begun, ended),
        [pltpu.VMEM((own_rows, 128), bf16)],
    )
    crossed = shift(leaving, 1)
    joined = seen(combine_kernel, [narrow] * 4, [LOCAL] * 3, (kept_query, kept_shared, crossed))
    home = [joined[0]] + [shift(joined[i], ROUTES[i]) for i in (1, 2, 3)]
    scale = (clips * VIS_DEV * pairs) ** (-0.5)
    return tuple(
        pl.pallas_call(
            functools.partial(unpack_kernel, scale),
            out_shape=[full] * 3 + [jax.ShapeDtypeStruct(out_weight.shape, jnp.float32)],
            in_specs=[LOCAL] * 7 + [ANYWHERE] * 3,
            out_specs=[ANYWHERE] * 4,
            scratch_shapes=[
                pltpu.VMEM((3, 2, MAXV, queries.shape[2]), bf16),
                pltpu.VMEM(out_weight.shape, jnp.float32),
                pltpu.SemaphoreType.DMA((7,)),
            ],
            input_output_aliases={7: 0, 8: 1, 9: 2},
            compiler_params=PARAMS,
            name="unpack",
        )(sides, *home, *shares, *blanks)
    )


def local(*arrays):
    if lax.axis_size("seq") == HEADS and lax.axis_size("clip") in (2, 4, 8, 16):
        return by_heads(*arrays)
    return by_rows(*arrays)


def solution(mesh):
    placed = (
        P("clip", "seq", None),
        P("clip", "seq", None),
        P("clip", "seq", None),
        P("clip", "seq", None),
        P("clip", None),
        P("clip", None),
        P("seq", None),
    )
    return jax.shard_map(
        local,
        mesh=mesh,
        in_specs=placed,
        out_specs=(
            P("clip", "seq", None),
            P("clip", "seq", None),
            P("clip", "seq", None),
            P("seq", None),
        ),
        check_vma=False,
    )
```

```python
import functools

import jax
import jax.numpy as jnp
from jax import lax
from jax.experimental import pallas as pl
from jax.experimental.pallas import tpu as pltpu
from jax.sharding import PartitionSpec as P


HEADS = 8
HD = 64
VIS_DEV = 48
MAXV = 96


def pick_entry(table, position):
    order = jnp.arange(table.shape[0], dtype=jnp.int32)
    chosen = jnp.where(order[None, :] == position[:, None], table[None, :], 0)
    return jnp.sum(chosen, axis=1)


def split_heads(block):
    return block.reshape(block.shape[0], HEADS, HD).transpose(1, 0, 2)


def join_heads(block):
    return block.transpose(1, 0, 2).reshape(block.shape[1], HEADS * HD)


def query_side(parts):
    query_head, key_head, value_head, dout_head = parts
    factor = HD ** (-0.5)
    scores = (
        lax.dot_general(
            query_head, key_head, (((1,), (1,)), ((), ())), preferred_element_type=jnp.float32
        )
        * factor
    )
    peak_score = jnp.max(scores, axis=1, keepdims=True)
    log_total = peak_score + jnp.log(jnp.sum(jnp.exp(scores - peak_score), axis=1, keepdims=True))
    weights = jnp.exp(scores - log_total)
    weights_low = weights.astype(jnp.bfloat16)
    attended = jnp.dot(weights_low, value_head, preferred_element_type=jnp.float32).astype(
        jnp.bfloat16
    )
    inner_sum = jnp.sum(
        dout_head.astype(jnp.float32) * attended.astype(jnp.float32), axis=1, keepdims=True
    )
    dweights = lax.dot_general(
        dout_head, value_head, (((1,), (1,)), ((), ())), preferred_element_type=jnp.float32
    )
    dscores = (weights * (dweights - inner_sum)).astype(jnp.bfloat16)
    grad_query = (jnp.dot(dscores, key_head, preferred_element_type=jnp.float32) * factor).astype(
        jnp.bfloat16
    )
    return (attended, grad_query, log_total[:, 0], inner_sum[:, 0])


def key_side_add(query_piece, dout_piece, log_piece, inner_piece, key_heads, value_heads):
    factor = HD ** (-0.5)

    def one_head(parts):
        query_head, dout_head, log_head, inner_head, key_head, value_head = parts
        scores = (
            lax.dot_general(
                query_head, key_head, (((1,), (1,)), ((), ())), preferred_element_type=jnp.float32
            )
            * factor
        )
        weights = jnp.exp(scores - log_head[:, None])
        weights_low = weights.astype(jnp.bfloat16)
        value_part = lax.dot_general(
            weights_low, dout_head, (((0,), (0,)), ((), ())), preferred_element_type=jnp.float32
        )
        dweights = lax.dot_general(
            dout_head, value_head, (((1,), (1,)), ((), ())), preferred_element_type=jnp.float32
        )
        dscores = (weights * (dweights - inner_head[:, None])).astype(jnp.bfloat16)
        key_part = lax.dot_general(
            dscores, query_head, (((0,), (0,)), ((), ())), preferred_element_type=jnp.float32
        )
        return (key_part, value_part)

    key_parts, value_parts = lax.map(
        one_head,
        (
            split_heads(query_piece),
            split_heads(dout_piece),
            log_piece.T,
            inner_piece.T,
            key_heads,
            value_heads,
        ),
    )
    return (key_parts, value_parts)


def by_rows(queries, keys, values, out_cotangent, visible_counts, span_offset, out_weight):
    devices = lax.axis_size("seq")
    device = lax.axis_index("seq")
    frames = queries.shape[1]
    visible_rows = VIS_DEV
    capacity = MAXV // devices
    counts = visible_counts[0]
    offsets = span_offset[0]
    shard_ends = jnp.cumsum(counts)
    starts = shard_ends - counts
    this_device = device.reshape(1)
    count_here = pick_entry(counts, this_device)[0]
    start_here = pick_entry(starts, this_device)[0]
    span_begin = pick_entry(offsets, this_device)[0] % (count_here + 1)
    masked = frames - count_here
    send_slots = jnp.arange(devices * capacity, dtype=jnp.int32)
    peer_index = send_slots // capacity
    within = send_slots % capacity
    first_slot = (start_here - peer_index + devices - 1) // devices
    global_index = (first_slot + within) * devices + peer_index
    ranked = global_index - start_here
    live_slot = ranked < count_here
    frame_of = jnp.clip(jnp.where(ranked < span_begin, ranked, ranked + masked), 0, frames - 1)

    def outgoing(block):
        return jnp.where(
            live_slot[:, None], jnp.take(block[0], frame_of, axis=0), jnp.zeros((), block.dtype)
        )

    arrived = (
        lax.all_to_all(outgoing(queries), "seq", split_axis=0, concat_axis=0, tiled=True),
        lax.all_to_all(outgoing(keys), "seq", split_axis=0, concat_axis=0, tiled=True),
        lax.all_to_all(outgoing(values), "seq", split_axis=0, concat_axis=0, tiled=True),
        lax.all_to_all(outgoing(out_cotangent), "seq", split_axis=0, concat_axis=0, tiled=True),
    )
    packed_slot = jnp.arange(visible_rows, dtype=jnp.int32)
    packed_index = packed_slot * devices + device
    owner_shard = jnp.sum((shard_ends[None, :] <= packed_index[:, None]).astype(jnp.int32), axis=1)
    owner_first = (pick_entry(starts, owner_shard) - device + devices - 1) // devices
    arrived_row = owner_shard * capacity + packed_slot - owner_first
    query_pack = jnp.take(arrived[0], arrived_row, axis=0)
    key_pack = jnp.take(arrived[1], arrived_row, axis=0)
    value_pack = jnp.take(arrived[2], arrived_row, axis=0)
    cotangent_pack = jnp.take(arrived[3], arrived_row, axis=0)
    output_grad = lax.dot_general(
        cotangent_pack,
        lax.all_gather(out_weight, "seq", axis=0, tiled=True),
        (((1,), (1,)), ((), ())),
        preferred_element_type=jnp.float32,
    ).astype(jnp.bfloat16)
    key_all, value_all = (
        lax.all_gather(key_pack, "seq", axis=0, tiled=True),
        lax.all_gather(value_pack, "seq", axis=0, tiled=True),
    )
    attended, query_grad, log_totals, inner_sums = lax.map(
        query_side,
        (
            split_heads(query_pack),
            split_heads(key_all),
            split_heads(value_all),
            split_heads(output_grad),
        ),
    )
    attended = join_heads(attended)
    query_grad = join_heads(query_grad)
    log_rows = log_totals.T
    inner_rows = inner_sums.T
    partial_term = lax.dot_general(
        attended, cotangent_pack, (((0,), (0,)), ((), ())), preferred_element_type=jnp.float32
    )
    seq_sum = lax.psum_scatter(
        partial_term.astype(jnp.bfloat16), "seq", scatter_dimension=0, tiled=True
    )
    clip_sum = lax.psum(seq_sum, "clip").astype(jnp.float32)
    weight_grad = clip_sum * (lax.axis_size("clip") * visible_rows * devices) ** (-0.5)
    log_every, inner_every = (
        lax.all_gather(log_rows, "seq", axis=0, tiled=True),
        lax.all_gather(inner_rows, "seq", axis=0, tiled=True),
    )
    key_heads = split_heads(key_pack)
    value_heads = split_heads(value_pack)
    key_sum, value_sum = key_side_add(
        lax.all_gather(query_pack, "seq", axis=0, tiled=True),
        lax.all_gather(output_grad, "seq", axis=0, tiled=True),
        log_every,
        inner_every,
        key_heads,
        value_heads,
    )
    key_grad = join_heads((key_sum * HD ** (-0.5)).astype(jnp.bfloat16))
    value_grad = join_heads(value_sum.astype(jnp.bfloat16))
    back_first = (pick_entry(starts, peer_index) - device + devices - 1) // devices
    back_slot = back_first + within
    back_live = back_slot * devices + device < pick_entry(shard_ends, peer_index)
    back_row = jnp.clip(back_slot, 0, visible_rows - 1)

    def returning(block):
        return jnp.where(
            back_live[:, None], jnp.take(block, back_row, axis=0), jnp.zeros((), block.dtype)
        )

    returned = (
        lax.all_to_all(returning(query_grad), "seq", split_axis=0, concat_axis=0, tiled=True),
        lax.all_to_all(returning(key_grad), "seq", split_axis=0, concat_axis=0, tiled=True),
        lax.all_to_all(returning(value_grad), "seq", split_axis=0, concat_axis=0, tiled=True),
    )
    position = jnp.arange(frames, dtype=jnp.int32)
    visible = (position < span_begin) | (position >= span_begin + masked)
    frame_rank = jnp.where(position < span_begin, position, position - masked)
    frame_global = start_here + frame_rank
    frame_peer = frame_global % devices
    frame_slot = frame_global // devices
    frame_first = (start_here - frame_peer + devices - 1) // devices
    frame_row = jnp.clip(
        frame_peer * capacity + frame_slot - frame_first, 0, devices * capacity - 1
    )

    def placed(block):
        return jnp.where(
            visible[:, None], jnp.take(block, frame_row, axis=0), jnp.zeros((), block.dtype)
        )[None]

    return (placed(returned[0]), placed(returned[1]), placed(returned[2]), weight_grad)


ROUTES = (0, 6, 4, 2)
FIRST = 128


def head_lanes(core):
    lane = lax.broadcasted_iota(jnp.int32, (1, 128), 1)
    return ((lane // HD) == core).astype(jnp.float32).astype(jnp.bfloat16)


def scalar_copies(sources, targets, sems):
    copies = [
        pltpu.make_async_copy(source, target, sems.at[index])
        for index, (source, target) in enumerate(zip(sources, targets))
    ]
    for copy in copies:
        copy.start()
    return copies


def span_of(counts_ref, offsets_ref, owner):
    count = counts_ref[0, owner]
    begin = lax.rem(offsets_ref[0, owner], count + 1)
    return begin, MAXV - (count - begin)


def slot_masks(begin, end_start):
    slot = lax.broadcasted_iota(jnp.int32, (MAXV, 1), 0)
    early = (slot < begin).astype(jnp.float32).astype(jnp.bfloat16)
    late = (slot >= end_start).astype(jnp.float32).astype(jnp.bfloat16)
    return early, late


def pack_kernel(counts_hbm, offsets_hbm, q_ref, k_ref, v_ref, g_ref, *rest):
    sends, cot_ref, sides_ref = rest[:4], rest[4], rest[5]
    narrow, wide, counts_ref, offsets_ref, sems, scalar_sems = rest[6:]
    scalars = scalar_copies((counts_hbm, offsets_hbm), (counts_ref, offsets_ref), scalar_sems)
    frames = q_ref.shape[1]
    last = frames - MAXV
    device = lax.axis_index("seq")
    copies = []
    for index, source in enumerate((q_ref, k_ref, v_ref)):
        for side, start in enumerate((0, last)):
            copies.append(
                pltpu.make_async_copy(
                    source.at[0, pl.ds(start, MAXV)], narrow.at[index, side], sems.at[len(copies)]
                )
            )
    for side, start in enumerate((0, last)):
        copies.append(
            pltpu.make_async_copy(
                g_ref.at[0, pl.ds(start, MAXV)], wide.at[side], sems.at[len(copies)]
            )
        )
    for copy in copies:
        copy.start()
    for copy in scalars:
        copy.wait()
    begin, end_start = span_of(counts_ref, offsets_ref, device)
    early, late = slot_masks(begin, end_start)
    for copy in copies[:6]:
        copy.wait()
    for route, send in zip(ROUTES, sends):
        chip = (device ^ route) // 2
        lanes = pl.ds(pl.multiple_of(chip * 128, 128), 128)
        for index in range(3):
            send[:, index * 128 : (index + 1) * 128] = (
                narrow[index, 0, :, lanes] * early + narrow[index, 1, :, lanes] * late
            )
    for copy in copies[6:]:
        copy.wait()
    cot_ref[...] = wide[0] * early + wide[1] * late
    for side, mask in enumerate((early, late)):
        sides_ref[side] = jnp.broadcast_to(mask, (MAXV, 128))


def tables_kernel(counts_hbm, offsets_hbm, bias_ref, *rest):
    outs, (blank, counts_ref, offsets_ref, sems, scalar_sems) = rest[:3], rest[3:]
    scalars = scalar_copies((counts_hbm, offsets_hbm), (counts_ref, offsets_ref), scalar_sems)
    blank[...] = jnp.zeros_like(blank)
    copies = [
        pltpu.make_async_copy(blank, out.at[0, pl.ds(MAXV, blank.shape[0])], sems.at[index])
        for index, out in enumerate(outs)
    ]
    for copy in copies:
        copy.start()
    device = lax.axis_index("seq")
    for copy in scalars:
        copy.wait()
    slot = lax.broadcasted_iota(jnp.int32, (MAXV, 128), 0)
    for index in range(8):
        owner = device ^ (ROUTES[index // 2] + index % 2)
        begin, end_start = span_of(counts_ref, offsets_ref, owner)
        dead = (slot >= begin) & (slot < end_start)
        bias_ref[index * MAXV : (index + 1) * MAXV, :] = jnp.where(dead, -1e30, 0.0)
    for copy in copies:
        copy.wait()


def forward_kernel(bias_ref, *rest):
    blocks = rest[:8]
    shared, query, first_ref, second_ref, attended_ref = rest[8:]
    for index in range(8):
        shared[index * MAXV : (index + 1) * MAXV, :] = blocks[index][:, 128:384]
    for index in range(4):
        query[index * MAXV : (index + 1) * MAXV, :] = blocks[2 * index][:, 0:128]
    bias = bias_ref[...]
    bias = jnp.concatenate([bias, bias, bias], axis=1)
    factor = HD ** (-0.5)
    value_t = shared[:, 128:256].T
    for head in range(2):
        key = shared[:, 0:128] * head_lanes(head)
        scores = (
            lax.dot_general(
                key, query[...], (((1,), (1,)), ((), ())), preferred_element_type=jnp.float32
            )
            * factor
        )
        scores = scores + bias
        scores = jnp.exp(scores - jnp.max(scores, axis=0, keepdims=True))
        weights = scores * (1.0 / jnp.sum(scores, axis=0, keepdims=True))
        first_ref[head] = weights[:, :FIRST]
        second_ref[head] = weights[:, FIRST:]
        own = slice(head * HD, (head + 1) * HD)
        attended_ref[own, :] = jnp.dot(
            value_t, weights.astype(jnp.bfloat16), preferred_element_type=jnp.float32
        )[own].astype(jnp.bfloat16)


def gather_cots(cots, cot):
    for index, block in enumerate(cots):
        cot[index * MAXV : (index + 1) * MAXV, :] = block[...]


def project(cot, w_ref, w_other_ref, core):
    first = (core == 0).astype(jnp.float32).astype(jnp.bfloat16)
    second = (core == 1).astype(jnp.float32).astype(jnp.bfloat16)
    top = w_ref[...] * first + w_other_ref[...] * second
    bottom = w_ref[...] * second + w_other_ref[...] * first
    return lax.dot_general(
        cot[...],
        jnp.concatenate([top, bottom], axis=0),
        (((1,), (1,)), ((), ())),
        preferred_element_type=jnp.float32,
    ).astype(jnp.bfloat16)


def early_kernel(attended_ref, w_ref, w_other_ref, *rest):
    cots, dout_ref, wg_ref, cot = rest[:2], rest[2], rest[3], rest[4]
    gather_cots(cots, cot)
    dout_ref[...] = project(cot, w_ref, w_other_ref, lax.axis_index("seq") % 2)
    wg_ref[...] = jnp.dot(
        attended_ref[:, : 2 * MAXV], cot[...], preferred_element_type=jnp.float32
    )


def late_kernel(attended_ref, w_ref, w_other_ref, begun_ref, *rest):
    cots, dout_ref, own_ref, other_ref, cot = rest[:2], rest[2], rest[3], rest[4], rest[5]
    core = lax.axis_index("seq") % 2
    gather_cots(cots, cot)
    total = begun_ref[...] + jnp.dot(
        attended_ref[:, 2 * MAXV :], cot[...], preferred_element_type=jnp.float32
    )
    own_ref[...] = jnp.where(core == 0, total[:HD], total[HD:])
    other_ref[...] = jnp.where(core == 0, total[HD:], total[:HD]).astype(jnp.bfloat16)
    dout_ref[...] = project(cot, w_ref, w_other_ref, core)


def pass_over(queries, shared, query, weights_ref, attended_ref, dout):
    products = dout.astype(jnp.float32).T * attended_ref[:, queries].astype(jnp.float32)
    own_query = query[queries, :]
    value = shared[:, 128:256]
    key_grad, value_grad, query_grad = [], [], []
    for head in range(2):
        lanes = head_lanes(head)
        dout_own = dout * lanes
        key_t = (shared[:, 0:128] * lanes).T
        inner = jnp.sum(products[head * HD : (head + 1) * HD], axis=0, keepdims=True)
        weights = weights_ref[head]
        dweights = lax.dot_general(
            value, dout_own, (((1,), (1,)), ((), ())), preferred_element_type=jnp.float32
        )
        dscores = (weights * (dweights - inner)).astype(jnp.bfloat16)
        value_grad.append(
            jnp.dot(weights.astype(jnp.bfloat16), dout_own, preferred_element_type=jnp.float32)
        )
        key_grad.append(
            jnp.dot(dscores, own_query * lanes, preferred_element_type=jnp.float32)
        )
        query_grad.append(jnp.dot(key_t, dscores, preferred_element_type=jnp.float32))
    query_grad = (sum(query_grad) * HD ** (-0.5)).T.astype(jnp.bfloat16)
    return query_grad, sum(key_grad), sum(value_grad)


def backward_first_kernel(shared, query, weights_ref, attended_ref, dout_ref, *outs):
    results = pass_over(
        slice(0, FIRST), shared, query, weights_ref, attended_ref, dout_ref[:FIRST, :]
    )
    for out, result in zip(outs, results):
        out[...] = result


def backward_kernel(shared, query, weights_ref, attended_ref, begun_ref, ended_ref, *rest):
    begun_query, begun_key, begun_value, kept_query, kept_shared, leaving, dout, dq = rest
    split = 2 * MAXV - FIRST
    dout[:split, :] = begun_ref[FIRST:, :]
    dout[split:, :] = ended_ref[...]
    query_grad, key_grad, value_grad = pass_over(
        slice(FIRST, 4 * MAXV), shared, query, weights_ref, attended_ref, dout[...]
    )
    dq[:FIRST, :] = begun_query[...]
    dq[FIRST:, :] = query_grad
    key_grad = (begun_key[...] + key_grad) * HD ** (-0.5)
    value_grad = begun_value[...] + value_grad
    for index in range(4):
        kept_query[index] = dq[index * MAXV : (index + 1) * MAXV, :]
        rows = slice(2 * index * MAXV, (2 * index + 1) * MAXV)
        kept_shared[index, :, 0:128] = key_grad[rows]
        kept_shared[index, :, 128:256] = value_grad[rows]
        rows = slice((2 * index + 1) * MAXV, (2 * index + 2) * MAXV)
        leaving[index, :, 0:128] = key_grad[rows].astype(jnp.bfloat16)
        leaving[index, :, 128:256] = value_grad[rows].astype(jnp.bfloat16)


def combine_kernel(kept_query, kept_shared, crossed, *outs):
    for index in range(4):
        outs[index][:, 0:128] = kept_query[index]
        outs[index][:, 128:384] = (
            kept_shared[index] + crossed[index].astype(jnp.float32)
        ).astype(jnp.bfloat16)


def unpack_kernel(scale, sides_ref, *rest):
    blocks, shares, outs, wg_hbm = rest[:4], rest[4:6], rest[9:12], rest[12]
    edges, wg_ref, sems = rest[13:]
    device = lax.axis_index("seq")
    last = outs[0].shape[1] - MAXV
    copies = []
    for index in range(3):
        for route, block in zip(ROUTES, blocks):
            chip = (device ^ route) // 2
            lanes = pl.ds(pl.multiple_of(chip * 128, 128), 128)
            piece = block[:, index * 128 : (index + 1) * 128]
            for side in range(2):
                edges[index, side, :, lanes] = piece * sides_ref[side]
        for side, start in enumerate((0, last)):
            copies.append(
                pltpu.make_async_copy(
                    edges.at[index, side],
                    outs[index].at[0, pl.ds(start, MAXV)],
                    sems.at[len(copies)],
                )
            )
            copies[-1].start()
    wg_ref[...] = (shares[0][...].astype(jnp.float32) + shares[1][...].astype(jnp.float32)) * scale
    copies.append(pltpu.make_async_copy(wg_ref, wg_hbm, sems.at[len(copies)]))
    copies[-1].start()
    for copy in copies:
        copy.wait()


PARAMS = pltpu.CompilerParams(vmem_limit_bytes=24 << 20)
ANYWHERE = pl.BlockSpec(memory_space=pl.ANY)
SCALARS = pl.BlockSpec(memory_space=pltpu.SMEM)
LOCAL = pl.BlockSpec(memory_space=pltpu.VMEM)


def in_hbm(block):
    return pltpu.with_memory_space_constraint(block, pltpu.HBM)


def by_heads(queries, keys, values, out_cotangent, visible_counts, span_offset, out_weight):
    bf16 = jnp.bfloat16
    pairs = lax.axis_size("seq")
    clips = lax.axis_size("clip")

    def shift(block, step):
        return lax.ppermute(block, "seq", [(i, i ^ step) for i in range(pairs)])

    narrow = jax.ShapeDtypeStruct((MAXV, 384), bf16)
    wide = jax.ShapeDtypeStruct((MAXV, out_cotangent.shape[2]), bf16)

    def seen(kernel, outs, specs, operands, scratch=(), out_specs=None):
        return pl.pallas_call(
            kernel,
            out_shape=outs,
            in_specs=specs,
            out_specs=out_specs or [LOCAL] * len(outs),
            scratch_shapes=scratch,
            compiler_params=PARAMS,
        )(*operands)

    width = out_cotangent.shape[2]
    rows = 8 * MAXV
    counts, offsets = in_hbm(visible_counts), in_hbm(span_offset)
    table = pltpu.SMEM(visible_counts.shape, jnp.int32)
    tables = [table, table]
    pair_sems = pltpu.SemaphoreType.DMA((2,))
    *sends, cot, sides = seen(
        pack_kernel,
        [narrow] * 4 + [wide, pltpu.VMEM((2, MAXV, 128), bf16)],
        [ANYWHERE] * 6,
        (counts, offsets, *map(in_hbm, (queries, keys, values, out_cotangent))),
        [
            pltpu.VMEM((3, 2, MAXV, queries.shape[2]), bf16),
            pltpu.VMEM((2, MAXV, width), bf16),
            *tables,
            pltpu.SemaphoreType.DMA((8,)),
            pair_sems,
        ],
    )
    even = [sends[0]] + [shift(sends[i], ROUTES[i]) for i in (1, 2, 3)]
    even_cot = [cot] + [shift(cot, ROUTES[i]) for i in (1, 2, 3)]
    odd = [shift(block, 1) for block in even]
    w_other = shift(out_weight, 1)
    blocks = [block for pair in zip(even, odd) for block in pair]
    full = jax.ShapeDtypeStruct(queries.shape, bf16)
    bias, *blanks = seen(
        tables_kernel,
        [pltpu.VMEM((rows, 128), jnp.float32)] + [full] * 3,
        [ANYWHERE] * 2,
        (counts, offsets),
        [
            pltpu.VMEM((queries.shape[1] - 2 * MAXV, queries.shape[2]), bf16),
            *tables,
            pltpu.SemaphoreType.DMA((3,)),
            pair_sems,
        ],
        [LOCAL] + [ANYWHERE] * 3,
    )
    own_rows = 4 * MAXV
    shared, query, first, second, attended = seen(
        forward_kernel,
        [
            pltpu.VMEM((rows, 256), bf16),
            pltpu.VMEM((own_rows, 128), bf16),
            pltpu.VMEM((2, rows, FIRST), jnp.float32),
            pltpu.VMEM((2, rows, own_rows - FIRST), jnp.float32),
            pltpu.VMEM((128, own_rows), bf16),
        ],
        [LOCAL] * 9,
        (bias, *blocks),
    )
    projected = pltpu.VMEM((2 * MAXV, 128), bf16)
    gathered = [pltpu.VMEM((2 * MAXV, width), bf16)]
    begun, begun_wg = seen(
        early_kernel,
        [projected, pltpu.VMEM((128, width), jnp.float32)],
        [LOCAL] * 5,
        (attended, out_weight, w_other, *even_cot[:2]),
        gathered,
    )
    partial = seen(
        backward_first_kernel,
        [
            pltpu.VMEM((FIRST, 128), bf16),
            pltpu.VMEM((rows, 128), jnp.float32),
            pltpu.VMEM((rows, 128), jnp.float32),
        ],
        [LOCAL] * 5,
        (shared, query, first, attended, begun),
    )
    ended, wg_own, wg_other = seen(
        late_kernel,
        [
            projected,
            pltpu.VMEM(out_weight.shape, jnp.float32),
            jax.ShapeDtypeStruct(out_weight.shape, bf16),
        ],
        [LOCAL] * 6,
        (attended, out_weight, w_other, begun_wg, *even_cot[2:]),
        gathered,
    )
    wg_crossed = shift(wg_other, 1)
    mine = (wg_own + wg_crossed.astype(jnp.float32)).astype(bf16)

    def across(block, step):
        return lax.ppermute(block, "clip", [(i, i ^ step) for i in range(clips)])

    other = across(mine, 1)
    step = 3
    while step < clips:
        mine = (mine.astype(jnp.float32) + other.astype(jnp.float32)).astype(bf16)
        other = across(mine, step)
        step = 2 * step + 1
    shares = [mine, other]
    kept_query, kept_shared, leaving = seen(
        backward_kernel,
        [
            jax.ShapeDtypeStruct((4, MAXV, 128), bf16),
            jax.ShapeDtypeStruct((4, MAXV, 256), jnp.float32),
            jax.ShapeDtypeStruct((4, MAXV, 256), bf16),
        ],
        [LOCAL] * 9,
        (shared, query, second, attended, begun, ended, *partial),
        [pltpu.VMEM((own_rows - FIRST, 128), bf16), pltpu.VMEM((own_rows, 128), bf16)],
    )
    crossed = shift(leaving, 1)
    joined = seen(combine_kernel, [narrow] * 4, [LOCAL] * 3, (kept_query, kept_shared, crossed))
    home = [joined[0]] + [shift(joined[i], ROUTES[i]) for i in (1, 2, 3)]
    scale = (clips * VIS_DEV * pairs) ** (-0.5)
    return tuple(
        pl.pallas_call(
            functools.partial(unpack_kernel, scale),
            out_shape=[full] * 3 + [jax.ShapeDtypeStruct(out_weight.shape, jnp.float32)],
            in_specs=[LOCAL] * 7 + [ANYWHERE] * 3,
            out_specs=[ANYWHERE] * 4,
            scratch_shapes=[
                pltpu.VMEM((3, 2, MAXV, queries.shape[2]), bf16),
                pltpu.VMEM(out_weight.shape, jnp.float32),
                pltpu.SemaphoreType.DMA((7,)),
            ],
            input_output_aliases={7: 0, 8: 1, 9: 2},
            compiler_params=PARAMS,
            name="unpack",
        )(sides, *home, *shares, *blanks)
    )


def local(*arrays):
    if lax.axis_size("seq") == HEADS and lax.axis_size("clip") in (2, 4, 8, 16):
        return by_heads(*arrays)
    return by_rows(*arrays)


def solution(mesh):
    placed = (
        P("clip", "seq", None),
        P("clip", "seq", None),
        P("clip", "seq", None),
        P("clip", "seq", None),
        P("clip", None),
        P("clip", None),
        P("seq", None),
    )
    return jax.shard_map(
        local,
        mesh=mesh,
        in_specs=placed,
        out_specs=(
            P("clip", "seq", None),
            P("clip", "seq", None),
            P("clip", "seq", None),
            P("seq", None),
        ),
        check_vma=False,
    )
```

```python
import functools

import jax
import jax.numpy as jnp
from jax import lax
from jax.experimental import pallas as pl
from jax.experimental.pallas import tpu as pltpu
from jax.sharding import PartitionSpec as P


HEADS = 8
HD = 64
VIS_DEV = 48
MAXV = 96


def pick_entry(table, position):
    order = jnp.arange(table.shape[0], dtype=jnp.int32)
    chosen = jnp.where(order[None, :] == position[:, None], table[None, :], 0)
    return jnp.sum(chosen, axis=1)


def split_heads(block):
    return block.reshape(block.shape[0], HEADS, HD).transpose(1, 0, 2)


def join_heads(block):
    return block.transpose(1, 0, 2).reshape(block.shape[1], HEADS * HD)


def query_side(parts):
    query_head, key_head, value_head, dout_head = parts
    factor = HD ** (-0.5)
    scores = (
        lax.dot_general(
            query_head, key_head, (((1,), (1,)), ((), ())), preferred_element_type=jnp.float32
        )
        * factor
    )
    peak_score = jnp.max(scores, axis=1, keepdims=True)
    log_total = peak_score + jnp.log(jnp.sum(jnp.exp(scores - peak_score), axis=1, keepdims=True))
    weights = jnp.exp(scores - log_total)
    weights_low = weights.astype(jnp.bfloat16)
    attended = jnp.dot(weights_low, value_head, preferred_element_type=jnp.float32).astype(
        jnp.bfloat16
    )
    inner_sum = jnp.sum(
        dout_head.astype(jnp.float32) * attended.astype(jnp.float32), axis=1, keepdims=True
    )
    dweights = lax.dot_general(
        dout_head, value_head, (((1,), (1,)), ((), ())), preferred_element_type=jnp.float32
    )
    dscores = (weights * (dweights - inner_sum)).astype(jnp.bfloat16)
    grad_query = (jnp.dot(dscores, key_head, preferred_element_type=jnp.float32) * factor).astype(
        jnp.bfloat16
    )
    return (attended, grad_query, log_total[:, 0], inner_sum[:, 0])


def key_side_add(query_piece, dout_piece, log_piece, inner_piece, key_heads, value_heads):
    factor = HD ** (-0.5)

    def one_head(parts):
        query_head, dout_head, log_head, inner_head, key_head, value_head = parts
        scores = (
            lax.dot_general(
                query_head, key_head, (((1,), (1,)), ((), ())), preferred_element_type=jnp.float32
            )
            * factor
        )
        weights = jnp.exp(scores - log_head[:, None])
        weights_low = weights.astype(jnp.bfloat16)
        value_part = lax.dot_general(
            weights_low, dout_head, (((0,), (0,)), ((), ())), preferred_element_type=jnp.float32
        )
        dweights = lax.dot_general(
            dout_head, value_head, (((1,), (1,)), ((), ())), preferred_element_type=jnp.float32
        )
        dscores = (weights * (dweights - inner_head[:, None])).astype(jnp.bfloat16)
        key_part = lax.dot_general(
            dscores, query_head, (((0,), (0,)), ((), ())), preferred_element_type=jnp.float32
        )
        return (key_part, value_part)

    key_parts, value_parts = lax.map(
        one_head,
        (
            split_heads(query_piece),
            split_heads(dout_piece),
            log_piece.T,
            inner_piece.T,
            key_heads,
            value_heads,
        ),
    )
    return (key_parts, value_parts)


def by_rows(queries, keys, values, out_cotangent, visible_counts, span_offset, out_weight):
    devices = lax.axis_size("seq")
    device = lax.axis_index("seq")
    frames = queries.shape[1]
    visible_rows = VIS_DEV
    capacity = MAXV // devices
    counts = visible_counts[0]
    offsets = span_offset[0]
    shard_ends = jnp.cumsum(counts)
    starts = shard_ends - counts
    this_device = device.reshape(1)
    count_here = pick_entry(counts, this_device)[0]
    start_here = pick_entry(starts, this_device)[0]
    span_begin = pick_entry(offsets, this_device)[0] % (count_here + 1)
    masked = frames - count_here
    send_slots = jnp.arange(devices * capacity, dtype=jnp.int32)
    peer_index = send_slots // capacity
    within = send_slots % capacity
    first_slot = (start_here - peer_index + devices - 1) // devices
    global_index = (first_slot + within) * devices + peer_index
    ranked = global_index - start_here
    live_slot = ranked < count_here
    frame_of = jnp.clip(jnp.where(ranked < span_begin, ranked, ranked + masked), 0, frames - 1)

    def outgoing(block):
        return jnp.where(
            live_slot[:, None], jnp.take(block[0], frame_of, axis=0), jnp.zeros((), block.dtype)
        )

    arrived = (
        lax.all_to_all(outgoing(queries), "seq", split_axis=0, concat_axis=0, tiled=True),
        lax.all_to_all(outgoing(keys), "seq", split_axis=0, concat_axis=0, tiled=True),
        lax.all_to_all(outgoing(values), "seq", split_axis=0, concat_axis=0, tiled=True),
        lax.all_to_all(outgoing(out_cotangent), "seq", split_axis=0, concat_axis=0, tiled=True),
    )
    packed_slot = jnp.arange(visible_rows, dtype=jnp.int32)
    packed_index = packed_slot * devices + device
    owner_shard = jnp.sum((shard_ends[None, :] <= packed_index[:, None]).astype(jnp.int32), axis=1)
    owner_first = (pick_entry(starts, owner_shard) - device + devices - 1) // devices
    arrived_row = owner_shard * capacity + packed_slot - owner_first
    query_pack = jnp.take(arrived[0], arrived_row, axis=0)
    key_pack = jnp.take(arrived[1], arrived_row, axis=0)
    value_pack = jnp.take(arrived[2], arrived_row, axis=0)
    cotangent_pack = jnp.take(arrived[3], arrived_row, axis=0)
    output_grad = lax.dot_general(
        cotangent_pack,
        lax.all_gather(out_weight, "seq", axis=0, tiled=True),
        (((1,), (1,)), ((), ())),
        preferred_element_type=jnp.float32,
    ).astype(jnp.bfloat16)
    key_all, value_all = (
        lax.all_gather(key_pack, "seq", axis=0, tiled=True),
        lax.all_gather(value_pack, "seq", axis=0, tiled=True),
    )
    attended, query_grad, log_totals, inner_sums = lax.map(
        query_side,
        (
            split_heads(query_pack),
            split_heads(key_all),
            split_heads(value_all),
            split_heads(output_grad),
        ),
    )
    attended = join_heads(attended)
    query_grad = join_heads(query_grad)
    log_rows = log_totals.T
    inner_rows = inner_sums.T
    partial_term = lax.dot_general(
        attended, cotangent_pack, (((0,), (0,)), ((), ())), preferred_element_type=jnp.float32
    )
    seq_sum = lax.psum_scatter(
        partial_term.astype(jnp.bfloat16), "seq", scatter_dimension=0, tiled=True
    )
    clip_sum = lax.psum(seq_sum, "clip").astype(jnp.float32)
    weight_grad = clip_sum * (lax.axis_size("clip") * visible_rows * devices) ** (-0.5)
    log_every, inner_every = (
        lax.all_gather(log_rows, "seq", axis=0, tiled=True),
        lax.all_gather(inner_rows, "seq", axis=0, tiled=True),
    )
    key_heads = split_heads(key_pack)
    value_heads = split_heads(value_pack)
    key_sum, value_sum = key_side_add(
        lax.all_gather(query_pack, "seq", axis=0, tiled=True),
        lax.all_gather(output_grad, "seq", axis=0, tiled=True),
        log_every,
        inner_every,
        key_heads,
        value_heads,
    )
    key_grad = join_heads((key_sum * HD ** (-0.5)).astype(jnp.bfloat16))
    value_grad = join_heads(value_sum.astype(jnp.bfloat16))
    back_first = (pick_entry(starts, peer_index) - device + devices - 1) // devices
    back_slot = back_first + within
    back_live = back_slot * devices + device < pick_entry(shard_ends, peer_index)
    back_row = jnp.clip(back_slot, 0, visible_rows - 1)

    def returning(block):
        return jnp.where(
            back_live[:, None], jnp.take(block, back_row, axis=0), jnp.zeros((), block.dtype)
        )

    returned = (
        lax.all_to_all(returning(query_grad), "seq", split_axis=0, concat_axis=0, tiled=True),
        lax.all_to_all(returning(key_grad), "seq", split_axis=0, concat_axis=0, tiled=True),
        lax.all_to_all(returning(value_grad), "seq", split_axis=0, concat_axis=0, tiled=True),
    )
    position = jnp.arange(frames, dtype=jnp.int32)
    visible = (position < span_begin) | (position >= span_begin + masked)
    frame_rank = jnp.where(position < span_begin, position, position - masked)
    frame_global = start_here + frame_rank
    frame_peer = frame_global % devices
    frame_slot = frame_global // devices
    frame_first = (start_here - frame_peer + devices - 1) // devices
    frame_row = jnp.clip(
        frame_peer * capacity + frame_slot - frame_first, 0, devices * capacity - 1
    )

    def placed(block):
        return jnp.where(
            visible[:, None], jnp.take(block, frame_row, axis=0), jnp.zeros((), block.dtype)
        )[None]

    return (placed(returned[0]), placed(returned[1]), placed(returned[2]), weight_grad)


ROUTES = (0, 6, 4, 2)
FIRST = 128


def head_lanes(core):
    lane = lax.broadcasted_iota(jnp.int32, (1, 128), 1)
    return ((lane // HD) == core).astype(jnp.float32).astype(jnp.bfloat16)


def scalar_copies(sources, targets, sems):
    copies = [
        pltpu.make_async_copy(source, target, sems.at[index])
        for index, (source, target) in enumerate(zip(sources, targets))
    ]
    for copy in copies:
        copy.start()
    return copies


def span_of(counts_ref, offsets_ref, owner):
    count = counts_ref[0, owner]
    begin = lax.rem(offsets_ref[0, owner], count + 1)
    return begin, MAXV - (count - begin)


def slot_masks(begin, end_start):
    slot = lax.broadcasted_iota(jnp.int32, (MAXV, 1), 0)
    early = (slot < begin).astype(jnp.float32).astype(jnp.bfloat16)
    late = (slot >= end_start).astype(jnp.float32).astype(jnp.bfloat16)
    return early, late


def pack_kernel(counts_hbm, offsets_hbm, q_ref, k_ref, v_ref, g_ref, *rest):
    sends, cot_ref, sides_ref = rest[:4], rest[4], rest[5]
    narrow, wide, counts_ref, offsets_ref, sems, scalar_sems = rest[6:]
    scalars = scalar_copies((counts_hbm, offsets_hbm), (counts_ref, offsets_ref), scalar_sems)
    frames = q_ref.shape[1]
    last = frames - MAXV
    device = lax.axis_index("seq")
    copies = []
    for index, source in enumerate((q_ref, k_ref, v_ref)):
        for side, start in enumerate((0, last)):
            copies.append(
                pltpu.make_async_copy(
                    source.at[0, pl.ds(start, MAXV)], narrow.at[index, side], sems.at[len(copies)]
                )
            )
    for side, start in enumerate((0, last)):
        copies.append(
            pltpu.make_async_copy(
                g_ref.at[0, pl.ds(start, MAXV)], wide.at[side], sems.at[len(copies)]
            )
        )
    for copy in copies:
        copy.start()
    for copy in scalars:
        copy.wait()
    begin, end_start = span_of(counts_ref, offsets_ref, device)
    early, late = slot_masks(begin, end_start)
    for copy in copies[:6]:
        copy.wait()
    for route, send in zip(ROUTES, sends):
        chip = (device ^ route) // 2
        lanes = pl.ds(pl.multiple_of(chip * 128, 128), 128)
        for index in range(3):
            send[:, index * 128 : (index + 1) * 128] = (
                narrow[index, 0, :, lanes] * early + narrow[index, 1, :, lanes] * late
            )
    for copy in copies[6:]:
        copy.wait()
    cot_ref[...] = wide[0] * early + wide[1] * late
    for side, mask in enumerate((early, late)):
        sides_ref[side] = jnp.broadcast_to(mask, (MAXV, 128))


def tables_kernel(counts_hbm, offsets_hbm, bias_ref, *rest):
    outs, (blank, counts_ref, offsets_ref, sems, scalar_sems) = rest[:3], rest[3:]
    scalars = scalar_copies((counts_hbm, offsets_hbm), (counts_ref, offsets_ref), scalar_sems)
    blank[...] = jnp.zeros_like(blank)
    copies = [
        pltpu.make_async_copy(blank, out.at[0, pl.ds(MAXV, blank.shape[0])], sems.at[index])
        for index, out in enumerate(outs)
    ]
    for copy in copies:
        copy.start()
    device = lax.axis_index("seq")
    for copy in scalars:
        copy.wait()
    slot = lax.broadcasted_iota(jnp.int32, (MAXV, 128), 0)
    for index in range(8):
        owner = device ^ (ROUTES[index // 2] + index % 2)
        begin, end_start = span_of(counts_ref, offsets_ref, owner)
        dead = (slot >= begin) & (slot < end_start)
        bias_ref[index * MAXV : (index + 1) * MAXV, :] = jnp.where(dead, -1e30, 0.0)
    for copy in copies:
        copy.wait()


def forward_kernel(bias_ref, *rest):
    blocks = rest[:8]
    shared, query, first_ref, second_ref, attended_ref = rest[8:]
    for index in range(8):
        shared[index * MAXV : (index + 1) * MAXV, :] = blocks[index][:, 128:384]
    for index in range(4):
        query[index * MAXV : (index + 1) * MAXV, :] = blocks[2 * index][:, 0:128]
    bias = bias_ref[...]
    bias = jnp.concatenate([bias, bias, bias], axis=1)
    factor = HD ** (-0.5)
    value_t = shared[:, 128:256].T
    for head in range(2):
        key = shared[:, 0:128] * head_lanes(head)
        scores = (
            lax.dot_general(
                key, query[...], (((1,), (1,)), ((), ())), preferred_element_type=jnp.float32
            )
            * factor
        )
        scores = scores + bias
        scores = jnp.exp(scores - jnp.max(scores, axis=0, keepdims=True))
        weights = scores * (1.0 / jnp.sum(scores, axis=0, keepdims=True))
        first_ref[head] = weights[:, :FIRST]
        second_ref[head] = weights[:, FIRST:]
        own = slice(head * HD, (head + 1) * HD)
        attended_ref[own, :] = jnp.dot(
            value_t, weights.astype(jnp.bfloat16), preferred_element_type=jnp.float32
        )[own].astype(jnp.bfloat16)


def gather_cots(cots, cot):
    for index, block in enumerate(cots):
        cot[index * MAXV : (index + 1) * MAXV, :] = block[...]


def project(cot, w_ref, w_other_ref, core):
    first = (core == 0).astype(jnp.float32).astype(jnp.bfloat16)
    second = (core == 1).astype(jnp.float32).astype(jnp.bfloat16)
    top = w_ref[...] * first + w_other_ref[...] * second
    bottom = w_ref[...] * second + w_other_ref[...] * first
    return lax.dot_general(
        cot[...],
        jnp.concatenate([top, bottom], axis=0),
        (((1,), (1,)), ((), ())),
        preferred_element_type=jnp.float32,
    ).astype(jnp.bfloat16)


def early_kernel(attended_ref, w_ref, w_other_ref, *rest):
    cots, dout_ref, wg_ref, cot = rest[:2], rest[2], rest[3], rest[4]
    gather_cots(cots, cot)
    dout_ref[...] = project(cot, w_ref, w_other_ref, lax.axis_index("seq") % 2)
    wg_ref[...] = jnp.dot(
        attended_ref[:, : 2 * MAXV], cot[...], preferred_element_type=jnp.float32
    )


def late_kernel(attended_ref, w_ref, w_other_ref, begun_ref, *rest):
    cots, dout_ref, own_ref, other_ref, cot = rest[:2], rest[2], rest[3], rest[4], rest[5]
    core = lax.axis_index("seq") % 2
    gather_cots(cots, cot)
    total = begun_ref[...] + jnp.dot(
        attended_ref[:, 2 * MAXV :], cot[...], preferred_element_type=jnp.float32
    )
    own_ref[...] = jnp.where(core == 0, total[:HD], total[HD:])
    other_ref[...] = jnp.where(core == 0, total[HD:], total[:HD]).astype(jnp.bfloat16)
    dout_ref[...] = project(cot, w_ref, w_other_ref, core)


def pass_over(queries, shared, query, weights_ref, attended_ref, dout):
    products = dout.astype(jnp.float32).T * attended_ref[:, queries].astype(jnp.float32)
    own_query = query[queries, :]
    value = shared[:, 128:256]
    key_grad, value_grad, query_grad = [], [], []
    for head in range(2):
        lanes = head_lanes(head)
        dout_own = dout * lanes
        key_t = (shared[:, 0:128] * lanes).T
        inner = jnp.sum(products[head * HD : (head + 1) * HD], axis=0, keepdims=True)
        weights = weights_ref[head]
        dweights = lax.dot_general(
            value, dout_own, (((1,), (1,)), ((), ())), preferred_element_type=jnp.float32
        )
        dscores = (weights * (dweights - inner)).astype(jnp.bfloat16)
        value_grad.append(
            jnp.dot(weights.astype(jnp.bfloat16), dout_own, preferred_element_type=jnp.float32)
        )
        key_grad.append(
            jnp.dot(dscores, own_query * lanes, preferred_element_type=jnp.float32)
        )
        query_grad.append(jnp.dot(key_t, dscores, preferred_element_type=jnp.float32))
    query_grad = (sum(query_grad) * HD ** (-0.5)).T.astype(jnp.bfloat16)
    return query_grad, sum(key_grad), sum(value_grad)


def backward_first_kernel(shared, query, weights_ref, attended_ref, dout_ref, *outs):
    results = pass_over(
        slice(0, FIRST), shared, query, weights_ref, attended_ref, dout_ref[:FIRST, :]
    )
    for out, result in zip(outs, results):
        out[...] = result


def backward_kernel(shared, query, weights_ref, attended_ref, begun_ref, ended_ref, *rest):
    begun_query, begun_key, begun_value, kept_query, kept_shared, leaving, dout, dq = rest
    split = 2 * MAXV - FIRST
    dout[:split, :] = begun_ref[FIRST:, :]
    dout[split:, :] = ended_ref[...]
    query_grad, key_grad, value_grad = pass_over(
        slice(FIRST, 4 * MAXV), shared, query, weights_ref, attended_ref, dout[...]
    )
    dq[:FIRST, :] = begun_query[...]
    dq[FIRST:, :] = query_grad
    key_grad = (begun_key[...] + key_grad) * HD ** (-0.5)
    value_grad = begun_value[...] + value_grad
    for index in range(4):
        kept_query[index] = dq[index * MAXV : (index + 1) * MAXV, :]
        rows = slice(2 * index * MAXV, (2 * index + 1) * MAXV)
        kept_shared[index, :, 0:128] = key_grad[rows]
        kept_shared[index, :, 128:256] = value_grad[rows]
        rows = slice((2 * index + 1) * MAXV, (2 * index + 2) * MAXV)
        leaving[index, :, 0:128] = key_grad[rows].astype(jnp.bfloat16)
        leaving[index, :, 128:256] = value_grad[rows].astype(jnp.bfloat16)


def combine_kernel(kept_query, kept_shared, crossed, *outs):
    for index in range(4):
        outs[index][:, 0:128] = kept_query[index]
        outs[index][:, 128:384] = (
            kept_shared[index] + crossed[index].astype(jnp.float32)
        ).astype(jnp.bfloat16)


def unpack_kernel(sides_ref, *rest):
    blocks, outs = rest[:4], rest[7:10]
    edges, sems = rest[10:]
    device = lax.axis_index("seq")
    last = outs[0].shape[1] - MAXV
    copies = []
    for index in range(3):
        for route, block in zip(ROUTES, blocks):
            chip = (device ^ route) // 2
            lanes = pl.ds(pl.multiple_of(chip * 128, 128), 128)
            piece = block[:, index * 128 : (index + 1) * 128]
            for side in range(2):
                edges[index, side, :, lanes] = piece * sides_ref[side]
        for side, start in enumerate((0, last)):
            copies.append(
                pltpu.make_async_copy(
                    edges.at[index, side],
                    outs[index].at[0, pl.ds(start, MAXV)],
                    sems.at[len(copies)],
                )
            )
            copies[-1].start()
    for copy in copies:
        copy.wait()


def finish_kernel(scale, mine_ref, other_ref, wg_hbm, wg_ref, sems):
    half = wg_ref.shape[0] // 2
    copies = []
    for part in range(2):
        rows = slice(part * half, (part + 1) * half)
        wg_ref[rows, :] = (
            mine_ref[rows, :].astype(jnp.float32) + other_ref[rows, :].astype(jnp.float32)
        ) * scale
        copies.append(
            pltpu.make_async_copy(
                wg_ref.at[pl.ds(part * half, half)],
                wg_hbm.at[pl.ds(part * half, half)],
                sems.at[part],
            )
        )
        copies[-1].start()
    for copy in copies:
        copy.wait()


PARAMS = pltpu.CompilerParams(vmem_limit_bytes=24 << 20)
ANYWHERE = pl.BlockSpec(memory_space=pl.ANY)
SCALARS = pl.BlockSpec(memory_space=pltpu.SMEM)
LOCAL = pl.BlockSpec(memory_space=pltpu.VMEM)


def in_hbm(block):
    return pltpu.with_memory_space_constraint(block, pltpu.HBM)


def by_heads(queries, keys, values, out_cotangent, visible_counts, span_offset, out_weight):
    bf16 = jnp.bfloat16
    pairs = lax.axis_size("seq")
    clips = lax.axis_size("clip")

    def shift(block, step):
        return lax.ppermute(block, "seq", [(i, i ^ step) for i in range(pairs)])

    narrow = jax.ShapeDtypeStruct((MAXV, 384), bf16)
    wide = jax.ShapeDtypeStruct((MAXV, out_cotangent.shape[2]), bf16)

    def seen(kernel, outs, specs, operands, scratch=(), out_specs=None):
        return pl.pallas_call(
            kernel,
            out_shape=outs,
            in_specs=specs,
            out_specs=out_specs or [LOCAL] * len(outs),
            scratch_shapes=scratch,
            compiler_params=PARAMS,
        )(*operands)

    width = out_cotangent.shape[2]
    rows = 8 * MAXV
    counts, offsets = in_hbm(visible_counts), in_hbm(span_offset)
    table = pltpu.SMEM(visible_counts.shape, jnp.int32)
    tables = [table, table]
    pair_sems = pltpu.SemaphoreType.DMA((2,))
    *sends, cot, sides = seen(
        pack_kernel,
        [narrow] * 4 + [wide, pltpu.VMEM((2, MAXV, 128), bf16)],
        [ANYWHERE] * 6,
        (counts, offsets, *map(in_hbm, (queries, keys, values, out_cotangent))),
        [
            pltpu.VMEM((3, 2, MAXV, queries.shape[2]), bf16),
            pltpu.VMEM((2, MAXV, width), bf16),
            *tables,
            pltpu.SemaphoreType.DMA((8,)),
            pair_sems,
        ],
    )
    even = [sends[0]] + [shift(sends[i], ROUTES[i]) for i in (1, 2, 3)]
    even_cot = [cot] + [shift(cot, ROUTES[i]) for i in (1, 2, 3)]
    odd = [shift(block, 1) for block in even]
    w_other = shift(out_weight, 1)
    blocks = [block for pair in zip(even, odd) for block in pair]
    full = jax.ShapeDtypeStruct(queries.shape, bf16)
    bias, *blanks = seen(
        tables_kernel,
        [pltpu.VMEM((rows, 128), jnp.float32)] + [full] * 3,
        [ANYWHERE] * 2,
        (counts, offsets),
        [
            pltpu.VMEM((queries.shape[1] - 2 * MAXV, queries.shape[2]), bf16),
            *tables,
            pltpu.SemaphoreType.DMA((3,)),
            pair_sems,
        ],
        [LOCAL] + [ANYWHERE] * 3,
    )
    own_rows = 4 * MAXV
    shared, query, first, second, attended = seen(
        forward_kernel,
        [
            pltpu.VMEM((rows, 256), bf16),
            pltpu.VMEM((own_rows, 128), bf16),
            pltpu.VMEM((2, rows, FIRST), jnp.float32),
            pltpu.VMEM((2, rows, own_rows - FIRST), jnp.float32),
            pltpu.VMEM((128, own_rows), bf16),
        ],
        [LOCAL] * 9,
        (bias, *blocks),
    )
    projected = pltpu.VMEM((2 * MAXV, 128), bf16)
    gathered = [pltpu.VMEM((2 * MAXV, width), bf16)]
    begun, begun_wg = seen(
        early_kernel,
        [projected, pltpu.VMEM((128, width), jnp.float32)],
        [LOCAL] * 5,
        (attended, out_weight, w_other, *even_cot[:2]),
        gathered,
    )
    partial = seen(
        backward_first_kernel,
        [
            pltpu.VMEM((FIRST, 128), bf16),
            pltpu.VMEM((rows, 128), jnp.float32),
            pltpu.VMEM((rows, 128), jnp.float32),
        ],
        [LOCAL] * 5,
        (shared, query, first, attended, begun),
    )
    ended, wg_own, wg_other = seen(
        late_kernel,
        [
            projected,
            pltpu.VMEM(out_weight.shape, jnp.float32),
            jax.ShapeDtypeStruct(out_weight.shape, bf16),
        ],
        [LOCAL] * 6,
        (attended, out_weight, w_other, begun_wg, *even_cot[2:]),
        gathered,
    )
    wg_crossed = shift(wg_other, 1)
    mine = (wg_own + wg_crossed.astype(jnp.float32)).astype(bf16)

    def across(block, step):
        return lax.ppermute(block, "clip", [(i, i ^ step) for i in range(clips)])

    other = across(mine, 1)
    step = 3
    while step < clips:
        mine = (mine.astype(jnp.float32) + other.astype(jnp.float32)).astype(bf16)
        other = across(mine, step)
        step = 2 * step + 1
    shares = [mine, other]
    kept_query, kept_shared, leaving = seen(
        backward_kernel,
        [
            jax.ShapeDtypeStruct((4, MAXV, 128), bf16),
            jax.ShapeDtypeStruct((4, MAXV, 256), jnp.float32),
            jax.ShapeDtypeStruct((4, MAXV, 256), bf16),
        ],
        [LOCAL] * 9,
        (shared, query, second, attended, begun, ended, *partial),
        [pltpu.VMEM((own_rows - FIRST, 128), bf16), pltpu.VMEM((own_rows, 128), bf16)],
    )
    crossed = shift(leaving, 1)
    joined = seen(combine_kernel, [narrow] * 4, [LOCAL] * 3, (kept_query, kept_shared, crossed))
    home = [joined[0]] + [shift(joined[i], ROUTES[i]) for i in (1, 2, 3)]
    scale = (clips * VIS_DEV * pairs) ** (-0.5)
    outs = pl.pallas_call(
        unpack_kernel,
        out_shape=[full] * 3,
        in_specs=[LOCAL] * 5 + [ANYWHERE] * 3,
        out_specs=[ANYWHERE] * 3,
        scratch_shapes=[
            pltpu.VMEM((3, 2, MAXV, queries.shape[2]), bf16),
            pltpu.SemaphoreType.DMA((6,)),
        ],
        input_output_aliases={5: 0, 6: 1, 7: 2},
        compiler_params=PARAMS,
        name="unpack",
    )(sides, *home, *blanks)
    weight_grad = seen(
        functools.partial(finish_kernel, scale),
        [jax.ShapeDtypeStruct(out_weight.shape, jnp.float32)],
        [LOCAL] * 2,
        shares,
        [pltpu.VMEM(out_weight.shape, jnp.float32), pltpu.SemaphoreType.DMA((2,))],
        [ANYWHERE],
    )[0]
    return (*outs, weight_grad)


def local(*arrays):
    if lax.axis_size("seq") == HEADS and lax.axis_size("clip") in (2, 4, 8, 16):
        return by_heads(*arrays)
    return by_rows(*arrays)


def solution(mesh):
    placed = (
        P("clip", "seq", None),
        P("clip", "seq", None),
        P("clip", "seq", None),
        P("clip", "seq", None),
        P("clip", None),
        P("clip", None),
        P("seq", None),
    )
    return jax.shard_map(
        local,
        mesh=mesh,
        in_specs=placed,
        out_specs=(
            P("clip", "seq", None),
            P("clip", "seq", None),
            P("clip", "seq", None),
            P("seq", None),
        ),
        check_vma=False,
    )
```
